32 devices in a mesh: dp: 2 (over x), expert: 16 (over z, y, core).
Axes of the slice: x: 2, y: 2, z: 4, core: 2. Of those that a mesh axis runs over, the one named last changes fastest.
Arguments:
- tokens: bfloat16 [4096, 1024], P(('dp', 'expert')), may hold values from -6 to 6
- route_ids: int32 [4096, 4], P(('dp', 'expert')), may hold values from 0 to 15, all different within a row; in each aligned block of 128 rows (0 to 127, 128 to 255, ...) at most 48 rows name the same one
- route_weights: float32 [4096, 4], P(('dp', 'expert')), may hold values from 0.2 to 1
- up_weight: bfloat16 [16, 1024, 704], P('expert', 'dp'), may hold values from -0.1875 to 0.1875
- down_weight: bfloat16 [16, 1024, 704], P('expert', 'dp'), may hold values from -0.21875 to 0.21875
- head_weight: bfloat16 [1024, 1024], P('dp'), may hold values from -0.75 to 0.75
- out_weight: float32 [1024], P('dp'), may hold values from -0.375 to 0.375
- pool_ids: int32 [32, 128], P(('dp', 'expert')), may hold values from 0 to 15, never falling along the last dimension, each value on 1 to 64 neighbouring positions
- list_ids: int32 [32, 16], P(('dp', 'expert')), may hold values from 0 to 7, as said below
- clicks: int32 [32, 16], P(('dp', 'expert')), may hold values 0 or 1
- ranks: int32 [32, 16], P(('dp', 'expert')), may hold values from 0 to 31
- alpha_table: float32 [32], replicated, may hold values from 0.3 to 1
- beta_table: float32 [32], replicated, may hold values from 0 to 0.3
Outputs:
- grad_up: bfloat16 [16, 1024, 704], P('expert', 'dp')
- grad_down: bfloat16 [16, 1024, 704], P('expert', 'dp')
- grad_head: float32 [1024, 1024], P('dp')
- grad_out: float32 [1024], P('dp')
- list_loss: float32 [16], P('expert')
The draws below stay inside these ranges and needn't reach their ends.
Inputs may be any that keep to these rules, and one draw needn't show every extreme that they name: `route_ids`: each token names 4 different experts; among the 128 tokens of one device no expert is named more than 48 times, a bound that some block reaches. `pool_ids`: in each row the candidate number never falls, every candidate has 1 to 64 tokens and one has exactly 64. `list_ids`: every list number appears in every row.
All inputs are finite; a program needn't handle non-finite values. No bound on the sum of `clicks` on one device may be relied on, other than what follows from the above.
Results may differ from the reference program's by a relative error of at most 0.028.
Values may be sent and summed in bfloat16 or wider, within the bound.
No kernel may reach another device: no remote copies, remote signals or barrier semaphores. Data moves between devices by JAX's collectives and lax.ppermute only.
A program may use at most 64 MiB of HBM per device.

```python
import math
import jax
import jax.numpy as jnp
import numpy as np
from jax import lax

D = 1024
FF = 704
HEAD = 1024
TOP = 4
TOK_DEV = 128
CAND_DEV = 16
SEG_MOST = 64
LISTS = 8
RANKS = 32
EXPERTS = 16
CAP = 48
TOKENS = 4096
SHARDS = 32
N_DP = 2
N_EXPERT = 16


def draw_list_ids(key, part):
    row_keys = jax.random.split(jax.random.fold_in(key, 11), SHARDS)
    permuted = jax.vmap(lambda single: jax.random.permutation(single, LISTS))(row_keys).astype(jnp.int32)
    filler = jax.random.randint(jax.random.fold_in(key, 12), (SHARDS, CAND_DEV), 0, LISTS).astype(jnp.int32)
    padded = jnp.concatenate([permuted, jnp.zeros((SHARDS, CAND_DEV - LISTS), jnp.int32)], axis=1)
    columns = jnp.arange(CAND_DEV, dtype=jnp.int32)[None, :]
    return jnp.where(columns < LISTS, padded, filler).astype(jnp.int32)


def place_ends(drawn, rng, least, high):
    shape = drawn.shape
    spot = [jax.random.randint(jax.random.fold_in(rng, axis), (), 0, shape[axis]) for axis in range(len(shape))]
    drawn = drawn.at[tuple(spot)].set(least)
    longest = shape.index(max(shape))
    spot[longest] = (spot[longest] + 1) % shape[longest]
    return drawn.at[tuple(spot)].set(high)


def block_levels(rng, dims, cuts, smallest, largest):
    def one(dim, shards_of):
        draws = jax.random.uniform(jax.random.fold_in(jax.random.fold_in(rng, 6), dim), (shards_of,), jnp.float32, smallest / len(cuts), largest / len(cuts))
        return jnp.repeat(jnp.exp(draws), dims[dim] // shards_of).reshape((-1,) + (1,) * (len(dims) - dim - 1))

    level = one(*cuts[0])
    for cut in cuts[1:]:
        level = level * one(*cut)
    return level


def length_profile(amount, total, reach, skew):
    weights = [(1 << 20) // math.isqrt(standing ** skew) + 1 for standing in range(2, amount + 1)]
    surplus, counts = total - reach - (amount - 1), [1] * (amount - 1)
    while surplus > 0:
        free = [i for i in range(amount - 1) if counts[i] < reach]
        whole, remaining = sum([weights[i] for i in free]), surplus
        for i in free:
            extra = min(reach - counts[i], max(1, remaining * weights[i] // whole), surplus)
            counts[i] = counts[i] + extra
            surplus = surplus - extra
    return np.array([reach] + counts)


def ragged(stream_key, count, total, bound, skew):
    if count == 2:
        one = jax.random.randint(stream_key, (), max(1, total - bound), min(bound, total - 1) + 1)
        return jnp.stack([one, total - one])
    tallies = jnp.asarray(length_profile(count, total, bound, skew), jnp.int32)
    couples = (count - 1) // 2
    donor, receiver = tallies[1:1 + 2 * couples:2], tallies[2:2 + 2 * couples:2]
    slack = jnp.minimum(donor - 1, bound - receiver)
    passed = jax.random.randint(jax.random.fold_in(stream_key, 1), (couples,), 0, 1 << 20) % (slack + 1)
    tallies = tallies.at[1:1 + 2 * couples:2].set(donor - passed).at[2:2 + 2 * couples:2].set(receiver + passed)
    return tallies[jax.random.permutation(jax.random.fold_in(stream_key, 2), count)]


def deal_out(own_key, own, number, rows, number_of, top, bound, skew):
    sequence = jax.random.permutation(own_key, number_of)
    heavy_load, usual = load_shares(number_of, rows * top, bound, skew, True), load_shares(number_of, rows * top, bound, skew, False)
    places = jnp.arange(number_of)

    def named(tallies, offset_by):
        used = int((tallies > 0).sum())
        fixed = max(1, used // 4)
        shifted = fixed + (places - fixed + offset_by * (used - fixed)) % max(1, number_of - fixed)
        return jnp.zeros((number_of,), jnp.int32).at[sequence[jnp.where(places < fixed, places, shifted)]].set(jnp.asarray(tallies, jnp.int32))

    tallies = jnp.where(number % 4 == 0, named(heavy_load, number // 4), named(usual, number - number // 4 - 1))
    mixed = jax.random.permutation(jax.random.fold_in(own, 3), number_of)
    giver, receiver = mixed[0:number_of // 2 * 2:2], mixed[1:number_of // 2 * 2:2]
    margin = jnp.minimum(tallies[giver] - 1, bound - tallies[receiver]) // 2
    margin = jnp.where((giver == sequence[0]) | (receiver == sequence[0]) | (tallies[receiver] == 0), 0, jnp.maximum(margin, 0))
    shifted = jax.random.randint(jax.random.fold_in(own, 4), (number_of // 2,), 0, 1 << 20) % (margin + 1)
    tallies = tallies.at[giver].add(-shifted).at[receiver].add(shifted)
    labels = jnp.searchsorted(jnp.cumsum(tallies), jnp.arange(rows * top), side="right").astype(jnp.int32)
    table = labels.reshape(top, rows).T
    table = table[jax.random.permutation(jax.random.fold_in(own, 1), rows)]
    offset_by = jax.random.randint(jax.random.fold_in(own, 2), (rows, 1), 0, top)
    return jnp.take_along_axis(table, (jnp.arange(top)[None, :] + offset_by) % top, axis=1)


def load_shares(amount, total, limit, skew, full):
    loads = [(1 << 20) // math.isqrt(standing ** skew) + 1 for standing in range(1, amount + 1)]
    largest = limit if full else min(limit, max(-(-total // amount), total * loads[0] // sum(loads)))
    least = 1 if total - largest >= amount - 1 else 0
    given, spare = [largest] + [least] * (amount - 1), total - largest - least * (amount - 1)
    while spare > 0:
        free = [i for i in range(1, amount) if given[i] < largest] or [i for i in range(1, amount) if given[i] < limit]
        mass, left = sum([loads[i] for i in free]), spare
        for i in free:
            addition = min(limit - given[i], max(1, left * loads[i] // mass), spare)
            given[i] = given[i] + addition
            spare = spare - addition
    return np.array(given)


def noise(rng, extent, scale, limit, cuts=(), held_as=jnp.bfloat16):
    factor_of = block_levels(rng, extent, cuts, -0.22, 0.18) if cuts else 1.0
    entries = jax.random.normal(rng, extent, jnp.float32) * scale * factor_of
    return jnp.minimum(jnp.maximum(entries, -limit), limit).astype(held_as)


def setup_inputs(seed: int = 0) -> dict:
    key_of = jax.random.split(jax.random.key(seed), 14)
    tokens = noise(key_of[0], (TOKENS, D), 1.0, 6.0, ((0, 32),))
    route_ids_keys = jax.random.split(jax.random.fold_in(key_of[1], 1), TOKENS // TOK_DEV)
    route_ids_turns = jax.random.permutation(jax.random.fold_in(key_of[1], 3), TOKENS // TOK_DEV)
    route_ids = jax.vmap(lambda own, number: deal_out(jax.random.fold_in(key_of[1], 2), own, number, TOK_DEV, EXPERTS, TOP, CAP, 2))(route_ids_keys, route_ids_turns).reshape((TOKENS, TOP))
    route_weights = jnp.clip(0.2 + 0.8 * jax.random.uniform(key_of[2], (TOKENS, TOP), jnp.float32) ** block_levels(key_of[2], (TOKENS, TOP), ((0, 32),), -0.2, 0.2), 0.2, 1.0)
    up_weight = noise(key_of[3], (EXPERTS, D, FF), D ** -0.5, 0.1875, ((0, 16), (1, 2)))
    down_weight = noise(key_of[4], (EXPERTS, D, FF), FF ** -0.5, 0.21875, ((0, 16), (1, 2)))
    head_weight = noise(key_of[5], (HEAD, D), (D // 16) ** -0.5, 0.75, ((0, 2),))
    out_weight = noise(key_of[6], (HEAD,), (HEAD // 4) ** -0.5, 0.375, ((0, 2),), jnp.float32)
    pool_ids = jax.vmap(lambda own: jnp.searchsorted(jnp.cumsum(ragged(own, CAND_DEV, TOK_DEV, SEG_MOST, 0)), jnp.arange(TOK_DEV), side="right"))(jax.random.split(key_of[7], SHARDS)).reshape((SHARDS, TOK_DEV)).astype(jnp.int32)
    list_ids = draw_list_ids(jax.random.fold_in(key_of[13], 71), 0)
    clicks = place_ends((jax.random.randint(key_of[9], (SHARDS, CAND_DEV), 0, 3) < 1).astype(jnp.int32), jax.random.fold_in(key_of[9], 1), 0, 1)
    ranks = place_ends(jax.random.randint(key_of[10], (SHARDS, CAND_DEV), 0, RANKS), jax.random.fold_in(key_of[10], 1), 0, RANKS - 1).astype(jnp.int32)
    alpha_table = jnp.clip(jnp.exp(jax.random.uniform(key_of[11], (RANKS,), jnp.float32, math.log(0.3), math.log(1.0))), 0.3, 1.0)
    beta_table = jnp.clip(jax.random.uniform(key_of[12], (RANKS,), jnp.float32, 0.0, 0.3), 0.0, 0.3)
    return dict(tokens=tokens, route_ids=route_ids, route_weights=route_weights, up_weight=up_weight, down_weight=down_weight, head_weight=head_weight, out_weight=out_weight, pool_ids=pool_ids, list_ids=list_ids, clicks=clicks, ranks=ranks, alpha_table=alpha_table, beta_table=beta_table)


def silu_slope(pre_act):
    sigmoid = jax.nn.sigmoid(pre_act)
    return sigmoid * (1.0 + pre_act * (1.0 - sigmoid))

def slots_of(flat_ids, owners):
    expert_hot = (flat_ids[:, None] == jnp.arange(owners, dtype=jnp.int32)[None, :]).astype(jnp.int32)
    running = jnp.cumsum(expert_hot, axis=0) - 1
    return lax.optimization_barrier(jnp.sum(running * expert_hot, axis=1)).astype(jnp.int32)

def expert_hidden(inputs, up_local):
    pre_act = jnp.dot(inputs, up_local, preferred_element_type=jnp.float32)
    return (pre_act, jax.nn.silu(pre_act).astype(jnp.bfloat16))

def reference(tokens, route_ids, route_weights, up_weight, down_weight, head_weight, out_weight, pool_ids, list_ids, clicks, ranks, alpha_table, beta_table):
    owners = N_EXPERT
    slot_total = owners * CAP
    assign_row = owners * TOK_DEV * TOP
    rows_all = N_DP * owners
    tok_all = tokens.reshape(N_DP, owners * TOK_DEV, D)
    ids_all = route_ids.reshape(N_DP, owners, TOK_DEV * TOP)
    weights_all = route_weights.reshape(N_DP, owners * TOK_DEV, TOP)
    slot_all = jax.vmap(jax.vmap(lambda flat: slots_of(flat, owners)))(ids_all)
    source = jnp.arange(owners, dtype=jnp.int32)[None, :, None]
    place = (ids_all * slot_total + source * CAP + slot_all).reshape(N_DP, assign_row).astype(jnp.int32)
    token_of = jnp.arange(assign_row, dtype=jnp.int32) // TOP

    def buffer_of(row_index):
        rows_in = tok_all[row_index]
        filled = jnp.zeros((owners * slot_total, D), jnp.bfloat16).at[place[row_index]].set(rows_in[token_of])
        return filled.reshape(owners, slot_total, D)

    def one_output(packed):
        inputs, up_local, down_local = packed
        pre_act, activated = expert_hidden(inputs, up_local)
        return lax.dot_general(activated, down_local, (((1,), (1,)), ((), ())), preferred_element_type=jnp.float32).astype(jnp.bfloat16)

    def routed_row(row_index):
        outputs = lax.map(one_output, (buffer_of(row_index), up_weight, down_weight))
        picked = outputs.reshape(owners * slot_total, D)[place[row_index]].reshape(owners * TOK_DEV, TOP, D)
        return lax.optimization_barrier(jnp.sum(weights_all[row_index][:, :, None] * picked.astype(jnp.float32), axis=1))
    routed = lax.map(routed_row, jnp.arange(N_DP, dtype=jnp.int32))
    mixed = (tok_all.astype(jnp.float32) + routed).reshape(rows_all, TOK_DEV, D)
    inv_rms = lax.rsqrt(lax.optimization_barrier(jnp.mean(mixed * mixed, axis=2, keepdims=True)) + 1e-06)
    normed = mixed * inv_rms
    member = (pool_ids[..., None] == jnp.arange(CAND_DEV, dtype=jnp.int32)).astype(jnp.float32)
    token_counts = lax.optimization_barrier(jnp.sum(member, axis=1))
    pooled = (jnp.einsum('ntc,ntd->ncd', member, normed, precision=lax.Precision.HIGHEST) / token_counts[..., None]).astype(jnp.bfloat16)
    pooled_flat = pooled.reshape(rows_all * CAND_DEV, D)
    head_act = jnp.tanh(lax.dot_general(pooled_flat, head_weight, (((1,), (1,)), ((), ())), preferred_element_type=jnp.float32))
    scores = lax.optimization_barrier(jnp.sum(head_act * out_weight[None, :], axis=1)).reshape(N_DP, owners, CAND_DEV)
    rank_hot = (ranks.reshape(N_DP, owners, CAND_DEV)[..., None] == jnp.arange(RANKS, dtype=jnp.int32)).astype(jnp.float32)
    alpha_of = lax.optimization_barrier(jnp.sum(rank_hot * alpha_table, axis=3))
    beta_of = lax.optimization_barrier(jnp.sum(rank_hot * beta_table, axis=3))
    corrected = (clicks.reshape(N_DP, owners, CAND_DEV).astype(jnp.float32) - beta_of) / alpha_of
    list_hot = (list_ids.reshape(N_DP, owners, CAND_DEV)[..., None] == jnp.arange(LISTS, dtype=jnp.int32)).astype(jnp.float32)
    exp_scores = jnp.exp(scores)
    exp_total = lax.optimization_barrier(jnp.sum(exp_scores[..., None] * list_hot, axis=(0, 2)))
    click_total = lax.optimization_barrier(jnp.sum(corrected[..., None] * list_hot, axis=(0, 2)))
    cross_total = lax.optimization_barrier(jnp.sum((corrected * scores)[..., None] * list_hot, axis=(0, 2)))
    list_loss = lax.optimization_barrier(jnp.sum(click_total * jnp.log(exp_total) - cross_total, axis=1))
    cand_grad = lax.optimization_barrier(jnp.sum(list_hot * (click_total / exp_total)[None, :, None, :], axis=3)) * exp_scores - corrected
    grad_flat = cand_grad.reshape(rows_all * CAND_DEV)
    hid_grad = (grad_flat[:, None] * out_weight[None, :] * (1.0 - head_act * head_act)).astype(jnp.bfloat16)
    grad_head = lax.dot_general(hid_grad, pooled_flat, (((0,), (0,)), ((), ())), preferred_element_type=jnp.float32)
    grad_out = lax.optimization_barrier(jnp.sum(grad_flat[:, None] * head_act, axis=0))
    pooled_grad = jnp.dot(hid_grad, head_weight, preferred_element_type=jnp.float32).reshape(rows_all, CAND_DEV, D)
    normed_grad = jnp.einsum('ntc,ncd->ntd', member, pooled_grad / token_counts[..., None], precision=lax.Precision.HIGHEST)
    mixed_grad = inv_rms * (normed_grad - normed * lax.optimization_barrier(jnp.mean(normed_grad * normed, axis=2, keepdims=True)))
    mixed_grad = mixed_grad.reshape(N_DP, owners * TOK_DEV, D)

    def backward_row(carry, row_index):
        up_sum, down_sum = carry
        buffers = buffer_of(row_index)
        cotangent = (weights_all[row_index][:, :, None] * mixed_grad[row_index][:, None, :]).astype(jnp.bfloat16).reshape(assign_row, D)
        slot_grads = jnp.zeros((owners * slot_total, D), jnp.bfloat16).at[place[row_index]].set(cotangent).reshape(owners, slot_total, D)

        def one_expert(packed):
            inputs, slot_grad, up_local, down_local = packed
            pre_act, activated = expert_hidden(inputs, up_local)
            act_grad = jnp.dot(slot_grad, down_local, preferred_element_type=jnp.float32)
            pre_grad = (act_grad * silu_slope(pre_act)).astype(jnp.bfloat16)
            up_term = lax.dot_general(inputs, pre_grad, (((0,), (0,)), ((), ())), preferred_element_type=jnp.float32).astype(jnp.bfloat16)
            down_term = lax.dot_general(slot_grad, activated, (((0,), (0,)), ((), ())), preferred_element_type=jnp.float32).astype(jnp.bfloat16)
            return (up_term, down_term)
        up_terms, down_terms = lax.map(one_expert, (buffers, slot_grads, up_weight, down_weight))
        return ((up_sum + up_terms.astype(jnp.float32), down_sum + down_terms.astype(jnp.float32)), None)
    start_carry = (jnp.zeros((owners, D, FF), jnp.float32), jnp.zeros((owners, D, FF), jnp.float32))
    (up_sum, down_sum), unused = lax.scan(backward_row, start_carry, jnp.arange(N_DP, dtype=jnp.int32))
    return (up_sum.astype(jnp.bfloat16), down_sum.astype(jnp.bfloat16), grad_head, grad_out, list_loss)
```

```python
import jax
import jax.numpy as jnp
import numpy as np
from jax import lax
from jax.sharding import PartitionSpec as P

LISTS = 8
RANKS = 32
BF = jnp.bfloat16
F32 = jnp.float32


def ring_order(chips):
    cols = 1
    while cols * cols * 4 <= chips and chips % (cols * 2) == 0:
        cols *= 2
    rows = chips // cols
    if cols == 1:
        return list(range(chips))
    cycle = [(r, 0) for r in range(rows)]
    for turn, r in enumerate(reversed(range(rows))):
        across = list(range(1, cols))
        if turn % 2:
            across.reverse()
        cycle += [(r, c) for c in across]
    return [r * cols + c for r, c in cycle]


class Ring:
    def __init__(self, devices):
        self.chips = devices // 2
        self.half = self.chips // 2
        cycle = ring_order(self.chips)
        count = self.chips
        self.forward = []
        for p in range(count):
            self.forward.append((2 * cycle[p], 2 * cycle[(p + 1) % count]))
            self.forward.append((2 * cycle[p] + 1, 2 * cycle[(p - 1) % count] + 1))
        self.swap_pairs = [(d, d ^ 1) for d in range(devices)]
        position = {chip: p for p, chip in enumerate(cycle)}
        table = np.zeros((devices, devices), np.int32)
        for device in range(devices):
            pos, core = position[device // 2], device % 2
            sign = 1 if core else -1

            def at(step, which):
                return 2 * cycle[(pos + step) % count] + which

            order = [at(0, core), at(0, 1 - core)]
            for r in range(1, self.half):
                order += [at(sign * r, core), at(sign * r, 1 - core)]
                order += [at(-sign * r, 1 - core), at(-sign * r, core)]
            order += [at(self.half, core), at(self.half, 1 - core)]
            table[device] = order
        self.table = table

    def send(self, x):
        return lax.ppermute(x, "expert", self.forward)

    def swap(self, x):
        return lax.ppermute(x, "expert", self.swap_pairs)

    def gather(self, x):
        rows = x.shape[0]
        current = jnp.concatenate([x, self.swap(x)], axis=0)
        rounds = [[current]]
        for r in range(1, self.half + 1):
            outgoing = current[:rows] if r == self.half else current
            current = self.send(outgoing)
            rounds.append([current, self.swap(current)])
        return rounds

    def scatter(self, rounds):
        rows = rounds[0].shape[0] // 2
        last = rounds[self.half]
        add = lambda a, b: (a.astype(F32) + b.astype(F32)).astype(BF)
        moving = add(last[:rows], self.swap(last[rows:]))
        for r in reversed(range(1, self.half)):
            block = rounds[r]
            came = self.send(moving)
            mine = block[2 * rows :]
            theirs = self.swap(block[: 2 * rows])
            if r == self.half - 1:
                low = add(mine[:rows], theirs[:rows])
                high = (
                    mine[rows:].astype(F32) + theirs[rows:].astype(F32) + came.astype(F32)
                ).astype(BF)
                moving = jnp.concatenate([low, high], axis=0)
            else:
                moving = (mine.astype(F32) + theirs.astype(F32) + came.astype(F32)).astype(BF)
        came = self.send(moving)
        own = rounds[0]
        given = self.swap(add(own[rows:], came[:rows]))
        return own[:rows].astype(F32) + came[rows:].astype(F32) + given.astype(F32)


def dp_slices(x, count):
    pieces = [x]
    for k in range(1, count):
        pieces.append(lax.ppermute(x, "dp", [((s + k) % count, s) for s in range(count)]))
    return pieces


def dp_halves(x, count):
    pieces = dp_slices(x, count)
    middle = count // 2
    join = lambda part: part[0] if len(part) == 1 else jnp.concatenate(part, axis=0)
    return join(pieces[:middle]), join(pieces[middle:])


def dp_reduce(term_of, count):
    total = term_of(0)
    for k in range(1, count):
        sent = term_of(k).astype(BF)
        pairs = [(s, (s + k) % count) for s in range(count)]
        total = total + lax.ppermute(sent, "dp", pairs).astype(F32)
    return total


def roll_columns(x, start):
    return lax.dynamic_slice_in_dim(jnp.concatenate([x, x], axis=1), start, x.shape[1], axis=1)


def silu_slope(pre_act):
    sigmoid = jax.nn.sigmoid(pre_act)
    return sigmoid * (1.0 + pre_act * (1.0 - sigmoid))


def routed_local(
    tokens,
    route_ids,
    route_weights,
    up_weight,
    down_weight,
    head_weight,
    out_weight,
    pool_ids,
    list_ids,
    clicks,
    ranks,
    alpha_table,
    beta_table,
):
    tok_count = tokens.shape[0]
    model_width = tokens.shape[1]
    top_count = route_ids.shape[1]
    owners = lax.axis_size("expert")
    capacity = 3 * tok_count * top_count // (2 * owners)
    slot_total = owners * capacity
    flat_ids = route_ids.reshape(-1)
    expert_hot = (flat_ids[:, None] == jnp.arange(owners, dtype=jnp.int32)[None, :]).astype(
        jnp.int32
    )
    running = jnp.cumsum(expert_hot, axis=0) - 1
    slot_index = jnp.sum(running * expert_hot, axis=1)
    target = flat_ids * capacity + slot_index
    token_index = jnp.arange(tok_count * top_count, dtype=jnp.int32) // top_count
    outgoing = (
        jnp.zeros((slot_total, model_width), jnp.bfloat16).at[target].set(tokens[token_index])
    )
    received = lax.all_to_all(
        outgoing.reshape(owners, capacity, model_width),
        "expert",
        split_axis=0,
        concat_axis=0,
        tiled=True,
    )
    inputs = received.reshape(slot_total, model_width)
    up_local = up_weight[0]
    down_local = down_weight[0]
    hidden_width = up_local.shape[1]
    columns = inputs
    pre_act = jnp.dot(
        columns,
        lax.all_gather(up_local, "dp", axis=0, tiled=True),
        preferred_element_type=jnp.float32,
    )
    activated = jax.nn.silu(pre_act).astype(jnp.bfloat16)
    expert_out = lax.dot_general(
        activated,
        lax.all_gather(down_local, "dp", axis=0, tiled=True),
        (((1,), (1,)), ((), ())),
        preferred_element_type=jnp.float32,
    ).astype(jnp.bfloat16)
    returned = lax.all_to_all(
        expert_out.reshape(owners, capacity, model_width),
        "expert",
        split_axis=0,
        concat_axis=0,
        tiled=True,
    ).reshape(slot_total, model_width)
    routed_rows = returned[target].reshape(tok_count, top_count, model_width)
    routed = jnp.sum(route_weights[:, :, None] * routed_rows.astype(jnp.float32), axis=1)
    mixed = tokens.astype(jnp.float32) + routed
    inv_rms = lax.rsqrt(jnp.mean(mixed * mixed, axis=1, keepdims=True) + 1e-06)
    normed = mixed * inv_rms
    cand_count = list_ids.shape[1]
    member = (pool_ids[0][:, None] == jnp.arange(cand_count, dtype=jnp.int32)[None, :]).astype(
        jnp.float32
    )
    token_counts = jnp.sum(member, axis=0)
    pooled_sum = lax.dot_general(
        member,
        normed,
        (((0,), (0,)), ((), ())),
        precision=lax.Precision.HIGHEST,
        preferred_element_type=jnp.float32,
    )
    pooled = (pooled_sum / token_counts[:, None]).astype(jnp.bfloat16)
    all_pooled = lax.all_gather(pooled, "dp", axis=0, tiled=True)
    head_act = jnp.tanh(
        lax.dot_general(
            all_pooled, head_weight, (((1,), (1,)), ((), ())), preferred_element_type=jnp.float32
        )
    )
    part_score = jnp.sum(head_act * out_weight[None, :], axis=1)
    rank_hot = (ranks[0][:, None] == jnp.arange(RANKS, dtype=jnp.int32)[None, :]).astype(
        jnp.float32
    )
    alpha_of = jnp.sum(rank_hot * alpha_table[None, :], axis=1)
    beta_of = jnp.sum(rank_hot * beta_table[None, :], axis=1)
    corrected = (clicks[0].astype(jnp.float32) - beta_of) / alpha_of
    list_hot = (list_ids[0][:, None] == jnp.arange(LISTS, dtype=jnp.int32)[None, :]).astype(
        jnp.float32
    )
    group_corrected, group_lists = (
        lax.all_gather(corrected, "dp", axis=0, tiled=True),
        lax.all_gather(list_hot, "dp", axis=0, tiled=True),
    )
    group_scores = lax.psum(part_score, "dp")
    exp_scores = jnp.exp(group_scores)
    exp_total = jnp.sum(exp_scores[:, None] * group_lists, axis=0)
    click_total = jnp.sum(group_corrected[:, None] * group_lists, axis=0)
    cross_total = jnp.sum((group_corrected * group_scores)[:, None] * group_lists, axis=0)
    list_loss = jnp.sum(click_total * jnp.log(exp_total) - cross_total).reshape(1)
    group_grad = (
        jnp.sum(group_lists * (click_total / exp_total)[None, :], axis=1) * exp_scores
        - group_corrected
    )
    hid_grad = (group_grad[:, None] * out_weight[None, :] * (1.0 - head_act * head_act)).astype(
        jnp.bfloat16
    )
    head_term = lax.dot_general(
        hid_grad, all_pooled, (((0,), (0,)), ((), ())), preferred_element_type=jnp.float32
    )
    out_term = jnp.sum(group_grad[:, None] * head_act, axis=0)
    grad_head, grad_out = (
        lax.psum(head_term.astype(jnp.bfloat16), "expert").astype(jnp.float32),
        lax.psum(out_term.astype(jnp.bfloat16), "expert").astype(jnp.float32),
    )
    pooled_grad = lax.psum_scatter(
        jnp.dot(hid_grad, head_weight, preferred_element_type=jnp.float32).astype(jnp.bfloat16),
        "dp",
        scatter_dimension=0,
        tiled=True,
    ).astype(jnp.float32)
    normed_grad = jnp.dot(
        member,
        pooled_grad / token_counts[:, None],
        precision=lax.Precision.HIGHEST,
        preferred_element_type=jnp.float32,
    )
    mixed_grad = inv_rms * (
        normed_grad - normed * jnp.mean(normed_grad * normed, axis=1, keepdims=True)
    )
    cotangent = (
        (route_weights[:, :, None] * mixed_grad[:, None, :])
        .astype(jnp.bfloat16)
        .reshape(tok_count * top_count, model_width)
    )
    outgoing_grad = jnp.zeros((slot_total, model_width), jnp.bfloat16).at[target].set(cotangent)
    slot_grad = lax.all_to_all(
        outgoing_grad.reshape(owners, capacity, model_width),
        "expert",
        split_axis=0,
        concat_axis=0,
        tiled=True,
    ).reshape(slot_total, model_width)
    columns = slot_grad
    act_grad = jnp.dot(
        columns,
        lax.all_gather(down_local, "dp", axis=0, tiled=True),
        preferred_element_type=jnp.float32,
    )
    pre_grad = (act_grad * silu_slope(pre_act)).astype(jnp.bfloat16)
    up_term = lax.dot_general(
        inputs, pre_grad, (((0,), (0,)), ((), ())), preferred_element_type=jnp.float32
    )
    down_term = lax.dot_general(
        slot_grad, activated, (((0,), (0,)), ((), ())), preferred_element_type=jnp.float32
    )
    summed = lax.psum_scatter(
        jnp.concatenate([up_term, down_term], axis=1).astype(jnp.bfloat16),
        "dp",
        scatter_dimension=0,
        tiled=True,
    ).astype(jnp.float32)
    grad_up = summed[:, :hidden_width].astype(jnp.bfloat16)[None]
    grad_down = summed[:, hidden_width:].astype(jnp.bfloat16)[None]
    return (grad_up, grad_down, grad_head, grad_out, list_loss)


def dense_local(
    tokens,
    route_ids,
    route_weights,
    up_weight,
    down_weight,
    head_weight,
    out_weight,
    pool_ids,
    list_ids,
    clicks,
    ranks,
    alpha_table,
    beta_table,
):
    n_dp = lax.axis_size("dp")
    n_exp = lax.axis_size("expert")
    dp_index = lax.axis_index("dp")
    exp_index = lax.axis_index("expert")
    ring = Ring(n_exp)
    tok_count, width = tokens.shape
    part = width // n_dp
    half = width // 2
    cand_count = list_ids.shape[1]

    rolled = roll_columns(tokens, dp_index * part)
    columns = [rolled[:, :half], rolled[:, half:]]
    gathered = [ring.gather(c) for c in columns]

    up = dp_halves(up_weight[0], n_dp)
    down_in, _ = lax.optimization_barrier((down_weight[0], up[1]))
    down = dp_halves(down_in, n_dp)
    head_in, out_in, _ = lax.optimization_barrier((head_weight, out_weight, down[1]))
    head = jnp.concatenate(dp_slices(head_in, n_dp), axis=0)
    out_w = jnp.concatenate(dp_slices(out_in, n_dp), axis=0)

    expert_range = jnp.arange(n_exp, dtype=jnp.int32)
    chosen = route_ids.T[:, None, :] == expert_range[None, :, None]
    weight_of = jnp.sum(jnp.where(chosen, route_weights.T[:, None, :], 0.0), axis=0)
    arrived = lax.all_to_all(weight_of, "expert", split_axis=0, concat_axis=0, tiled=True)
    order = lax.dynamic_index_in_dim(jnp.asarray(ring.table), exp_index, keepdims=False)
    weight_rows = arrived[order].reshape(n_exp * tok_count, 1)

    inputs = [
        [jnp.concatenate(blocks, axis=0) if len(blocks) > 1 else blocks[0] for blocks in side]
        for side in gathered
    ]
    acted, slopes, outs = [], [], [[], []]
    start = 0
    for r in range(ring.half + 1):
        rows = inputs[0][r].shape[0]
        w = weight_rows[start : start + rows]
        start += rows
        pre = sum(
            jnp.dot(inputs[h][r], up[h], preferred_element_type=F32) for h in range(2)
        )
        sig = jax.nn.sigmoid(pre)
        acted.append((w * (pre * sig)).astype(BF))
        slopes.append((w * (sig * (1.0 + pre * (1.0 - sig)))).astype(BF))
    for h in range(2):
        for r in range(ring.half + 1):
            outs[h].append(
                lax.dot_general(
                    acted[r], down[h], (((1,), (1,)), ((), ())), preferred_element_type=F32
                ).astype(BF)
            )
    routed = jnp.concatenate([ring.scatter(outs[h]) for h in range(2)], axis=1)
    mixed = rolled.astype(F32) + routed
    inv_rms = lax.rsqrt(jnp.mean(mixed * mixed, axis=1, keepdims=True) + 1e-06)
    normed = mixed * inv_rms

    member = (pool_ids[0][:, None] == jnp.arange(cand_count, dtype=jnp.int32)[None, :]).astype(F32)
    token_counts = jnp.sum(member, axis=0)
    pooled_sum = lax.dot_general(
        member,
        normed,
        (((0,), (0,)), ((), ())),
        precision=lax.Precision.HIGHEST,
        preferred_element_type=F32,
    )
    pooled = (pooled_sum / token_counts[:, None]).astype(BF)
    pooled = roll_columns(pooled, width - dp_index * part)
    head_act = jnp.tanh(
        lax.dot_general(pooled, head, (((1,), (1,)), ((), ())), preferred_element_type=F32)
    )
    scores = jnp.sum(head_act * out_w[None, :], axis=1)
    rank_hot = (ranks[0][:, None] == jnp.arange(RANKS, dtype=jnp.int32)[None, :]).astype(F32)
    alpha_of = jnp.sum(rank_hot * alpha_table[None, :], axis=1)
    beta_of = jnp.sum(rank_hot * beta_table[None, :], axis=1)
    corrected = (clicks[0].astype(F32) - beta_of) / alpha_of
    list_hot = (list_ids[0][:, None] == jnp.arange(LISTS, dtype=jnp.int32)[None, :]).astype(F32)

    def dp_total(x):
        if n_dp == 2:
            return x + lax.ppermute(x, "dp", [(0, 1), (1, 0)])
        return lax.psum(x, "dp")

    click_total = dp_total(jnp.sum(corrected[:, None] * list_hot, axis=0))
    exp_scores = jnp.exp(scores)
    totals = dp_total(
        jnp.stack(
            [
                jnp.sum(exp_scores[:, None] * list_hot, axis=0),
                jnp.sum((corrected * scores)[:, None] * list_hot, axis=0),
            ]
        )
    )
    exp_total, cross_total = totals[0], totals[1]
    list_loss = jnp.sum(click_total * jnp.log(exp_total) - cross_total).reshape(1)
    cand_grad = (
        jnp.sum(list_hot * (click_total / exp_total)[None, :], axis=1) * exp_scores - corrected
    )
    hid_grad = (cand_grad[:, None] * out_w[None, :] * (1.0 - head_act * head_act)).astype(BF)
    pooled_grad = jnp.dot(hid_grad, head, preferred_element_type=F32)
    pooled_grad = roll_columns(pooled_grad, dp_index * part)
    normed_grad = jnp.dot(
        member,
        pooled_grad / token_counts[:, None],
        precision=lax.Precision.HIGHEST,
        preferred_element_type=F32,
    )
    mixed_grad = (
        inv_rms * (normed_grad - normed * jnp.mean(normed_grad * normed, axis=1, keepdims=True))
    ).astype(BF)

    cat = lambda parts: jnp.concatenate(parts, axis=0)
    act_all = cat(acted)
    slope_all = cat(slopes)
    input_all = [cat(inputs[h]) for h in range(2)]
    grads = [None, None]
    for h in (1, 0):
        grads[h] = cat(
            [b for blocks in ring.gather(mixed_grad[:, h * half : (h + 1) * half]) for b in blocks]
        )

    def slice_of(sides, k):
        if n_dp == 2:
            return sides[k]
        side, within = divmod(k, n_dp // 2)
        return sides[side][:, within * part : (within + 1) * part]

    def term(sides, other):
        return lambda k: lax.dot_general(
            slice_of(sides, k), other, (((0,), (0,)), ((), ())), preferred_element_type=F32
        )

    grad_down = dp_reduce(term(grads, act_all), n_dp).astype(BF)[None]
    act_grad = sum(jnp.dot(grads[h], down[h], preferred_element_type=F32) for h in (1, 0))
    pre_grad = (act_grad * slope_all.astype(F32)).astype(BF)
    grad_up = dp_reduce(term(input_all, pre_grad), n_dp).astype(BF)[None]

    units = head_weight.shape[0]
    rows_cand = [pooled]
    rows_hid = [hid_grad[:, :units]]
    act_mine = [jnp.sum(cand_grad[:, None] * head_act, axis=0)[None, :units]]
    for k in range(1, n_dp):
        pairs = [(s, (s + k) % n_dp) for s in range(n_dp)]
        packed = jnp.concatenate([pooled, hid_grad[:, k * units : (k + 1) * units]], axis=1)
        packed = lax.ppermute(packed, "dp", pairs)
        rows_cand.append(packed[:, :width])
        rows_hid.append(packed[:, width:])
    packed = jnp.concatenate([cat(rows_cand), cat(rows_hid)], axis=1)
    blocks = cat([b for blocks in ring.gather(packed) for b in blocks])
    blocks = blocks.reshape(n_exp, packed.shape[0], width + units)
    placed = blocks[jnp.argsort(order)].reshape(n_exp * packed.shape[0], width + units)
    grad_head = lax.dot_general(
        placed[:, width:], placed[:, :width], (((0,), (0,)), ((), ())), preferred_element_type=F32
    )
    out_terms = jnp.sum(cand_grad[:, None] * head_act, axis=0)
    out_mine = out_terms[:units]
    for k in range(1, n_dp):
        pairs = [(s, (s + k) % n_dp) for s in range(n_dp)]
        out_mine = out_mine + lax.ppermute(out_terms[k * units : (k + 1) * units], "dp", pairs)
    grad_out = lax.psum(out_mine.astype(BF), "expert").astype(F32)
    return (grad_up, grad_down, grad_head, grad_out, list_loss)


def solution(mesh):
    paired = mesh.shape["dp"] == 2 and mesh.shape["expert"] % 4 == 0
    return jax.shard_map(
        dense_local if paired else routed_local,
        mesh=mesh,
        in_specs=(
            P(("dp", "expert"), None),
            P(("dp", "expert"), None),
            P(("dp", "expert"), None),
            P("expert", "dp", None),
            P("expert", "dp", None),
            P("dp", None),
            P("dp"),
            P(("dp", "expert"), None),
            P(("dp", "expert"), None),
            P(("dp", "expert"), None),
            P(("dp", "expert"), None),
            P(),
            P(),
        ),
        out_specs=(
            P("expert", "dp", None),
            P("expert", "dp", None),
            P("dp", None),
            P("dp"),
            P("expert"),
        ),
        check_vma=False,
    )
```

```python
import jax
import jax.numpy as jnp
import numpy as np
from jax import lax
from jax.experimental import pallas as pl
from jax.experimental.pallas import tpu as pltpu
from jax.sharding import PartitionSpec as P

LISTS = 8
RANKS = 32
BF = jnp.bfloat16
F32 = jnp.float32


def ring_order(chips):
    cols = 1
    while cols * cols * 4 <= chips and chips % (cols * 2) == 0:
        cols *= 2
    rows = chips // cols
    if cols == 1:
        return list(range(chips))
    cycle = [(r, 0) for r in range(rows)]
    for turn, r in enumerate(reversed(range(rows))):
        across = list(range(1, cols))
        if turn % 2:
            across.reverse()
        cycle += [(r, c) for c in across]
    return [r * cols + c for r, c in cycle]


class Ring:
    def __init__(self, devices):
        self.chips = devices // 2
        self.half = self.chips // 2
        cycle = ring_order(self.chips)
        count = self.chips
        self.forward = []
        for p in range(count):
            self.forward.append((2 * cycle[p], 2 * cycle[(p + 1) % count]))
            self.forward.append((2 * cycle[p] + 1, 2 * cycle[(p - 1) % count] + 1))
        self.swap_pairs = [(d, d ^ 1) for d in range(devices)]
        position = {chip: p for p, chip in enumerate(cycle)}
        table = np.zeros((devices, devices), np.int32)
        for device in range(devices):
            pos, core = position[device // 2], device % 2
            sign = 1 if core else -1

            def at(step, which):
                return 2 * cycle[(pos + step) % count] + which

            order = [at(0, core), at(0, 1 - core)]
            for r in range(1, self.half):
                order += [at(sign * r, core), at(sign * r, 1 - core)]
                order += [at(-sign * r, 1 - core), at(-sign * r, core)]
            order += [at(self.half, core), at(self.half, 1 - core)]
            table[device] = order
        self.table = table

    def send(self, x):
        return lax.ppermute(x, "expert", self.forward)

    def swap(self, x):
        return lax.ppermute(x, "expert", self.swap_pairs)

    def gather(self, x):
        rows = x.shape[0]
        current = jnp.concatenate([x, self.swap(x)], axis=0)
        rounds = [[current]]
        for r in range(1, self.half + 1):
            outgoing = current[:rows] if r == self.half else current
            current = self.send(outgoing)
            rounds.append([current, self.swap(current)])
        return rounds


def silu_slope(pre_act):
    sigmoid = jax.nn.sigmoid(pre_act)
    return sigmoid * (1.0 + pre_act * (1.0 - sigmoid))


def routed_local(
    tokens,
    route_ids,
    route_weights,
    up_weight,
    down_weight,
    head_weight,
    out_weight,
    pool_ids,
    list_ids,
    clicks,
    ranks,
    alpha_table,
    beta_table,
):
    tok_count = tokens.shape[0]
    model_width = tokens.shape[1]
    top_count = route_ids.shape[1]
    owners = lax.axis_size("expert")
    capacity = 3 * tok_count * top_count // (2 * owners)
    slot_total = owners * capacity
    flat_ids = route_ids.reshape(-1)
    expert_hot = (flat_ids[:, None] == jnp.arange(owners, dtype=jnp.int32)[None, :]).astype(
        jnp.int32
    )
    running = jnp.cumsum(expert_hot, axis=0) - 1
    slot_index = jnp.sum(running * expert_hot, axis=1)
    target = flat_ids * capacity + slot_index
    token_index = jnp.arange(tok_count * top_count, dtype=jnp.int32) // top_count
    outgoing = (
        jnp.zeros((slot_total, model_width), jnp.bfloat16).at[target].set(tokens[token_index])
    )
    received = lax.all_to_all(
        outgoing.reshape(owners, capacity, model_width),
        "expert",
        split_axis=0,
        concat_axis=0,
        tiled=True,
    )
    inputs = received.reshape(slot_total, model_width)
    up_local = up_weight[0]
    down_local = down_weight[0]
    hidden_width = up_local.shape[1]
    columns = inputs
    pre_act = jnp.dot(
        columns,
        lax.all_gather(up_local, "dp", axis=0, tiled=True),
        preferred_element_type=jnp.float32,
    )
    activated = jax.nn.silu(pre_act).astype(jnp.bfloat16)
    expert_out = lax.dot_general(
        activated,
        lax.all_gather(down_local, "dp", axis=0, tiled=True),
        (((1,), (1,)), ((), ())),
        preferred_element_type=jnp.float32,
    ).astype(jnp.bfloat16)
    returned = lax.all_to_all(
        expert_out.reshape(owners, capacity, model_width),
        "expert",
        split_axis=0,
        concat_axis=0,
        tiled=True,
    ).reshape(slot_total, model_width)
    routed_rows = returned[target].reshape(tok_count, top_count, model_width)
    routed = jnp.sum(route_weights[:, :, None] * routed_rows.astype(jnp.float32), axis=1)
    mixed = tokens.astype(jnp.float32) + routed
    inv_rms = lax.rsqrt(jnp.mean(mixed * mixed, axis=1, keepdims=True) + 1e-06)
    normed = mixed * inv_rms
    cand_count = list_ids.shape[1]
    member = (pool_ids[0][:, None] == jnp.arange(cand_count, dtype=jnp.int32)[None, :]).astype(
        jnp.float32
    )
    token_counts = jnp.sum(member, axis=0)
    pooled_sum = lax.dot_general(
        member,
        normed,
        (((0,), (0,)), ((), ())),
        precision=lax.Precision.HIGHEST,
        preferred_element_type=jnp.float32,
    )
    pooled = (pooled_sum / token_counts[:, None]).astype(jnp.bfloat16)
    all_pooled = lax.all_gather(pooled, "dp", axis=0, tiled=True)
    head_act = jnp.tanh(
        lax.dot_general(
            all_pooled, head_weight, (((1,), (1,)), ((), ())), preferred_element_type=jnp.float32
        )
    )
    part_score = jnp.sum(head_act * out_weight[None, :], axis=1)
    rank_hot = (ranks[0][:, None] == jnp.arange(RANKS, dtype=jnp.int32)[None, :]).astype(
        jnp.float32
    )
    alpha_of = jnp.sum(rank_hot * alpha_table[None, :], axis=1)
    beta_of = jnp.sum(rank_hot * beta_table[None, :], axis=1)
    corrected = (clicks[0].astype(jnp.float32) - beta_of) / alpha_of
    list_hot = (list_ids[0][:, None] == jnp.arange(LISTS, dtype=jnp.int32)[None, :]).astype(
        jnp.float32
    )
    group_corrected, group_lists = (
        lax.all_gather(corrected, "dp", axis=0, tiled=True),
        lax.all_gather(list_hot, "dp", axis=0, tiled=True),
    )
    group_scores = lax.psum(part_score, "dp")
    exp_scores = jnp.exp(group_scores)
    exp_total = jnp.sum(exp_scores[:, None] * group_lists, axis=0)
    click_total = jnp.sum(group_corrected[:, None] * group_lists, axis=0)
    cross_total = jnp.sum((group_corrected * group_scores)[:, None] * group_lists, axis=0)
    list_loss = jnp.sum(click_total * jnp.log(exp_total) - cross_total).reshape(1)
    group_grad = (
        jnp.sum(group_lists * (click_total / exp_total)[None, :], axis=1) * exp_scores
        - group_corrected
    )
    hid_grad = (group_grad[:, None] * out_weight[None, :] * (1.0 - head_act * head_act)).astype(
        jnp.bfloat16
    )
    head_term = lax.dot_general(
        hid_grad, all_pooled, (((0,), (0,)), ((), ())), preferred_element_type=jnp.float32
    )
    out_term = jnp.sum(group_grad[:, None] * head_act, axis=0)
    grad_head, grad_out = (
        lax.psum(head_term.astype(jnp.bfloat16), "expert").astype(jnp.float32),
        lax.psum(out_term.astype(jnp.bfloat16), "expert").astype(jnp.float32),
    )
    pooled_grad = lax.psum_scatter(
        jnp.dot(hid_grad, head_weight, preferred_element_type=jnp.float32).astype(jnp.bfloat16),
        "dp",
        scatter_dimension=0,
        tiled=True,
    ).astype(jnp.float32)
    normed_grad = jnp.dot(
        member,
        pooled_grad / token_counts[:, None],
        precision=lax.Precision.HIGHEST,
        preferred_element_type=jnp.float32,
    )
    mixed_grad = inv_rms * (
        normed_grad - normed * jnp.mean(normed_grad * normed, axis=1, keepdims=True)
    )
    cotangent = (
        (route_weights[:, :, None] * mixed_grad[:, None, :])
        .astype(jnp.bfloat16)
        .reshape(tok_count * top_count, model_width)
    )
    outgoing_grad = jnp.zeros((slot_total, model_width), jnp.bfloat16).at[target].set(cotangent)
    slot_grad = lax.all_to_all(
        outgoing_grad.reshape(owners, capacity, model_width),
        "expert",
        split_axis=0,
        concat_axis=0,
        tiled=True,
    ).reshape(slot_total, model_width)
    columns = slot_grad
    act_grad = jnp.dot(
        columns,
        lax.all_gather(down_local, "dp", axis=0, tiled=True),
        preferred_element_type=jnp.float32,
    )
    pre_grad = (act_grad * silu_slope(pre_act)).astype(jnp.bfloat16)
    up_term = lax.dot_general(
        inputs, pre_grad, (((0,), (0,)), ((), ())), preferred_element_type=jnp.float32
    )
    down_term = lax.dot_general(
        slot_grad, activated, (((0,), (0,)), ((), ())), preferred_element_type=jnp.float32
    )
    summed = lax.psum_scatter(
        jnp.concatenate([up_term, down_term], axis=1).astype(jnp.bfloat16),
        "dp",
        scatter_dimension=0,
        tiled=True,
    ).astype(jnp.float32)
    grad_up = summed[:, :hidden_width].astype(jnp.bfloat16)[None]
    grad_down = summed[:, hidden_width:].astype(jnp.bfloat16)[None]
    return (grad_up, grad_down, grad_head, grad_out, list_loss)


def vmem_call(kernel, outs, args, scratch=(), flops=0, smem=0):
    specs = [pl.BlockSpec(memory_space=pltpu.SMEM)] * smem + [
        pl.BlockSpec(memory_space=pltpu.VMEM)
    ] * (len(args) - smem)
    moved = sum(a.size * a.dtype.itemsize for a in args) + sum(
        o.size * o.dtype.itemsize for o in outs
    )
    return pl.pallas_call(
        kernel,
        out_shape=outs,
        in_specs=specs,
        out_specs=[pl.BlockSpec(memory_space=pltpu.VMEM)] * len(outs),
        scratch_shapes=list(scratch),
        cost_estimate=pl.CostEstimate(flops=flops, bytes_accessed=moved, transcendentals=0),
    )(*args)


def shaped(shape, dtype):
    return jax.ShapeDtypeStruct(shape, dtype)


def fill(buffer, refs, start=0):
    at = 0
    for ref in refs:
        buffer[pl.ds(at, ref.shape[0]), :] = ref[:, start : start + buffer.shape[1]]
        at += ref.shape[0]


def hidden_stage(blocks, groups, up, weights, first):
    count = len(blocks)
    tok, width = blocks[0].shape
    hidden = up[0].shape[1]
    half = width // 2
    rows = count * tok
    sizes = [g * tok for g in groups]

    def kernel(*refs):
        xs, (up0, up1, w_ref) = refs[:count], refs[count : count + 3]
        act_refs = refs[count + 3 : count + 3 + len(groups)]
        slope_refs = refs[count + 3 + len(groups) : count + 3 + 2 * len(groups)]
        buffer = refs[-1]
        fill(buffer, xs)
        at, j = 0, 0
        for index, g in enumerate(groups):
            x = buffer[pl.ds(at, g * tok), :]
            pre = jnp.dot(x[:, :half], up0[...], preferred_element_type=F32)
            pre = pre + jnp.dot(x[:, half:], up1[...], preferred_element_type=F32)
            sig = 1.0 / (1.0 + jnp.exp(-pre))
            for b in range(g):
                w = w_ref[:, first + j : first + j + 1]
                p = pre[b * tok : (b + 1) * tok]
                s = sig[b * tok : (b + 1) * tok]
                ws = w * s
                act_refs[index][pl.ds(b * tok, tok), :] = (ws * p).astype(BF)
                slope_refs[index][pl.ds(b * tok, tok), :] = (ws * (1.0 + p * (1.0 - s))).astype(BF)
                j += 1
            at += g * tok

    outs = [shaped((s, hidden), BF) for s in sizes]
    result = vmem_call(
        kernel,
        outs + outs,
        list(blocks) + [up[0], up[1], weights],
        scratch=[pltpu.VMEM((rows, width), BF)],
        flops=2 * rows * width * hidden,
    )
    return result[: len(groups)], result[len(groups) :]


def project(act, down, theirs=None, came=None):
    rows = act.shape[0]
    out_width = down.shape[0]
    extra = [a for a in (theirs, came) if a is not None]

    def kernel(act_ref, down_ref, *refs):
        out_ref = refs[-1]
        value = lax.dot_general(
            act_ref[...], down_ref[...], (((1,), (1,)), ((), ())), preferred_element_type=F32
        )
        for ref in refs[:-1]:
            add = ref[...].astype(F32)
            missing = rows - add.shape[0]
            if missing:
                low = value[:missing]
                value = jnp.concatenate([low, value[missing:] + add], axis=0)
            else:
                value = value + add
        out_ref[...] = value.astype(BF)

    return vmem_call(
        kernel,
        [shaped((rows, out_width), BF)],
        [act, down] + extra,
        flops=2 * rows * out_width * act.shape[1],
    )[0]


def outer_sum(lefts, rights, out_dtype, lw, start=0):
    nl, nr = len(lefts), len(rights)
    rows = sum(a.shape[0] for a in lefts)
    rw = rights[0].shape[1]
    step = 128 if lw % 128 == 0 else lw

    def kernel(*refs):
        left, right, out_ref = refs[-2], refs[-1], refs[-3]
        fill(left, refs[:nl], start)
        fill(right, refs[nl : nl + nr])

        @pl.loop(0, lw // step)
        def _(i):
            at = pl.ds(pl.multiple_of(i * step, step), step)
            value = lax.dot_general(
                left[:, at], right[...], (((0,), (0,)), ((), ())), preferred_element_type=F32
            )
            out_ref[at, :] = value.astype(out_dtype)

    return vmem_call(
        kernel,
        [shaped((lw, rw), out_dtype)],
        list(lefts) + list(rights),
        scratch=[pltpu.VMEM((rows, lw), BF), pltpu.VMEM((rows, rw), BF)],
        flops=2 * rows * lw * rw,
    )[0]


def back_stage(grads, slopes, down):
    count = len(slopes)
    hidden = down[0].shape[1]

    def kernel(*refs):
        g0, g1 = refs[:count], refs[count : 2 * count]
        slope = refs[2 * count : 3 * count]
        down0, down1 = refs[3 * count : 3 * count + 2]
        outs = refs[3 * count + 2 :]
        for b in range(count):
            value = jnp.dot(g0[b][...], down0[...], preferred_element_type=F32)
            value = value + jnp.dot(g1[b][...], down1[...], preferred_element_type=F32)
            outs[b][...] = (value * slope[b][...].astype(F32)).astype(BF)

    rows = sum(s.shape[0] for s in slopes)
    return vmem_call(
        kernel,
        [shaped(s.shape, BF) for s in slopes],
        list(grads[0]) + list(grads[1]) + list(slopes) + list(down),
        flops=4 * rows * down[0].shape[0] * hidden,
    )


def score_stage(flag, rolled, sums, pool_col, pool_row, head, out_w, list_hot, corrected):
    tok, width = rolled.shape
    half = width // 2
    cands, lists = list_hot.shape
    units = sum(h.shape[0] for h in head)
    per_half = len(sums) // 2
    nh = len(head)

    def kernel(*refs):
        flag_ref, rolled_ref = refs[:2]
        sum_refs = refs[2 : 2 + 2 * per_half]
        rest = refs[2 + 2 * per_half :]
        pool_row_ref = rest[0]
        head_refs = rest[1 : 1 + nh]
        out_refs = rest[1 + nh : 1 + 2 * nh]
        list_ref, corr_ref = rest[1 + 2 * nh : 3 + 2 * nh]
        normed_ref, inv_ref, pooled_ref, act_ref, exp_ref, tot_ref = rest[3 + 2 * nh :]
        mixed = []
        for h in range(2):
            value = rolled_ref[:, h * half : (h + 1) * half].astype(F32)
            for ref in sum_refs[h * per_half : (h + 1) * per_half]:
                value = value + ref[...].astype(F32)
            mixed.append(value)
        square = sum(jnp.sum(m * m, axis=1, keepdims=True) for m in mixed)
        inv = lax.rsqrt(square * (1.0 / width) + 1e-06)
        inv_ref[...] = inv
        hot = (
            lax.broadcasted_iota(jnp.int32, (cands, tok), 0) == pool_row_ref[...]
        ).astype(F32)
        counts = jnp.sum(hot, axis=1, keepdims=True)
        pooled = []
        for h in range(2):
            normed = mixed[h] * inv
            normed_ref[:, h * half : (h + 1) * half] = normed
            pooled.append(
                jnp.dot(
                    hot, normed, precision=lax.Precision.HIGHEST, preferred_element_type=F32
                )
                / counts
            )
        swapped = flag_ref[0] != 0
        low = jnp.where(swapped, pooled[1], pooled[0]).astype(BF)
        high = jnp.where(swapped, pooled[0], pooled[1]).astype(BF)
        pooled_ref[:, :half] = low
        pooled_ref[:, half:] = high
        both = pooled_ref[...]
        scores = jnp.zeros((cands, 1), F32)
        at = 0
        for head_ref, out_ref in zip(head_refs, out_refs):
            size = head_ref.shape[0]
            act = jnp.tanh(
                lax.dot_general(
                    both, head_ref[...], (((1,), (1,)), ((), ())), preferred_element_type=F32
                )
            )
            act_ref[:, at : at + size] = act
            scores = scores + jnp.sum(act * out_ref[...], axis=1, keepdims=True)
            at += size
        exp_scores = jnp.exp(scores)
        exp_ref[...] = exp_scores
        tot_ref[0:1, :] = jnp.sum(exp_scores * list_ref[...], axis=0, keepdims=True)
        tot_ref[1:2, :] = jnp.sum(corr_ref[...] * scores * list_ref[...], axis=0, keepdims=True)

    return vmem_call(
        kernel,
        [
            shaped((tok, width), F32),
            shaped((tok, 1), F32),
            shaped((cands, width), BF),
            shaped((cands, units), F32),
            shaped((cands, 1), F32),
            shaped((2, lists), F32),
        ],
        [flag, rolled] + sums + [pool_row] + head + out_w + [list_hot, corrected],
        flops=4 * cands * width * units,
        smem=1,
    )


def grad_stage(
    flag, own, other, clicks, normed, inv, pooled, head_act, exp_scores, pool_col, pool_row,
    head, out_w, list_hot, corrected,
):
    tok, width = normed.shape
    half = width // 2
    cands, lists = list_hot.shape
    nh = len(head)

    def kernel(*refs):
        (flag_ref, own_ref, other_ref, click_ref, normed_ref, inv_ref, pooled_ref, act_ref,
         exp_ref, pool_col_ref, pool_row_ref) = refs[:11]
        head_refs = refs[11 : 11 + nh]
        out_refs = refs[11 + nh : 11 + 2 * nh]
        list_ref, corr_ref = refs[11 + 2 * nh : 13 + 2 * nh]
        loss_ref, low_ref, high_ref, packed_ref = refs[13 + 2 * nh :]
        totals = own_ref[...] + other_ref[...]
        exp_total, cross_total = totals[0:1], totals[1:2]
        click_total = click_ref[...]
        loss_ref[...] = jnp.sum(
            click_total * jnp.log(exp_total) - cross_total, axis=1, keepdims=True
        )
        ratio = click_total / exp_total
        cand = (
            jnp.sum(list_ref[...] * ratio, axis=1, keepdims=True) * exp_ref[...] - corr_ref[...]
        )
        back = jnp.zeros((cands, width), F32)
        at = 0
        for head_ref, out_ref in zip(head_refs, out_refs):
            size = head_ref.shape[0]
            act = act_ref[:, at : at + size]
            hid = (cand * out_ref[...] * (1.0 - act * act)).astype(BF)
            back = back + jnp.dot(hid, head_ref[...], preferred_element_type=F32)
            at += size
        hot_row = (
            lax.broadcasted_iota(jnp.int32, (cands, tok), 0) == pool_row_ref[...]
        ).astype(F32)
        back = back / jnp.sum(hot_row, axis=1, keepdims=True)
        swapped = flag_ref[0] != 0
        parts = [
            jnp.where(swapped, back[:, half:], back[:, :half]),
            jnp.where(swapped, back[:, :half], back[:, half:]),
        ]
        hot = (
            lax.broadcasted_iota(jnp.int32, (tok, cands), 1) == pool_col_ref[...]
        ).astype(F32)
        grads = [
            jnp.dot(hot, p, precision=lax.Precision.HIGHEST, preferred_element_type=F32)
            for p in parts
        ]
        mean = sum(
            jnp.sum(g * normed_ref[:, h * half : (h + 1) * half], axis=1, keepdims=True)
            for h, g in enumerate(grads)
        ) * (1.0 / width)
        for h, ref in enumerate((low_ref, high_ref)):
            n = normed_ref[:, h * half : (h + 1) * half]
            ref[...] = (inv_ref[...] * (grads[h] - n * mean)).astype(BF)
        packed_ref[:, :width] = pooled_ref[...]
        top = cand.astype(BF)
        rest = cand - top.astype(F32)
        middle = rest.astype(BF)
        bottom = rest - middle.astype(F32)
        lane = lax.broadcasted_iota(jnp.int32, (cands, 128), 1)
        packed_ref[:, width:] = jnp.where(
            lane == 0,
            top.astype(F32),
            jnp.where(lane == 1, middle.astype(F32), jnp.where(lane == 2, bottom, 0.0)),
        ).astype(BF)

    return vmem_call(
        kernel,
        [
            shaped((1, 1), F32),
            shaped((tok, half), BF),
            shaped((tok, half), BF),
            shaped((cands, width + 128), BF),
        ],
        [flag, own, other, clicks, normed, inv, pooled, head_act, exp_scores, pool_col, pool_row]
        + head + out_w + [list_hot, corrected],
        flops=4 * cands * width * sum(h.shape[0] for h in head),
        smem=1,
    )


def head_stage(order, blocks, head, out_w):
    count = len(blocks)
    rows_each, packed_width = blocks[0].shape
    total = order.shape[0]
    units, width = head.shape
    each = sum(b.shape[0] for b in blocks) // total

    def kernel(order_ref, *refs):
        block_refs = refs[:count]
        head_ref, out_ref, grad_ref, out_grad_ref, buffer = refs[count:]
        j = 0
        for ref in block_refs:
            for piece in range(ref.shape[0] // each):
                at = pl.multiple_of(order_ref[j] * each, each)
                buffer[pl.ds(at, each), :] = ref[pl.ds(piece * each, each), :]
                j += 1
        pooled = buffer[:, :width]
        act = jnp.tanh(
            lax.dot_general(
                pooled, head_ref[...], (((1,), (1,)), ((), ())), preferred_element_type=F32
            )
        )
        tail = buffer[:, width:].astype(F32)
        cand = tail[:, 0:1] + tail[:, 1:2] + tail[:, 2:3]
        hid = (cand * out_ref[...] * (1.0 - act * act)).astype(BF)
        out_grad_ref[...] = jnp.sum(cand * act, axis=0, keepdims=True)
        grad_ref[...] = lax.dot_general(
            hid, pooled, (((0,), (0,)), ((), ())), preferred_element_type=F32
        )

    return vmem_call(
        kernel,
        [shaped((units, width), F32), shaped((1, units), F32)],
        [order] + blocks + [head, out_w],
        scratch=[pltpu.VMEM((total * each, packed_width), BF)],
        flops=4 * total * each * width * units,
        smem=1,
    )


def after(value, *others):
    return lax.optimization_barrier((value,) + others)[0]


def dense_local(
    tokens,
    route_ids,
    route_weights,
    up_weight,
    down_weight,
    head_weight,
    out_weight,
    pool_ids,
    list_ids,
    clicks,
    ranks,
    alpha_table,
    beta_table,
):
    n_exp = lax.axis_size("expert")
    dp_index = lax.axis_index("dp")
    exp_index = lax.axis_index("expert")
    ring = Ring(n_exp)
    last = ring.half
    tok, width = tokens.shape
    half = width // 2
    cands = list_ids.shape[1]
    units = head_weight.shape[0]
    across = lambda x: lax.ppermute(x, "dp", [(0, 1), (1, 0)])
    second = dp_index != 0
    flag = dp_index.astype(jnp.int32).reshape(1)

    up = [up_weight[0], across(up_weight[0])]
    rolled = jnp.where(second, jnp.roll(tokens, half, axis=1), tokens)

    mine, theirs = [rolled], [ring.swap(rolled)]
    mine_swapped, theirs_swapped = [None], [None]
    for r in range(1, last + 1):
        outgoing = after(mine[-1], up[1]) if r == last else mine[-1]
        mine.append(ring.send(outgoing))
        mine_swapped.append(ring.swap(mine[-1]))
        if r < last:
            theirs.append(ring.send(theirs[-1]))
            theirs_swapped.append(ring.swap(theirs[-1]))

    down = [down_weight[0], across(after(down_weight[0], up[1]))]
    core = exp_index % 2
    pick = lambda x: lax.dynamic_slice_in_dim(x, core * (units // 2), units // 2, axis=0)
    head_came = across(pick(after(head_weight, down[1])))
    head = [head_weight, head_came, ring.swap(head_came)]
    out_came = across(pick(out_weight))
    out_w = [o[None, :] for o in (out_weight, out_came, ring.swap(out_came))]

    chosen = route_ids.T[:, None, :] == jnp.arange(n_exp, dtype=jnp.int32)[None, :, None]
    weight_of = jnp.sum(jnp.where(chosen, route_weights.T[:, None, :], 0.0), axis=0)
    weight_of = after(weight_of, mine[1])
    arrived = lax.all_to_all(weight_of, "expert", split_axis=0, concat_axis=0, tiled=True)
    order = lax.dynamic_index_in_dim(jnp.asarray(ring.table), exp_index, keepdims=False)
    weights = arrived[order].T

    rank_hot = (ranks[0][:, None] == jnp.arange(RANKS, dtype=jnp.int32)[None, :]).astype(F32)
    alpha_of = jnp.sum(rank_hot * alpha_table[None, :], axis=1)
    beta_of = jnp.sum(rank_hot * beta_table[None, :], axis=1)
    corrected = ((clicks[0].astype(F32) - beta_of) / alpha_of)[:, None]
    list_hot = (list_ids[0][:, None] == jnp.arange(LISTS, dtype=jnp.int32)[None, :]).astype(F32)
    click_own = jnp.sum(corrected * list_hot, axis=0, keepdims=True)
    click_total = click_own + across(click_own)

    acts, slopes = [], []
    first = 0
    for r in range(last + 1):
        if r == 0:
            blocks, groups = [mine[0], theirs[0]], [2]
        elif r < last:
            blocks = [mine[r], theirs[r], mine_swapped[r], theirs_swapped[r]]
            groups = [2, 2]
        else:
            blocks, groups = [mine[r], mine_swapped[r]], [1, 1]
        a, s = hidden_stage(blocks, groups, up, weights, first)
        acts.append(a)
        slopes.append(s)
        first += len(blocks)

    sums = []
    for h in range(2):
        given = ring.swap(project(acts[last][1], down[h]))
        moving = project(acts[last][0], down[h], given)
        for r in reversed(range(1, last)):
            given = ring.swap(project(acts[r][0], down[h]))
            came = ring.send(moving)
            moving = project(acts[r][1], down[h], given, came)
        came = ring.send(moving)
        own = project(acts[0][0], down[h])
        back = (own[tok:].astype(F32) + came[:tok].astype(F32)).astype(BF)
        sums += [own[:tok], came[tok:], ring.swap(back)]

    pool_row, pool_col = pool_ids, pool_ids.T
    normed, inv, pooled, head_act, exp_scores, totals = score_stage(
        flag, rolled, sums, pool_col, pool_row, head, out_w, list_hot, corrected
    )
    list_loss, low, high, packed = grad_stage(
        flag, totals, across(totals), click_total, normed, inv, pooled, head_act, exp_scores,
        pool_col, pool_row, head, out_w, list_hot, corrected,
    )

    def gather_blocks(x):
        blocks = []
        for rounds in ring.gather(x):
            blocks += rounds
        return blocks

    grads = [None, None]
    grads[1] = gather_blocks(high)
    grads[0] = gather_blocks(low)
    flat = lambda lists: [x for part in lists for x in part]
    act_blocks, slope_blocks = flat(acts), flat(slopes)
    sent_down = across(outer_sum(grads[1], act_blocks, BF, half))
    split = len(slope_blocks) - 4
    early = back_stage(
        [grads[0][:split], grads[1][:split]], slope_blocks[:split], down
    )
    late = back_stage([grads[0][split:], grads[1][split:]], slope_blocks[split:], down)
    pre_grads = list(early) + list(late)
    inputs = [mine[0], theirs[0]]
    for r in range(1, last):
        inputs += [mine[r], theirs[r], mine_swapped[r], theirs_swapped[r]]
    inputs += [mine[last], mine_swapped[last]]
    sent_up = across(outer_sum(inputs, pre_grads, BF, half, half))
    down_local = outer_sum(grads[0], act_blocks, F32, half)
    up_local = outer_sum(inputs, pre_grads, F32, half)

    packed = after(packed, grads[0][-1])
    other = across(packed)
    pair = jnp.where(
        second, jnp.concatenate([other, packed]), jnp.concatenate([packed, other])
    )
    grad_head, grad_out = head_stage(order, gather_blocks(pair), head_weight, out_w[0])

    grad_down = (down_local + sent_down.astype(F32)).astype(BF)[None]
    grad_up = (up_local + sent_up.astype(F32)).astype(BF)[None]
    return (grad_up, grad_down, grad_head, grad_out[0], list_loss[0])


def solution(mesh):
    paired = mesh.shape["dp"] == 2 and mesh.shape["expert"] % 4 == 0
    return jax.shard_map(
        dense_local if paired else routed_local,
        mesh=mesh,
        in_specs=(
            P(("dp", "expert"), None),
            P(("dp", "expert"), None),
            P(("dp", "expert"), None),
            P("expert", "dp", None),
            P("expert", "dp", None),
            P("dp", None),
            P("dp"),
            P(("dp", "expert"), None),
            P(("dp", "expert"), None),
            P(("dp", "expert"), None),
            P(("dp", "expert"), None),
            P(),
            P(),
        ),
        out_specs=(
            P("expert", "dp", None),
            P("expert", "dp", None),
            P("dp", None),
            P("dp"),
            P("expert"),
        ),
        check_vma=False,
    )
```

```python
import jax
import jax.numpy as jnp
import numpy as np
from jax import lax
from jax.experimental import pallas as pl
from jax.experimental.pallas import tpu as pltpu
from jax.sharding import PartitionSpec as P

LISTS = 8
RANKS = 32
BF = jnp.bfloat16
F32 = jnp.float32


def ring_order(chips):
    cols = 1
    while cols * cols * 4 <= chips and chips % (cols * 2) == 0:
        cols *= 2
    rows = chips // cols
    if cols == 1:
        return list(range(chips))
    cycle = [(r, 0) for r in range(rows)]
    for turn, r in enumerate(reversed(range(rows))):
        across = list(range(1, cols))
        if turn % 2:
            across.reverse()
        cycle += [(r, c) for c in across]
    return [r * cols + c for r, c in cycle]


class Ring:
    def __init__(self, devices):
        self.chips = devices // 2
        self.half = self.chips // 2
        cycle = ring_order(self.chips)
        count = self.chips
        self.forward = []
        for p in range(count):
            self.forward.append((2 * cycle[p], 2 * cycle[(p + 1) % count]))
            self.forward.append((2 * cycle[p] + 1, 2 * cycle[(p - 1) % count] + 1))
        self.swap_pairs = [(d, d ^ 1) for d in range(devices)]
        position = {chip: p for p, chip in enumerate(cycle)}
        table = np.zeros((devices, devices), np.int32)
        for device in range(devices):
            pos, core = position[device // 2], device % 2
            sign = 1 if core else -1

            def at(step, which):
                return 2 * cycle[(pos + step) % count] + which

            order = [at(0, core), at(0, 1 - core)]
            for r in range(1, self.half):
                order += [at(sign * r, core), at(sign * r, 1 - core)]
                order += [at(-sign * r, 1 - core), at(-sign * r, core)]
            order += [at(self.half, core), at(self.half, 1 - core)]
            table[device] = order
        self.table = table

    def send(self, x):
        return lax.ppermute(x, "expert", self.forward)

    def swap(self, x):
        return lax.ppermute(x, "expert", self.swap_pairs)

    def gather(self, x):
        rows = x.shape[0]
        partner = self.swap(x)
        current = jnp.concatenate([x, partner], axis=0)
        rounds = [[x, partner]]
        for r in range(1, self.half + 1):
            outgoing = current[:rows] if r == self.half else current
            current = self.send(outgoing)
            rounds.append([current, self.swap(current)])
        return rounds


def silu_slope(pre_act):
    sigmoid = jax.nn.sigmoid(pre_act)
    return sigmoid * (1.0 + pre_act * (1.0 - sigmoid))


def routed_local(
    tokens,
    route_ids,
    route_weights,
    up_weight,
    down_weight,
    head_weight,
    out_weight,
    pool_ids,
    list_ids,
    clicks,
    ranks,
    alpha_table,
    beta_table,
):
    tok_count = tokens.shape[0]
    model_width = tokens.shape[1]
    top_count = route_ids.shape[1]
    owners = lax.axis_size("expert")
    capacity = 3 * tok_count * top_count // (2 * owners)
    slot_total = owners * capacity
    flat_ids = route_ids.reshape(-1)
    expert_hot = (flat_ids[:, None] == jnp.arange(owners, dtype=jnp.int32)[None, :]).astype(
        jnp.int32
    )
    running = jnp.cumsum(expert_hot, axis=0) - 1
    slot_index = jnp.sum(running * expert_hot, axis=1)
    target = flat_ids * capacity + slot_index
    token_index = jnp.arange(tok_count * top_count, dtype=jnp.int32) // top_count
    outgoing = (
        jnp.zeros((slot_total, model_width), jnp.bfloat16).at[target].set(tokens[token_index])
    )
    received = lax.all_to_all(
        outgoing.reshape(owners, capacity, model_width),
        "expert",
        split_axis=0,
        concat_axis=0,
        tiled=True,
    )
    inputs = received.reshape(slot_total, model_width)
    up_local = up_weight[0]
    down_local = down_weight[0]
    hidden_width = up_local.shape[1]
    columns = inputs
    pre_act = jnp.dot(
        columns,
        lax.all_gather(up_local, "dp", axis=0, tiled=True),
        preferred_element_type=jnp.float32,
    )
    activated = jax.nn.silu(pre_act).astype(jnp.bfloat16)
    expert_out = lax.dot_general(
        activated,
        lax.all_gather(down_local, "dp", axis=0, tiled=True),
        (((1,), (1,)), ((), ())),
        preferred_element_type=jnp.float32,
    ).astype(jnp.bfloat16)
    returned = lax.all_to_all(
        expert_out.reshape(owners, capacity, model_width),
        "expert",
        split_axis=0,
        concat_axis=0,
        tiled=True,
    ).reshape(slot_total, model_width)
    routed_rows = returned[target].reshape(tok_count, top_count, model_width)
    routed = jnp.sum(route_weights[:, :, None] * routed_rows.astype(jnp.float32), axis=1)
    mixed = tokens.astype(jnp.float32) + routed
    inv_rms = lax.rsqrt(jnp.mean(mixed * mixed, axis=1, keepdims=True) + 1e-06)
    normed = mixed * inv_rms
    cand_count = list_ids.shape[1]
    member = (pool_ids[0][:, None] == jnp.arange(cand_count, dtype=jnp.int32)[None, :]).astype(
        jnp.float32
    )
    token_counts = jnp.sum(member, axis=0)
    pooled_sum = lax.dot_general(
        member,
        normed,
        (((0,), (0,)), ((), ())),
        precision=lax.Precision.HIGHEST,
        preferred_element_type=jnp.float32,
    )
    pooled = (pooled_sum / token_counts[:, None]).astype(jnp.bfloat16)
    all_pooled = lax.all_gather(pooled, "dp", axis=0, tiled=True)
    head_act = jnp.tanh(
        lax.dot_general(
            all_pooled, head_weight, (((1,), (1,)), ((), ())), preferred_element_type=jnp.float32
        )
    )
    part_score = jnp.sum(head_act * out_weight[None, :], axis=1)
    rank_hot = (ranks[0][:, None] == jnp.arange(RANKS, dtype=jnp.int32)[None, :]).astype(
        jnp.float32
    )
    alpha_of = jnp.sum(rank_hot * alpha_table[None, :], axis=1)
    beta_of = jnp.sum(rank_hot * beta_table[None, :], axis=1)
    corrected = (clicks[0].astype(jnp.float32) - beta_of) / alpha_of
    list_hot = (list_ids[0][:, None] == jnp.arange(LISTS, dtype=jnp.int32)[None, :]).astype(
        jnp.float32
    )
    group_corrected, group_lists = (
        lax.all_gather(corrected, "dp", axis=0, tiled=True),
        lax.all_gather(list_hot, "dp", axis=0, tiled=True),
    )
    group_scores = lax.psum(part_score, "dp")
    exp_scores = jnp.exp(group_scores)
    exp_total = jnp.sum(exp_scores[:, None] * group_lists, axis=0)
    click_total = jnp.sum(group_corrected[:, None] * group_lists, axis=0)
    cross_total = jnp.sum((group_corrected * group_scores)[:, None] * group_lists, axis=0)
    list_loss = jnp.sum(click_total * jnp.log(exp_total) - cross_total).reshape(1)
    group_grad = (
        jnp.sum(group_lists * (click_total / exp_total)[None, :], axis=1) * exp_scores
        - group_corrected
    )
    hid_grad = (group_grad[:, None] * out_weight[None, :] * (1.0 - head_act * head_act)).astype(
        jnp.bfloat16
    )
    head_term = lax.dot_general(
        hid_grad, all_pooled, (((0,), (0,)), ((), ())), preferred_element_type=jnp.float32
    )
    out_term = jnp.sum(group_grad[:, None] * head_act, axis=0)
    grad_head, grad_out = (
        lax.psum(head_term.astype(jnp.bfloat16), "expert").astype(jnp.float32),
        lax.psum(out_term.astype(jnp.bfloat16), "expert").astype(jnp.float32),
    )
    pooled_grad = lax.psum_scatter(
        jnp.dot(hid_grad, head_weight, preferred_element_type=jnp.float32).astype(jnp.bfloat16),
        "dp",
        scatter_dimension=0,
        tiled=True,
    ).astype(jnp.float32)
    normed_grad = jnp.dot(
        member,
        pooled_grad / token_counts[:, None],
        precision=lax.Precision.HIGHEST,
        preferred_element_type=jnp.float32,
    )
    mixed_grad = inv_rms * (
        normed_grad - normed * jnp.mean(normed_grad * normed, axis=1, keepdims=True)
    )
    cotangent = (
        (route_weights[:, :, None] * mixed_grad[:, None, :])
        .astype(jnp.bfloat16)
        .reshape(tok_count * top_count, model_width)
    )
    outgoing_grad = jnp.zeros((slot_total, model_width), jnp.bfloat16).at[target].set(cotangent)
    slot_grad = lax.all_to_all(
        outgoing_grad.reshape(owners, capacity, model_width),
        "expert",
        split_axis=0,
        concat_axis=0,
        tiled=True,
    ).reshape(slot_total, model_width)
    columns = slot_grad
    act_grad = jnp.dot(
        columns,
        lax.all_gather(down_local, "dp", axis=0, tiled=True),
        preferred_element_type=jnp.float32,
    )
    pre_grad = (act_grad * silu_slope(pre_act)).astype(jnp.bfloat16)
    up_term = lax.dot_general(
        inputs, pre_grad, (((0,), (0,)), ((), ())), preferred_element_type=jnp.float32
    )
    down_term = lax.dot_general(
        slot_grad, activated, (((0,), (0,)), ((), ())), preferred_element_type=jnp.float32
    )
    summed = lax.psum_scatter(
        jnp.concatenate([up_term, down_term], axis=1).astype(jnp.bfloat16),
        "dp",
        scatter_dimension=0,
        tiled=True,
    ).astype(jnp.float32)
    grad_up = summed[:, :hidden_width].astype(jnp.bfloat16)[None]
    grad_down = summed[:, hidden_width:].astype(jnp.bfloat16)[None]
    return (grad_up, grad_down, grad_head, grad_out, list_loss)


SPARE_VMEM = 6 * 1024 * 1024


def padded_bytes(x):
    lead = int(np.prod(x.shape[:-2])) if len(x.shape) > 2 else 1
    rows = -(-x.shape[-2] // 16) * 16 if len(x.shape) > 1 else 1
    return lead * rows * (-(-x.shape[-1] // 128) * 128) * x.dtype.itemsize


def vmem_call(kernel, outs, args, scratch=(), flops=0, smem=0):
    held = sum(padded_bytes(a) for a in list(args)[smem:] + list(outs))
    held += sum(int(np.prod(b.shape)) * jnp.dtype(b.dtype).itemsize for b in scratch)
    specs = [pl.BlockSpec(memory_space=pltpu.SMEM)] * smem + [
        pl.BlockSpec(memory_space=pltpu.VMEM)
    ] * (len(args) - smem)
    moved = sum(a.size * a.dtype.itemsize for a in args) + sum(
        o.size * o.dtype.itemsize for o in outs
    )
    return pl.pallas_call(
        kernel,
        out_shape=outs,
        in_specs=specs,
        out_specs=[pl.BlockSpec(memory_space=pltpu.VMEM)] * len(outs),
        scratch_shapes=list(scratch),
        cost_estimate=pl.CostEstimate(flops=flops, bytes_accessed=moved, transcendentals=0),
        compiler_params=pltpu.CompilerParams(vmem_limit_bytes=held + SPARE_VMEM),
    )(*args)


def shaped(shape, dtype):
    return jax.ShapeDtypeStruct(shape, dtype)


def fill(buffer, refs, start=0):
    at = 0
    for ref in refs:
        buffer[pl.ds(at, ref.shape[0]), :] = ref[:, start : start + buffer.shape[1]]
        at += ref.shape[0]


def dot_rows(a, b):
    return lax.dot_general(a, b, (((1,), (1,)), ((), ())), preferred_element_type=F32)


def hidden_stage(blocks, groups, up, weights, first):
    count = len(blocks)
    tok, width = blocks[0].shape
    hidden = up[0].shape[0]
    half = width // 2
    rows = count * tok
    sizes = [g * tok for g in groups]

    def kernel(*refs):
        xs, (up0, up1, w_ref) = refs[:count], refs[count : count + 3]
        act_refs = refs[count + 3 : count + 3 + len(groups)]
        slope_refs = refs[count + 3 + len(groups) : count + 3 + 2 * len(groups)]
        buffer = refs[-1]
        fill(buffer, xs)
        at, j = 0, 0
        for index, g in enumerate(groups):
            x = buffer[pl.ds(at, g * tok), :]
            pre = dot_rows(x[:, :half], up0[...]) + dot_rows(x[:, half:], up1[...])
            sig = 1.0 / (1.0 + jnp.exp(-pre))
            for b in range(g):
                w = w_ref[:, first + j : first + j + 1]
                p = pre[b * tok : (b + 1) * tok]
                s = sig[b * tok : (b + 1) * tok]
                ws = w * s
                act_refs[index][pl.ds(b * tok, tok), :] = (ws * p).astype(BF)
                slope_refs[index][pl.ds(b * tok, tok), :] = (ws * (1.0 + p * (1.0 - s))).astype(BF)
                j += 1
            at += g * tok

    outs = [shaped((s, hidden), BF) for s in sizes]
    result = vmem_call(
        kernel,
        outs + outs,
        list(blocks) + [up[0], up[1], weights],
        scratch=[pltpu.VMEM((rows, width), BF)],
        flops=2 * rows * width * hidden,
    )
    return result[: len(groups)], result[len(groups) :]


def project(act, down, *adds):
    total = jnp.dot(act, down, preferred_element_type=F32)
    for add in adds:
        missing = act.shape[0] - add.shape[0]
        total = total + jnp.pad(add, ((missing, 0), (0, 0))).astype(F32)
    return total


def outer_sum(lefts, rights, out_dtype, rw, start=0):
    nl, nr = len(lefts), len(rights)
    rows = sum(a.shape[0] for a in lefts)
    lw = lefts[0].shape[1]

    def kernel(*refs):
        out_ref, left, right = refs[-3:]
        fill(left, refs[:nl])
        fill(right, refs[nl : nl + nr], start)
        at = 0
        while at < lw:
            size = min(256, lw - at)
            value = lax.dot_general(
                left[:, at : at + size],
                right[...],
                (((0,), (0,)), ((), ())),
                preferred_element_type=F32,
            )
            out_ref[at : at + size, :] = value.astype(out_dtype)
            at += size

    return vmem_call(
        kernel,
        [shaped((lw, rw), out_dtype)],
        list(lefts) + list(rights),
        scratch=[pltpu.VMEM((rows, lw), BF), pltpu.VMEM((rows, rw), BF)],
        flops=2 * rows * lw * rw,
    )[0]


def back_stage(grads, slopes, down):
    count = len(slopes)
    hidden = down[0].shape[0]

    def kernel(*refs):
        g0, g1 = refs[:count], refs[count : 2 * count]
        slope = refs[2 * count : 3 * count]
        down0, down1 = refs[3 * count : 3 * count + 2]
        outs = refs[3 * count + 2 :]
        for b in range(count):
            value = dot_rows(g0[b][...], down0[...]) + dot_rows(g1[b][...], down1[...])
            outs[b][...] = (value * slope[b][...].astype(F32)).astype(BF)

    rows = sum(s.shape[0] for s in slopes)
    return vmem_call(
        kernel,
        [shaped(s.shape, BF) for s in slopes],
        list(grads[0]) + list(grads[1]) + list(slopes) + list(down),
        flops=4 * rows * down[0].shape[1] * hidden,
    )


def score_stage(flag, rolled, sums, pool_col, pool_row, head, out_w, list_hot, corrected):
    tok, width = rolled.shape
    half = width // 2
    cands, lists = list_hot.shape
    units = sum(h.shape[0] for h in head)
    per_half = len(sums) // 2
    nh = len(head)

    def kernel(*refs):
        flag_ref, rolled_ref = refs[:2]
        sum_refs = refs[2 : 2 + 2 * per_half]
        rest = refs[2 + 2 * per_half :]
        pool_row_ref = rest[0]
        head_refs = rest[1 : 1 + nh]
        out_refs = rest[1 + nh : 1 + 2 * nh]
        list_ref, corr_ref = rest[1 + 2 * nh : 3 + 2 * nh]
        normed_ref, inv_ref, pooled_ref, act_ref, exp_ref, tot_ref = rest[3 + 2 * nh :]
        mixed = []
        for h in range(2):
            value = rolled_ref[:, h * half : (h + 1) * half].astype(F32)
            for ref in sum_refs[h * per_half : (h + 1) * per_half]:
                value = value + ref[...].astype(F32)
            mixed.append(value)
        square = sum(jnp.sum(m * m, axis=1, keepdims=True) for m in mixed)
        inv = lax.rsqrt(square * (1.0 / width) + 1e-06)
        inv_ref[...] = inv
        hot = (
            lax.broadcasted_iota(jnp.int32, (cands, tok), 0) == pool_row_ref[...]
        ).astype(F32)
        counts = jnp.sum(hot, axis=1, keepdims=True)
        pooled = []
        for h in range(2):
            normed = mixed[h] * inv
            normed_ref[:, h * half : (h + 1) * half] = normed
            pooled.append(
                jnp.dot(
                    hot, normed, precision=lax.Precision.HIGHEST, preferred_element_type=F32
                )
                / counts
            )
        swapped = flag_ref[0] != 0
        low = jnp.where(swapped, pooled[1], pooled[0]).astype(BF)
        high = jnp.where(swapped, pooled[0], pooled[1]).astype(BF)
        pooled_ref[:, :half] = low
        pooled_ref[:, half:] = high
        both = pooled_ref[...]
        scores = jnp.zeros((cands, 1), F32)
        at = 0
        for head_ref, out_ref in zip(head_refs, out_refs):
            size = head_ref.shape[0]
            act = jnp.tanh(
                lax.dot_general(
                    both, head_ref[...], (((1,), (1,)), ((), ())), preferred_element_type=F32
                )
            )
            act_ref[:, at : at + size] = act
            scores = scores + jnp.sum(act * out_ref[...], axis=1, keepdims=True)
            at += size
        exp_scores = jnp.exp(scores)
        exp_ref[...] = exp_scores
        tot_ref[0:1, :] = jnp.sum(exp_scores * list_ref[...], axis=0, keepdims=True)
        tot_ref[1:2, :] = jnp.sum(corr_ref[...] * scores * list_ref[...], axis=0, keepdims=True)

    return vmem_call(
        kernel,
        [
            shaped((tok, width), F32),
            shaped((tok, 1), F32),
            shaped((cands, width), BF),
            shaped((cands, units), F32),
            shaped((cands, 1), F32),
            shaped((2, lists), F32),
        ],
        [flag, rolled] + sums + [pool_row] + head + out_w + [list_hot, corrected],
        flops=4 * cands * width * units,
        smem=1,
    )


def grad_stage(
    flag, own, other, clicks, normed, inv, pooled, head_act, exp_scores, pool_col, pool_row,
    head, out_w, list_hot, corrected,
):
    tok, width = normed.shape
    half = width // 2
    cands, lists = list_hot.shape
    nh = len(head)

    def kernel(*refs):
        (flag_ref, own_ref, other_ref, click_ref, normed_ref, inv_ref, pooled_ref, act_ref,
         exp_ref, pool_col_ref, pool_row_ref) = refs[:11]
        head_refs = refs[11 : 11 + nh]
        out_refs = refs[11 + nh : 11 + 2 * nh]
        list_ref, corr_ref = refs[11 + 2 * nh : 13 + 2 * nh]
        loss_ref, low_ref, high_ref, packed_ref = refs[13 + 2 * nh :]
        totals = own_ref[...] + other_ref[...]
        exp_total, cross_total = totals[0:1], totals[1:2]
        click_total = click_ref[...]
        loss_ref[...] = jnp.sum(
            click_total * jnp.log(exp_total) - cross_total, axis=1, keepdims=True
        )
        ratio = click_total / exp_total
        cand = (
            jnp.sum(list_ref[...] * ratio, axis=1, keepdims=True) * exp_ref[...] - corr_ref[...]
        )
        back = jnp.zeros((cands, width), F32)
        at = 0
        for head_ref, out_ref in zip(head_refs, out_refs):
            size = head_ref.shape[0]
            act = act_ref[:, at : at + size]
            hid = (cand * out_ref[...] * (1.0 - act * act)).astype(BF)
            back = back + jnp.dot(hid, head_ref[...], preferred_element_type=F32)
            at += size
        hot_row = (
            lax.broadcasted_iota(jnp.int32, (cands, tok), 0) == pool_row_ref[...]
        ).astype(F32)
        back = back / jnp.sum(hot_row, axis=1, keepdims=True)
        swapped = flag_ref[0] != 0
        parts = [
            jnp.where(swapped, back[:, half:], back[:, :half]),
            jnp.where(swapped, back[:, :half], back[:, half:]),
        ]
        hot = (
            lax.broadcasted_iota(jnp.int32, (tok, cands), 1) == pool_col_ref[...]
        ).astype(F32)
        grads = [
            jnp.dot(hot, p, precision=lax.Precision.HIGHEST, preferred_element_type=F32)
            for p in parts
        ]
        mean = sum(
            jnp.sum(g * normed_ref[:, h * half : (h + 1) * half], axis=1, keepdims=True)
            for h, g in enumerate(grads)
        ) * (1.0 / width)
        for h, ref in enumerate((low_ref, high_ref)):
            n = normed_ref[:, h * half : (h + 1) * half]
            ref[...] = (inv_ref[...] * (grads[h] - n * mean)).astype(BF)
        packed_ref[:, :width] = pooled_ref[...]
        top = cand.astype(BF)
        rest = cand - top.astype(F32)
        middle = rest.astype(BF)
        bottom = rest - middle.astype(F32)
        lane = lax.broadcasted_iota(jnp.int32, (cands, 128), 1)
        packed_ref[:, width:] = jnp.where(
            lane == 0,
            top.astype(F32),
            jnp.where(lane == 1, middle.astype(F32), jnp.where(lane == 2, bottom, 0.0)),
        ).astype(BF)

    return vmem_call(
        kernel,
        [
            shaped((1, 1), F32),
            shaped((tok, half), BF),
            shaped((tok, half), BF),
            shaped((cands, width + 128), BF),
        ],
        [flag, own, other, clicks, normed, inv, pooled, head_act, exp_scores, pool_col, pool_row]
        + head + out_w + [list_hot, corrected],
        flops=4 * cands * width * sum(h.shape[0] for h in head),
        smem=1,
    )


def head_stage(order, blocks, head, out_w):
    count = len(blocks)
    rows_each, packed_width = blocks[0].shape
    total = order.shape[0]
    units, width = head.shape
    each = sum(b.shape[0] for b in blocks) // total

    def kernel(order_ref, *refs):
        block_refs = refs[:count]
        head_ref, out_ref, grad_ref, out_grad_ref, buffer = refs[count:]
        j = 0
        for ref in block_refs:
            for piece in range(ref.shape[0] // each):
                at = pl.multiple_of(order_ref[j] * each, each)
                buffer[pl.ds(at, each), :] = ref[pl.ds(piece * each, each), :]
                j += 1
        pooled = buffer[:, :width]
        act = jnp.tanh(
            lax.dot_general(
                pooled, head_ref[...], (((1,), (1,)), ((), ())), preferred_element_type=F32
            )
        )
        tail = buffer[:, width:].astype(F32)
        cand = tail[:, 0:1] + tail[:, 1:2] + tail[:, 2:3]
        hid = (cand * out_ref[...] * (1.0 - act * act)).astype(BF)
        out_grad_ref[...] = jnp.sum(cand * act, axis=0, keepdims=True)
        grad_ref[...] = lax.dot_general(
            hid, pooled, (((0,), (0,)), ((), ())), preferred_element_type=F32
        )

    return vmem_call(
        kernel,
        [shaped((units, width), F32), shaped((1, units), F32)],
        [order] + blocks + [head, out_w],
        scratch=[pltpu.VMEM((total * each, packed_width), BF)],
        flops=4 * total * each * width * units,
        smem=1,
    )


def after(value, *others):
    return lax.optimization_barrier((value,) + others)[0]


def dense_local(
    tokens,
    route_ids,
    route_weights,
    up_weight,
    down_weight,
    head_weight,
    out_weight,
    pool_ids,
    list_ids,
    clicks,
    ranks,
    alpha_table,
    beta_table,
):
    n_exp = lax.axis_size("expert")
    dp_index = lax.axis_index("dp")
    exp_index = lax.axis_index("expert")
    ring = Ring(n_exp)
    last = ring.half
    tok, width = tokens.shape
    half = width // 2
    cands = list_ids.shape[1]
    units = head_weight.shape[0]
    across = lambda x: lax.ppermute(x, "dp", [(0, 1), (1, 0)])
    second = dp_index != 0
    flag = dp_index.astype(jnp.int32).reshape(1)

    up_own, down_own = up_weight[0].T, down_weight[0].T
    up = [up_own, across(up_own)]
    rolled = jnp.where(second, jnp.roll(tokens, half, axis=1), tokens)

    mine, theirs = [rolled], [ring.swap(rolled)]
    mine_swapped, theirs_swapped = [None], [None]
    for r in range(1, last + 1):
        outgoing = after(mine[-1], up[1]) if r == last else mine[-1]
        mine.append(ring.send(outgoing))
        mine_swapped.append(ring.swap(mine[-1]))
        if r < last:
            theirs.append(ring.send(theirs[-1]))
            theirs_swapped.append(ring.swap(theirs[-1]))

    down = [down_own, across(after(down_own, up[1]))]
    core = exp_index % 2
    pick = lambda x: lax.dynamic_slice_in_dim(x, core * (units // 2), units // 2, axis=0)
    head_came = across(pick(after(head_weight, down[1])))
    head = [head_weight, head_came, ring.swap(head_came)]
    out_came = across(pick(out_weight))
    out_w = [o[None, :] for o in (out_weight, out_came, ring.swap(out_came))]

    chosen = route_ids.T[:, None, :] == jnp.arange(n_exp, dtype=jnp.int32)[None, :, None]
    weight_of = jnp.sum(jnp.where(chosen, route_weights.T[:, None, :], 0.0), axis=0)
    weight_of = after(weight_of, mine[1])
    arrived = lax.all_to_all(weight_of, "expert", split_axis=0, concat_axis=0, tiled=True)
    order = lax.dynamic_index_in_dim(jnp.asarray(ring.table), exp_index, keepdims=False)
    weights = arrived[order].T

    rank_hot = (ranks[0][:, None] == jnp.arange(RANKS, dtype=jnp.int32)[None, :]).astype(F32)
    alpha_of = jnp.sum(rank_hot * alpha_table[None, :], axis=1)
    beta_of = jnp.sum(rank_hot * beta_table[None, :], axis=1)
    corrected = ((clicks[0].astype(F32) - beta_of) / alpha_of)[:, None]
    list_hot = (list_ids[0][:, None] == jnp.arange(LISTS, dtype=jnp.int32)[None, :]).astype(F32)
    click_own = jnp.sum(corrected * list_hot, axis=0, keepdims=True)
    click_total = click_own + across(click_own)

    acts, slopes = [], []
    first = 0
    for r in range(last + 1):
        if r == 0:
            blocks, groups = [mine[0], theirs[0]], [1, 1]
        elif r < last:
            blocks = [mine[r], theirs[r], mine_swapped[r], theirs_swapped[r]]
            groups = [2, 2]
        else:
            blocks, groups = [mine[r], mine_swapped[r]], [1, 1]
        a, s = hidden_stage(blocks, groups, up, weights, first)
        acts.append(a)
        slopes.append(s)
        first += len(blocks)

    sums = []
    for h in range(2):
        given = ring.swap(project(acts[last][1], down[h]).astype(BF))
        moving = project(acts[last][0], down[h], given).astype(BF)
        for r in reversed(range(1, last)):
            given = ring.swap(project(acts[r][0], down[h]).astype(BF))
            came = ring.send(moving)
            moving = project(acts[r][1], down[h], given, came).astype(BF)
        came = ring.send(moving)
        back = ring.swap(project(acts[0][1], down[h], came[:tok]).astype(BF))
        sums += [project(acts[0][0], down[h], came[tok:]), back]

    pool_row, pool_col = pool_ids, pool_ids.T
    normed, inv, pooled, head_act, exp_scores, totals = score_stage(
        flag, rolled, sums, pool_col, pool_row, head, out_w, list_hot, corrected
    )
    list_loss, low, high, packed = grad_stage(
        flag, totals, across(totals), click_total, normed, inv, pooled, head_act, exp_scores,
        pool_col, pool_row, head, out_w, list_hot, corrected,
    )

    def gather_blocks(x):
        blocks = []
        for rounds in ring.gather(x):
            blocks += rounds
        return blocks

    grads = [None, None]
    grads[1] = gather_blocks(high)
    grads[0] = gather_blocks(low)
    flat = lambda lists: [x for part in lists for x in part]
    act_blocks, slope_blocks = flat(acts), flat(slopes)
    sent_down = across(outer_sum(act_blocks, grads[1], BF, half))
    split = len(slope_blocks) - 4
    early = back_stage(
        [grads[0][:split], grads[1][:split]], slope_blocks[:split], down
    )
    late = back_stage([grads[0][split:], grads[1][split:]], slope_blocks[split:], down)
    pre_grads = list(early) + list(late)
    inputs = [mine[0], theirs[0]]
    for r in range(1, last):
        inputs += [mine[r], theirs[r], mine_swapped[r], theirs_swapped[r]]
    inputs += [mine[last], mine_swapped[last]]
    sent_up = across(outer_sum(pre_grads, inputs, BF, half, half))
    down_local = outer_sum(act_blocks, grads[0], F32, half)
    up_local = outer_sum(pre_grads, inputs, F32, half)

    packed = after(packed, grads[0][-1])
    other = across(packed)
    pair = jnp.where(
        second, jnp.concatenate([other, packed]), jnp.concatenate([packed, other])
    )
    grad_head, grad_out = head_stage(order, gather_blocks(pair), head_weight, out_w[0])

    grad_down = (down_local + sent_down.astype(F32)).astype(BF).T[None]
    grad_up = (up_local + sent_up.astype(F32)).astype(BF).T[None]
    return (grad_up, grad_down, grad_head, grad_out[0], list_loss[0])


def solution(mesh):
    paired = mesh.shape["dp"] == 2 and mesh.shape["expert"] % 4 == 0
    return jax.shard_map(
        dense_local if paired else routed_local,
        mesh=mesh,
        in_specs=(
            P(("dp", "expert"), None),
            P(("dp", "expert"), None),
            P(("dp", "expert"), None),
            P("expert", "dp", None),
            P("expert", "dp", None),
            P("dp", None),
            P("dp"),
            P(("dp", "expert"), None),
            P(("dp", "expert"), None),
            P(("dp", "expert"), None),
            P(("dp", "expert"), None),
            P(),
            P(),
        ),
        out_specs=(
            P("expert", "dp", None),
            P("expert", "dp", None),
            P("dp", None),
            P("dp"),
            P("expert"),
        ),
        check_vma=False,
    )
```

```python
import jax
import jax.numpy as jnp
import numpy as np
from jax import lax
from jax.experimental import pallas as pl
from jax.experimental.pallas import tpu as pltpu
from jax.sharding import PartitionSpec as P

LISTS = 8
RANKS = 32
BF = jnp.bfloat16
F32 = jnp.float32


def ring_order(chips):
    cols = 1
    while cols * cols * 4 <= chips and chips % (cols * 2) == 0:
        cols *= 2
    rows = chips // cols
    if cols == 1:
        return list(range(chips))
    cycle = [(r, 0) for r in range(rows)]
    for turn, r in enumerate(reversed(range(rows))):
        across = list(range(1, cols))
        if turn % 2:
            across.reverse()
        cycle += [(r, c) for c in across]
    return [r * cols + c for r, c in cycle]


class Ring:
    def __init__(self, devices):
        self.chips = devices // 2
        self.half = self.chips // 2
        cycle = ring_order(self.chips)
        count = self.chips
        self.forward = []
        for p in range(count):
            self.forward.append((2 * cycle[p], 2 * cycle[(p + 1) % count]))
            self.forward.append((2 * cycle[p] + 1, 2 * cycle[(p - 1) % count] + 1))
        self.swap_pairs = [(d, d ^ 1) for d in range(devices)]
        position = {chip: p for p, chip in enumerate(cycle)}
        table = np.zeros((devices, devices), np.int32)
        for device in range(devices):
            pos, core = position[device // 2], device % 2
            sign = 1 if core else -1

            def at(step, which):
                return 2 * cycle[(pos + step) % count] + which

            order = [at(0, core), at(0, 1 - core)]
            for r in range(1, self.half):
                order += [at(sign * r, core), at(sign * r, 1 - core)]
                order += [at(-sign * r, 1 - core), at(-sign * r, core)]
            order += [at(self.half, core), at(self.half, 1 - core)]
            table[device] = order
        self.table = table

    def send(self, x):
        return lax.ppermute(x, "expert", self.forward)

    def swap(self, x):
        return lax.ppermute(x, "expert", self.swap_pairs)

    def gather(self, x):
        rows = x.shape[0]
        partner = self.swap(x)
        current = jnp.concatenate([x, partner], axis=0)
        rounds = [[x, partner]]
        for r in range(1, self.half + 1):
            outgoing = current[:rows] if r == self.half else current
            current = self.send(outgoing)
            rounds.append([current, self.swap(current)])
        return rounds


def silu_slope(pre_act):
    sigmoid = jax.nn.sigmoid(pre_act)
    return sigmoid * (1.0 + pre_act * (1.0 - sigmoid))


def routed_local(
    tokens,
    route_ids,
    route_weights,
    up_weight,
    down_weight,
    head_weight,
    out_weight,
    pool_ids,
    list_ids,
    clicks,
    ranks,
    alpha_table,
    beta_table,
):
    tok_count = tokens.shape[0]
    model_width = tokens.shape[1]
    top_count = route_ids.shape[1]
    owners = lax.axis_size("expert")
    capacity = 3 * tok_count * top_count // (2 * owners)
    slot_total = owners * capacity
    flat_ids = route_ids.reshape(-1)
    expert_hot = (flat_ids[:, None] == jnp.arange(owners, dtype=jnp.int32)[None, :]).astype(
        jnp.int32
    )
    running = jnp.cumsum(expert_hot, axis=0) - 1
    slot_index = jnp.sum(running * expert_hot, axis=1)
    target = flat_ids * capacity + slot_index
    token_index = jnp.arange(tok_count * top_count, dtype=jnp.int32) // top_count
    outgoing = (
        jnp.zeros((slot_total, model_width), jnp.bfloat16).at[target].set(tokens[token_index])
    )
    received = lax.all_to_all(
        outgoing.reshape(owners, capacity, model_width),
        "expert",
        split_axis=0,
        concat_axis=0,
        tiled=True,
    )
    inputs = received.reshape(slot_total, model_width)
    up_local = up_weight[0]
    down_local = down_weight[0]
    hidden_width = up_local.shape[1]
    columns = inputs
    pre_act = jnp.dot(
        columns,
        lax.all_gather(up_local, "dp", axis=0, tiled=True),
        preferred_element_type=jnp.float32,
    )
    activated = jax.nn.silu(pre_act).astype(jnp.bfloat16)
    expert_out = lax.dot_general(
        activated,
        lax.all_gather(down_local, "dp", axis=0, tiled=True),
        (((1,), (1,)), ((), ())),
        preferred_element_type=jnp.float32,
    ).astype(jnp.bfloat16)
    returned = lax.all_to_all(
        expert_out.reshape(owners, capacity, model_width),
        "expert",
        split_axis=0,
        concat_axis=0,
        tiled=True,
    ).reshape(slot_total, model_width)
    routed_rows = returned[target].reshape(tok_count, top_count, model_width)
    routed = jnp.sum(route_weights[:, :, None] * routed_rows.astype(jnp.float32), axis=1)
    mixed = tokens.astype(jnp.float32) + routed
    inv_rms = lax.rsqrt(jnp.mean(mixed * mixed, axis=1, keepdims=True) + 1e-06)
    normed = mixed * inv_rms
    cand_count = list_ids.shape[1]
    member = (pool_ids[0][:, None] == jnp.arange(cand_count, dtype=jnp.int32)[None, :]).astype(
        jnp.float32
    )
    token_counts = jnp.sum(member, axis=0)
    pooled_sum = lax.dot_general(
        member,
        normed,
        (((0,), (0,)), ((), ())),
        precision=lax.Precision.HIGHEST,
        preferred_element_type=jnp.float32,
    )
    pooled = (pooled_sum / token_counts[:, None]).astype(jnp.bfloat16)
    all_pooled = lax.all_gather(pooled, "dp", axis=0, tiled=True)
    head_act = jnp.tanh(
        lax.dot_general(
            all_pooled, head_weight, (((1,), (1,)), ((), ())), preferred_element_type=jnp.float32
        )
    )
    part_score = jnp.sum(head_act * out_weight[None, :], axis=1)
    rank_hot = (ranks[0][:, None] == jnp.arange(RANKS, dtype=jnp.int32)[None, :]).astype(
        jnp.float32
    )
    alpha_of = jnp.sum(rank_hot * alpha_table[None, :], axis=1)
    beta_of = jnp.sum(rank_hot * beta_table[None, :], axis=1)
    corrected = (clicks[0].astype(jnp.float32) - beta_of) / alpha_of
    list_hot = (list_ids[0][:, None] == jnp.arange(LISTS, dtype=jnp.int32)[None, :]).astype(
        jnp.float32
    )
    group_corrected, group_lists = (
        lax.all_gather(corrected, "dp", axis=0, tiled=True),
        lax.all_gather(list_hot, "dp", axis=0, tiled=True),
    )
    group_scores = lax.psum(part_score, "dp")
    exp_scores = jnp.exp(group_scores)
    exp_total = jnp.sum(exp_scores[:, None] * group_lists, axis=0)
    click_total = jnp.sum(group_corrected[:, None] * group_lists, axis=0)
    cross_total = jnp.sum((group_corrected * group_scores)[:, None] * group_lists, axis=0)
    list_loss = jnp.sum(click_total * jnp.log(exp_total) - cross_total).reshape(1)
    group_grad = (
        jnp.sum(group_lists * (click_total / exp_total)[None, :], axis=1) * exp_scores
        - group_corrected
    )
    hid_grad = (group_grad[:, None] * out_weight[None, :] * (1.0 - head_act * head_act)).astype(
        jnp.bfloat16
    )
    head_term = lax.dot_general(
        hid_grad, all_pooled, (((0,), (0,)), ((), ())), preferred_element_type=jnp.float32
    )
    out_term = jnp.sum(group_grad[:, None] * head_act, axis=0)
    grad_head, grad_out = (
        lax.psum(head_term.astype(jnp.bfloat16), "expert").astype(jnp.float32),
        lax.psum(out_term.astype(jnp.bfloat16), "expert").astype(jnp.float32),
    )
    pooled_grad = lax.psum_scatter(
        jnp.dot(hid_grad, head_weight, preferred_element_type=jnp.float32).astype(jnp.bfloat16),
        "dp",
        scatter_dimension=0,
        tiled=True,
    ).astype(jnp.float32)
    normed_grad = jnp.dot(
        member,
        pooled_grad / token_counts[:, None],
        precision=lax.Precision.HIGHEST,
        preferred_element_type=jnp.float32,
    )
    mixed_grad = inv_rms * (
        normed_grad - normed * jnp.mean(normed_grad * normed, axis=1, keepdims=True)
    )
    cotangent = (
        (route_weights[:, :, None] * mixed_grad[:, None, :])
        .astype(jnp.bfloat16)
        .reshape(tok_count * top_count, model_width)
    )
    outgoing_grad = jnp.zeros((slot_total, model_width), jnp.bfloat16).at[target].set(cotangent)
    slot_grad = lax.all_to_all(
        outgoing_grad.reshape(owners, capacity, model_width),
        "expert",
        split_axis=0,
        concat_axis=0,
        tiled=True,
    ).reshape(slot_total, model_width)
    columns = slot_grad
    act_grad = jnp.dot(
        columns,
        lax.all_gather(down_local, "dp", axis=0, tiled=True),
        preferred_element_type=jnp.float32,
    )
    pre_grad = (act_grad * silu_slope(pre_act)).astype(jnp.bfloat16)
    up_term = lax.dot_general(
        inputs, pre_grad, (((0,), (0,)), ((), ())), preferred_element_type=jnp.float32
    )
    down_term = lax.dot_general(
        slot_grad, activated, (((0,), (0,)), ((), ())), preferred_element_type=jnp.float32
    )
    summed = lax.psum_scatter(
        jnp.concatenate([up_term, down_term], axis=1).astype(jnp.bfloat16),
        "dp",
        scatter_dimension=0,
        tiled=True,
    ).astype(jnp.float32)
    grad_up = summed[:, :hidden_width].astype(jnp.bfloat16)[None]
    grad_down = summed[:, hidden_width:].astype(jnp.bfloat16)[None]
    return (grad_up, grad_down, grad_head, grad_out, list_loss)


SPARE_VMEM = 6 * 1024 * 1024


def padded_bytes(x):
    lead = int(np.prod(x.shape[:-2])) if len(x.shape) > 2 else 1
    rows = -(-x.shape[-2] // 16) * 16 if len(x.shape) > 1 else 1
    return lead * rows * (-(-x.shape[-1] // 128) * 128) * x.dtype.itemsize


def vmem_call(kernel, outs, args, scratch=(), flops=0, smem=0):
    held = sum(padded_bytes(a) for a in list(args)[smem:] + list(outs))
    held += sum(int(np.prod(b.shape)) * jnp.dtype(b.dtype).itemsize for b in scratch)
    specs = [pl.BlockSpec(memory_space=pltpu.SMEM)] * smem + [
        pl.BlockSpec(memory_space=pltpu.VMEM)
    ] * (len(args) - smem)
    moved = sum(a.size * a.dtype.itemsize for a in args) + sum(
        o.size * o.dtype.itemsize for o in outs
    )
    return pl.pallas_call(
        kernel,
        out_shape=outs,
        in_specs=specs,
        out_specs=[pl.BlockSpec(memory_space=pltpu.VMEM)] * len(outs),
        scratch_shapes=list(scratch),
        cost_estimate=pl.CostEstimate(flops=flops, bytes_accessed=moved, transcendentals=0),
        compiler_params=pltpu.CompilerParams(vmem_limit_bytes=held + SPARE_VMEM),
    )(*args)


def shaped(shape, dtype):
    return jax.ShapeDtypeStruct(shape, dtype)


def fill(buffer, refs, start=0, limit=None):
    at = 0
    for ref in refs:
        size = limit or ref.shape[0]
        buffer[pl.ds(at, size), :] = ref[:size, start : start + buffer.shape[1]]
        at += size


def dot_rows(a, b):
    return lax.dot_general(a, b, (((1,), (1,)), ((), ())), preferred_element_type=F32)


def pack_stage(tokens, ids, weights, owners):
    tok, width = tokens.shape
    half = width // 2
    per_row = width // tok
    top = ids.shape[0]
    extra = 2 * -(-owners // per_row)
    rows = tok + -(-extra // 8) * 8

    def kernel(tok_ref, id_ref, weight_ref, out_ref):
        swapped = lax.axis_index("dp") != 0
        out_ref[:tok, :half] = jnp.where(swapped, tok_ref[:, half:], tok_ref[:, :half])
        out_ref[:tok, half:] = jnp.where(swapped, tok_ref[:, :half], tok_ref[:, half:])
        lanes = [[] for _ in range(extra)]
        for owner in range(owners):
            value = jnp.zeros((1, tok), F32)
            for k in range(top):
                hit = id_ref[k : k + 1, :] == owner
                value = value + jnp.where(hit, weight_ref[k : k + 1, :], 0.0)
            high = value.astype(BF).astype(F32)
            row = owner // per_row
            lanes[2 * row].append(high)
            lanes[2 * row + 1].append(value - high)
        filled = []
        for row in lanes:
            row += [jnp.zeros((1, tok), F32)] * (per_row - len(row))
            filled.append(jnp.concatenate(row, axis=1))
        filled.append(jnp.zeros((rows - tok - extra, width), F32))
        out_ref[tok:, :] = jnp.concatenate(filled, axis=0).astype(BF)

    return vmem_call(kernel, [shaped((rows, width), BF)], [tokens, ids, weights])[0]


def weight_column(ref, tok, owners, mine):
    width = ref.shape[1]
    per_row = width // tok
    extra = ref[tok:, :].astype(F32)
    row = jnp.zeros((1, tok), F32)
    for owner in range(owners):
        at, lane = 2 * (owner // per_row), (owner % per_row) * tok
        both = extra[at : at + 1, lane : lane + tok] + extra[at + 1 : at + 2, lane : lane + tok]
        row = row + jnp.where(mine == owner, both, 0.0)
    diagonal = lax.broadcasted_iota(jnp.int32, (tok, tok), 0) == lax.broadcasted_iota(
        jnp.int32, (tok, tok), 1
    )
    return jnp.sum(jnp.where(diagonal, row, 0.0), axis=1, keepdims=True)


def hidden_stage(blocks, groups, up, tok, owners):
    count = len(blocks)
    width = blocks[0].shape[1]
    hidden = up[0].shape[0]
    half = width // 2
    rows = count * tok
    sizes = [g * tok for g in groups]

    def kernel(*refs):
        xs, (up0, up1) = refs[:count], refs[count : count + 2]
        act_refs = refs[count + 2 : count + 2 + len(groups)]
        slope_refs = refs[count + 2 + len(groups) : count + 2 + 2 * len(groups)]
        buffer = refs[-1]
        fill(buffer, xs, limit=tok)
        at, j = 0, 0
        for index, g in enumerate(groups):
            x = buffer[pl.ds(at, g * tok), :]
            pre = dot_rows(x[:, :half], up0[...]) + dot_rows(x[:, half:], up1[...])
            sig = 1.0 / (1.0 + jnp.exp(-pre))
            for b in range(g):
                w = weight_column(xs[j], tok, owners, lax.axis_index("expert"))
                p = pre[b * tok : (b + 1) * tok]
                s = sig[b * tok : (b + 1) * tok]
                ws = w * s
                act_refs[index][pl.ds(b * tok, tok), :] = (ws * p).astype(BF)
                slope_refs[index][pl.ds(b * tok, tok), :] = (ws * (1.0 + p * (1.0 - s))).astype(BF)
                j += 1
            at += g * tok

    outs = [shaped((size, hidden), BF) for size in sizes]
    result = vmem_call(
        kernel,
        outs + outs,
        list(blocks) + [up[0], up[1]],
        scratch=[pltpu.VMEM((rows, width), BF)],
        flops=2 * rows * width * hidden,
    )
    return result[: len(groups)], result[len(groups) :]


def project(act, down, *adds):
    total = jnp.dot(act, down, preferred_element_type=F32)
    for add in adds:
        missing = act.shape[0] - add.shape[0]
        total = total + jnp.pad(add, ((missing, 0), (0, 0))).astype(F32)
    return total


def outer_sum(lefts, rights, out_dtype, rw, start=0, limit=None):
    nl, nr = len(lefts), len(rights)
    rows = sum(a.shape[0] for a in lefts)
    lw = lefts[0].shape[1]

    def kernel(*refs):
        out_ref, left, right = refs[-3:]
        fill(left, refs[:nl])
        fill(right, refs[nl : nl + nr], start, limit)
        at = 0
        while at < lw:
            size = min(256, lw - at)
            value = lax.dot_general(
                left[:, at : at + size],
                right[...],
                (((0,), (0,)), ((), ())),
                preferred_element_type=F32,
            )
            out_ref[at : at + size, :] = value.astype(out_dtype)
            at += size

    return vmem_call(
        kernel,
        [shaped((lw, rw), out_dtype)],
        list(lefts) + list(rights),
        scratch=[pltpu.VMEM((rows, lw), BF), pltpu.VMEM((rows, rw), BF)],
        flops=2 * rows * lw * rw,
    )[0]


def back_stage(grads, slopes, down):
    count = len(slopes)
    hidden = down[0].shape[0]

    def kernel(*refs):
        g0, g1 = refs[:count], refs[count : 2 * count]
        slope = refs[2 * count : 3 * count]
        down0, down1 = refs[3 * count : 3 * count + 2]
        outs = refs[3 * count + 2 :]
        for b in range(count):
            value = dot_rows(g0[b][...], down0[...]) + dot_rows(g1[b][...], down1[...])
            outs[b][...] = (value * slope[b][...].astype(F32)).astype(BF)

    rows = sum(s.shape[0] for s in slopes)
    return vmem_call(
        kernel,
        [shaped(s.shape, BF) for s in slopes],
        list(grads[0]) + list(grads[1]) + list(slopes) + list(down),
        flops=4 * rows * down[0].shape[1] * hidden,
    )


def eye(size):
    return lax.broadcasted_iota(jnp.int32, (size, size), 0) == lax.broadcasted_iota(
        jnp.int32, (size, size), 1
    )


def to_column(row):
    return jnp.sum(jnp.where(eye(row.shape[1]), row, 0.0), axis=1, keepdims=True)


def to_row(column):
    return jnp.sum(jnp.where(eye(column.shape[0]), column, 0.0), axis=0, keepdims=True)


def clicks_of(rank_ref, click_ref, alpha_ref, beta_ref):
    rank_row = rank_ref[...]
    hot = (
        lax.broadcasted_iota(jnp.int32, (alpha_ref.shape[1], rank_row.shape[1]), 0) == rank_row
    ).astype(F32)
    alpha = jnp.sum(hot * to_column(alpha_ref[...]), axis=0, keepdims=True)
    beta = jnp.sum(hot * to_column(beta_ref[...]), axis=0, keepdims=True)
    return (click_ref[...].astype(F32) - beta) / alpha


def lists_of(list_ref, count):
    row = list_ref[...]
    return (lax.broadcasted_iota(jnp.int32, (count, row.shape[1]), 0) == row).astype(F32)


def pool_of(pool_ref, cands):
    row = pool_ref[...]
    return (lax.broadcasted_iota(jnp.int32, (cands, row.shape[1]), 0) == row).astype(F32)


def units_of(head_refs, own_ref, other_ref):
    part = head_refs[1].shape[0]
    first = lax.axis_index("expert") % 2 == 0
    low, high = other_ref[:, :part], other_ref[:, part:]
    return [own_ref[...], jnp.where(first, low, high), jnp.where(first, high, low)]


def score_stage(rolled, sums, head, out_w, lists_in):
    width = rolled.shape[1]
    tok = sums[0].shape[0]
    half = width // 2
    cands = lists_in[1].shape[1]
    units = sum(h.shape[0] for h in head)
    per_half = len(sums) // 2

    def kernel(*refs):
        rolled_ref = refs[0]
        sum_refs = refs[1 : 1 + 2 * per_half]
        rest = refs[1 + 2 * per_half :]
        head_refs, out_refs = rest[:3], rest[3:5]
        pool_ref, list_ref, click_ref, rank_ref, alpha_ref, beta_ref = rest[5:11]
        normed_ref, inv_ref, pooled_ref, act_ref, exp_ref, corr_ref, tot_ref = rest[11:]
        mixed = []
        for h in range(2):
            value = rolled_ref[:tok, h * half : (h + 1) * half].astype(F32)
            for ref in sum_refs[h * per_half : (h + 1) * per_half]:
                value = value + ref[...].astype(F32)
            mixed.append(value)
        square = sum(jnp.sum(m * m, axis=1, keepdims=True) for m in mixed)
        inv = lax.rsqrt(square * (1.0 / width) + 1e-06)
        inv_ref[...] = inv
        hot = pool_of(pool_ref, cands)
        counts = jnp.sum(hot, axis=1, keepdims=True)
        pooled = []
        for h in range(2):
            normed = mixed[h] * inv
            normed_ref[:, h * half : (h + 1) * half] = normed
            pooled.append(
                jnp.dot(
                    hot, normed, precision=lax.Precision.HIGHEST, preferred_element_type=F32
                )
                / counts
            )
        swapped = lax.axis_index("dp") != 0
        pooled_ref[:, :half] = jnp.where(swapped, pooled[1], pooled[0]).astype(BF)
        pooled_ref[:, half:] = jnp.where(swapped, pooled[0], pooled[1]).astype(BF)
        both = pooled_ref[...]
        scores = jnp.zeros((cands, 1), F32)
        at = 0
        for head_ref, out_row in zip(head_refs, units_of(head_refs, *out_refs)):
            size = head_ref.shape[0]
            act = jnp.tanh(dot_rows(both, head_ref[...]))
            act_ref[:, at : at + size] = act
            scores = scores + jnp.sum(act * out_row, axis=1, keepdims=True)
            at += size
        score_row = to_row(scores)
        exp_row = jnp.exp(score_row)
        exp_ref[...] = exp_row
        corrected = clicks_of(rank_ref, click_ref, alpha_ref, beta_ref)
        corr_ref[...] = corrected
        member = lists_of(list_ref, LISTS)
        lane = lax.broadcasted_iota(jnp.int32, (LISTS, 128), 1)
        total = jnp.zeros((LISTS, 128), F32)
        for k, row in enumerate((exp_row, corrected * score_row, corrected)):
            total = jnp.where(lane == k, jnp.sum(member * row, axis=1, keepdims=True), total)
        tot_ref[...] = total

    return vmem_call(
        kernel,
        [
            shaped((tok, width), F32),
            shaped((tok, 1), F32),
            shaped((cands, width), BF),
            shaped((cands, units), F32),
            shaped((1, cands), F32),
            shaped((1, cands), F32),
            shaped((LISTS, 128), F32),
        ],
        [rolled] + sums + head + out_w + lists_in,
        flops=4 * cands * width * units,
    )


def grad_stage(own, other, state, head, out_w, pool_ids, list_ids):
    normed, _, _, _, _, _ = state
    tok, width = normed.shape
    half = width // 2
    cands = list_ids.shape[1]

    def kernel(*refs):
        own_ref, other_ref, normed_ref, inv_ref, pooled_ref, act_ref, exp_ref, corr_ref = refs[:8]
        head_refs, out_refs = refs[8:11], refs[11:13]
        pool_ref, list_ref = refs[13:15]
        loss_ref, low_ref, high_ref, packed_ref = refs[15:]
        totals = own_ref[...] + other_ref[...]
        exp_total, cross_total, click_total = totals[:, 0:1], totals[:, 1:2], totals[:, 2:3]
        loss_ref[...] = jnp.sum(
            click_total * jnp.log(exp_total) - cross_total, axis=0, keepdims=True
        )
        member = lists_of(list_ref, LISTS)
        cand_row = (
            jnp.sum(member * (click_total / exp_total), axis=0, keepdims=True) * exp_ref[...]
            - corr_ref[...]
        )
        cand = to_column(cand_row)
        back = jnp.zeros((cands, width), F32)
        at = 0
        for head_ref, out_row in zip(head_refs, units_of(head_refs, *out_refs)):
            size = head_ref.shape[0]
            act = act_ref[:, at : at + size]
            hid = (cand * out_row * (1.0 - act * act)).astype(BF)
            back = back + jnp.dot(hid, head_ref[...], preferred_element_type=F32)
            at += size
        hot = pool_of(pool_ref, cands)
        back = back / jnp.sum(hot, axis=1, keepdims=True)
        swapped = lax.axis_index("dp") != 0
        parts = [
            jnp.where(swapped, back[:, half:], back[:, :half]),
            jnp.where(swapped, back[:, :half], back[:, half:]),
        ]
        grads = [
            lax.dot_general(
                hot,
                p,
                (((0,), (0,)), ((), ())),
                precision=lax.Precision.HIGHEST,
                preferred_element_type=F32,
            )
            for p in parts
        ]
        mean = sum(
            jnp.sum(g * normed_ref[:, h * half : (h + 1) * half], axis=1, keepdims=True)
            for h, g in enumerate(grads)
        ) * (1.0 / width)
        for h, ref in enumerate((low_ref, high_ref)):
            n = normed_ref[:, h * half : (h + 1) * half]
            ref[...] = (inv_ref[...] * (grads[h] - n * mean)).astype(BF)
        packed_ref[:, :width] = pooled_ref[...]
        top = cand.astype(BF).astype(F32)
        middle = (cand - top).astype(BF).astype(F32)
        bottom = cand - top - middle
        lane = lax.broadcasted_iota(jnp.int32, (cands, 128), 1)
        packed_ref[:, width:] = jnp.where(
            lane == 0, top, jnp.where(lane == 1, middle, jnp.where(lane == 2, bottom, 0.0))
        ).astype(BF)

    return vmem_call(
        kernel,
        [
            shaped((1, 1), F32),
            shaped((tok, half), BF),
            shaped((tok, half), BF),
            shaped((cands, width + 128), BF),
        ],
        [own, other] + list(state) + head + out_w + [pool_ids, list_ids],
        flops=4 * cands * width * sum(h.shape[0] for h in head),
    )


def head_stage(table, blocks, head, out_w):
    count = len(blocks)
    packed_width = blocks[0].shape[1]
    total = table.shape[0]
    units, width = head.shape
    each = sum(b.shape[0] for b in blocks) // total
    cands = each // 2

    def kernel(table_ref, *refs):
        block_refs = refs[:count]
        head_ref, out_ref, grad_ref, out_grad_ref, buffer = refs[count:]
        mine, plane = lax.axis_index("expert"), lax.axis_index("dp")
        j = 0
        for ref in block_refs:
            for piece in range(ref.shape[0] // each):
                at = table_ref[mine, j] * each
                for k in range(2):
                    place = pl.multiple_of(at + (plane ^ k) * cands, cands)
                    start = piece * each + k * cands
                    buffer[pl.ds(place, cands), :] = ref[start : start + cands, :]
                j += 1
        pooled = buffer[:, :width]
        act = jnp.tanh(dot_rows(pooled, head_ref[...]))
        tail = buffer[:, width:].astype(F32)
        cand = tail[:, 0:1] + tail[:, 1:2] + tail[:, 2:3]
        hid = (cand * out_ref[...] * (1.0 - act * act)).astype(BF)
        out_grad_ref[...] = jnp.sum(cand * act, axis=0, keepdims=True)
        grad_ref[...] = lax.dot_general(
            hid, pooled, (((0,), (0,)), ((), ())), preferred_element_type=F32
        )

    return vmem_call(
        kernel,
        [shaped((units, width), F32), shaped((1, units), F32)],
        [table] + blocks + [head, out_w],
        scratch=[pltpu.VMEM((total * each, packed_width), BF)],
        flops=4 * total * each * width * units,
        smem=1,
    )


def pick_half(head):
    rows = head.shape[0] // 2

    def kernel(head_ref, out_ref):
        first = lax.axis_index("expert") % 2 == 0
        out_ref[...] = jnp.where(first, head_ref[:rows, :], head_ref[rows:, :])

    return vmem_call(kernel, [shaped((rows, head.shape[1]), head.dtype)], [head])[0]


def after(value, *others):
    return lax.optimization_barrier((value,) + others)[0]


def dense_local(*args):
    return dense_step(*args)


def dense_step(
    tokens,
    route_ids,
    route_weights,
    up_weight,
    down_weight,
    head_weight,
    out_weight,
    pool_ids,
    list_ids,
    clicks,
    ranks,
    alpha_table,
    beta_table,
):
    n_exp = lax.axis_size("expert")
    ring = Ring(n_exp)
    last = ring.half
    tok, width = tokens.shape
    half = width // 2

    def across(x):
        return lax.ppermute(x, "dp", [(0, 1), (1, 0)])

    up_own, down_own = up_weight[0].T, down_weight[0].T
    up = [up_own, across(up_own)]
    rolled = pack_stage(tokens, route_ids.T, route_weights.T, n_exp)

    mine, theirs = [rolled], [ring.swap(rolled)]
    mine_swapped, theirs_swapped = [None], [None]
    for r in range(1, last + 1):
        mine.append(ring.send(mine[-1]))
        mine_swapped.append(ring.swap(mine[-1]))
        if r < last:
            theirs.append(ring.send(theirs[-1]))
            theirs_swapped.append(ring.swap(theirs[-1]))

    down = [down_own, across(down_own)]
    head_came = across(after(pick_half(head_weight), down[1]))
    head = [head_weight, head_came, ring.swap(head_came)]
    out_row = out_weight[None, :]
    out_w = [out_row, across(after(out_row, down[1]))]

    acts, slopes = [], []
    for r in range(last + 1):
        if r == 0:
            blocks, groups = [mine[0], theirs[0]], [1, 1]
        elif r < last:
            blocks = [mine[r], theirs[r], mine_swapped[r], theirs_swapped[r]]
            groups = [2, 2]
        else:
            blocks, groups = [mine[r], mine_swapped[r]], [1, 1]
        a, s = hidden_stage(blocks, groups, up, tok, n_exp)
        acts.append(a)
        slopes.append(s)

    sums = []
    for h in range(2):
        first = project(acts[last][1], down[h]).astype(BF)
        given = ring.swap(first)
        moving = project(acts[last][0], down[h], given).astype(BF)
        for r in reversed(range(1, last)):
            block = after(acts[r][0], first) if h else acts[r][0]
            given = ring.swap(project(block, down[h]).astype(BF))
            came = ring.send(moving)
            moving = project(acts[r][1], down[h], given, came).astype(BF)
        came = ring.send(moving)
        back = project(acts[0][1], down[h], came[:tok]).astype(BF)
        sums += [project(acts[0][0], down[h], came[tok:]), ring.swap(back)]

    lists_in = [pool_ids, list_ids, clicks, ranks, alpha_table[None, :], beta_table[None, :]]
    *state, totals = score_stage(rolled, sums, head, out_w, lists_in)
    list_loss, low, high, packed = grad_stage(
        totals, across(totals), state, head, out_w, pool_ids, list_ids
    )

    def gather_blocks(x):
        blocks = []
        for rounds in ring.gather(x):
            blocks += rounds
        return blocks

    grads = [None, None]
    grads[1] = gather_blocks(high)
    grads[0] = gather_blocks(low)
    flat = lambda lists: [x for part in lists for x in part]
    act_blocks, slope_blocks = flat(acts), flat(slopes)
    sent_down = across(outer_sum(act_blocks, grads[1], BF, half))
    split = 2 * (last - 1)
    early = back_stage([grads[0][:split], grads[1][:split]], slope_blocks[:split], down)
    late = back_stage([grads[0][split:], grads[1][split:]], slope_blocks[split:], down)
    pre_grads = list(early) + list(late)
    inputs = [mine[0], theirs[0]]
    for r in range(1, last):
        inputs += [mine[r], theirs[r], mine_swapped[r], theirs_swapped[r]]
    inputs += [mine[last], mine_swapped[last]]
    sent_up = across(outer_sum(pre_grads, inputs, BF, half, half, tok))
    down_local = outer_sum(act_blocks, grads[0], F32, half)
    up_local = outer_sum(pre_grads, inputs, F32, half, 0, tok)

    pair = jnp.concatenate([packed, across(packed)])
    grad_head, grad_out = head_stage(
        jnp.asarray(ring.table), gather_blocks(pair), head_weight, out_row
    )

    grad_down = (down_local + sent_down.astype(F32)).astype(BF).T[None]
    grad_up = (up_local + sent_up.astype(F32)).astype(BF).T[None]
    return (grad_up, grad_down, grad_head, grad_out[0], list_loss[0])


def solution(mesh):
    paired = mesh.shape["dp"] == 2 and mesh.shape["expert"] % 4 == 0
    return jax.shard_map(
        dense_local if paired else routed_local,
        mesh=mesh,
        in_specs=(
            P(("dp", "expert"), None),
            P(("dp", "expert"), None),
            P(("dp", "expert"), None),
            P("expert", "dp", None),
            P("expert", "dp", None),
            P("dp", None),
            P("dp"),
            P(("dp", "expert"), None),
            P(("dp", "expert"), None),
            P(("dp", "expert"), None),
            P(("dp", "expert"), None),
            P(),
            P(),
        ),
        out_specs=(
            P("expert", "dp", None),
            P("expert", "dp", None),
            P("dp", None),
            P("dp"),
            P("expert"),
        ),
        check_vma=False,
    )
```

```python
import jax
import jax.numpy as jnp
import numpy as np
from jax import lax
from jax.experimental import pallas as pl
from jax.experimental.pallas import tpu as pltpu
from jax.sharding import PartitionSpec as P

LISTS = 8
RANKS = 32
BF = jnp.bfloat16
F32 = jnp.float32


def ring_order(chips):
    cols = 1
    while cols * cols * 4 <= chips and chips % (cols * 2) == 0:
        cols *= 2
    rows = chips // cols
    if cols == 1:
        return list(range(chips))
    cycle = [(r, 0) for r in range(rows)]
    for turn, r in enumerate(reversed(range(rows))):
        across = list(range(1, cols))
        if turn % 2:
            across.reverse()
        cycle += [(r, c) for c in across]
    return [r * cols + c for r, c in cycle]


class Ring:
    def __init__(self, devices):
        self.chips = devices // 2
        self.half = self.chips // 2
        cycle = ring_order(self.chips)
        count = self.chips
        self.forward = []
        for p in range(count):
            self.forward.append((2 * cycle[p], 2 * cycle[(p + 1) % count]))
            self.forward.append((2 * cycle[p] + 1, 2 * cycle[(p - 1) % count] + 1))
        self.swap_pairs = [(d, d ^ 1) for d in range(devices)]
        position = {chip: p for p, chip in enumerate(cycle)}
        table = np.zeros((devices, devices), np.int32)
        for device in range(devices):
            pos, core = position[device // 2], device % 2
            sign = 1 if core else -1

            def at(step, which):
                return 2 * cycle[(pos + step) % count] + which

            order = [at(0, core), at(0, 1 - core)]
            for r in range(1, self.half):
                order += [at(sign * r, core), at(sign * r, 1 - core)]
                order += [at(-sign * r, 1 - core), at(-sign * r, core)]
            order += [at(self.half, core), at(self.half, 1 - core)]
            table[device] = order
        self.table = table

    def send(self, x):
        return lax.ppermute(x, "expert", self.forward)

    def swap(self, x):
        return lax.ppermute(x, "expert", self.swap_pairs)

    def gather(self, x):
        rows = x.shape[0]
        partner = self.swap(x)
        current = jnp.concatenate([x, partner], axis=0)
        rounds = [[x, partner]]
        for r in range(1, self.half + 1):
            outgoing = current[:rows] if r == self.half else current
            current = self.send(outgoing)
            rounds.append([current, self.swap(current)])
        return rounds


def silu_slope(pre_act):
    sigmoid = jax.nn.sigmoid(pre_act)
    return sigmoid * (1.0 + pre_act * (1.0 - sigmoid))


def routed_local(
    tokens,
    route_ids,
    route_weights,
    up_weight,
    down_weight,
    head_weight,
    out_weight,
    pool_ids,
    list_ids,
    clicks,
    ranks,
    alpha_table,
    beta_table,
):
    tok_count = tokens.shape[0]
    model_width = tokens.shape[1]
    top_count = route_ids.shape[1]
    owners = lax.axis_size("expert")
    capacity = 3 * tok_count * top_count // (2 * owners)
    slot_total = owners * capacity
    flat_ids = route_ids.reshape(-1)
    expert_hot = (flat_ids[:, None] == jnp.arange(owners, dtype=jnp.int32)[None, :]).astype(
        jnp.int32
    )
    running = jnp.cumsum(expert_hot, axis=0) - 1
    slot_index = jnp.sum(running * expert_hot, axis=1)
    target = flat_ids * capacity + slot_index
    token_index = jnp.arange(tok_count * top_count, dtype=jnp.int32) // top_count
    outgoing = (
        jnp.zeros((slot_total, model_width), jnp.bfloat16).at[target].set(tokens[token_index])
    )
    received = lax.all_to_all(
        outgoing.reshape(owners, capacity, model_width),
        "expert",
        split_axis=0,
        concat_axis=0,
        tiled=True,
    )
    inputs = received.reshape(slot_total, model_width)
    up_local = up_weight[0]
    down_local = down_weight[0]
    hidden_width = up_local.shape[1]
    columns = inputs
    pre_act = jnp.dot(
        columns,
        lax.all_gather(up_local, "dp", axis=0, tiled=True),
        preferred_element_type=jnp.float32,
    )
    activated = jax.nn.silu(pre_act).astype(jnp.bfloat16)
    expert_out = lax.dot_general(
        activated,
        lax.all_gather(down_local, "dp", axis=0, tiled=True),
        (((1,), (1,)), ((), ())),
        preferred_element_type=jnp.float32,
    ).astype(jnp.bfloat16)
    returned = lax.all_to_all(
        expert_out.reshape(owners, capacity, model_width),
        "expert",
        split_axis=0,
        concat_axis=0,
        tiled=True,
    ).reshape(slot_total, model_width)
    routed_rows = returned[target].reshape(tok_count, top_count, model_width)
    routed = jnp.sum(route_weights[:, :, None] * routed_rows.astype(jnp.float32), axis=1)
    mixed = tokens.astype(jnp.float32) + routed
    inv_rms = lax.rsqrt(jnp.mean(mixed * mixed, axis=1, keepdims=True) + 1e-06)
    normed = mixed * inv_rms
    cand_count = list_ids.shape[1]
    member = (pool_ids[0][:, None] == jnp.arange(cand_count, dtype=jnp.int32)[None, :]).astype(
        jnp.float32
    )
    token_counts = jnp.sum(member, axis=0)
    pooled_sum = lax.dot_general(
        member,
        normed,
        (((0,), (0,)), ((), ())),
        precision=lax.Precision.HIGHEST,
        preferred_element_type=jnp.float32,
    )
    pooled = (pooled_sum / token_counts[:, None]).astype(jnp.bfloat16)
    all_pooled = lax.all_gather(pooled, "dp", axis=0, tiled=True)
    head_act = jnp.tanh(
        lax.dot_general(
            all_pooled, head_weight, (((1,), (1,)), ((), ())), preferred_element_type=jnp.float32
        )
    )
    part_score = jnp.sum(head_act * out_weight[None, :], axis=1)
    rank_hot = (ranks[0][:, None] == jnp.arange(RANKS, dtype=jnp.int32)[None, :]).astype(
        jnp.float32
    )
    alpha_of = jnp.sum(rank_hot * alpha_table[None, :], axis=1)
    beta_of = jnp.sum(rank_hot * beta_table[None, :], axis=1)
    corrected = (clicks[0].astype(jnp.float32) - beta_of) / alpha_of
    list_hot = (list_ids[0][:, None] == jnp.arange(LISTS, dtype=jnp.int32)[None, :]).astype(
        jnp.float32
    )
    group_corrected, group_lists = (
        lax.all_gather(corrected, "dp", axis=0, tiled=True),
        lax.all_gather(list_hot, "dp", axis=0, tiled=True),
    )
    group_scores = lax.psum(part_score, "dp")
    exp_scores = jnp.exp(group_scores)
    exp_total = jnp.sum(exp_scores[:, None] * group_lists, axis=0)
    click_total = jnp.sum(group_corrected[:, None] * group_lists, axis=0)
    cross_total = jnp.sum((group_corrected * group_scores)[:, None] * group_lists, axis=0)
    list_loss = jnp.sum(click_total * jnp.log(exp_total) - cross_total).reshape(1)
    group_grad = (
        jnp.sum(group_lists * (click_total / exp_total)[None, :], axis=1) * exp_scores
        - group_corrected
    )
    hid_grad = (group_grad[:, None] * out_weight[None, :] * (1.0 - head_act * head_act)).astype(
        jnp.bfloat16
    )
    head_term = lax.dot_general(
        hid_grad, all_pooled, (((0,), (0,)), ((), ())), preferred_element_type=jnp.float32
    )
    out_term = jnp.sum(group_grad[:, None] * head_act, axis=0)
    grad_head, grad_out = (
        lax.psum(head_term.astype(jnp.bfloat16), "expert").astype(jnp.float32),
        lax.psum(out_term.astype(jnp.bfloat16), "expert").astype(jnp.float32),
    )
    pooled_grad = lax.psum_scatter(
        jnp.dot(hid_grad, head_weight, preferred_element_type=jnp.float32).astype(jnp.bfloat16),
        "dp",
        scatter_dimension=0,
        tiled=True,
    ).astype(jnp.float32)
    normed_grad = jnp.dot(
        member,
        pooled_grad / token_counts[:, None],
        precision=lax.Precision.HIGHEST,
        preferred_element_type=jnp.float32,
    )
    mixed_grad = inv_rms * (
        normed_grad - normed * jnp.mean(normed_grad * normed, axis=1, keepdims=True)
    )
    cotangent = (
        (route_weights[:, :, None] * mixed_grad[:, None, :])
        .astype(jnp.bfloat16)
        .reshape(tok_count * top_count, model_width)
    )
    outgoing_grad = jnp.zeros((slot_total, model_width), jnp.bfloat16).at[target].set(cotangent)
    slot_grad = lax.all_to_all(
        outgoing_grad.reshape(owners, capacity, model_width),
        "expert",
        split_axis=0,
        concat_axis=0,
        tiled=True,
    ).reshape(slot_total, model_width)
    columns = slot_grad
    act_grad = jnp.dot(
        columns,
        lax.all_gather(down_local, "dp", axis=0, tiled=True),
        preferred_element_type=jnp.float32,
    )
    pre_grad = (act_grad * silu_slope(pre_act)).astype(jnp.bfloat16)
    up_term = lax.dot_general(
        inputs, pre_grad, (((0,), (0,)), ((), ())), preferred_element_type=jnp.float32
    )
    down_term = lax.dot_general(
        slot_grad, activated, (((0,), (0,)), ((), ())), preferred_element_type=jnp.float32
    )
    summed = lax.psum_scatter(
        jnp.concatenate([up_term, down_term], axis=1).astype(jnp.bfloat16),
        "dp",
        scatter_dimension=0,
        tiled=True,
    ).astype(jnp.float32)
    grad_up = summed[:, :hidden_width].astype(jnp.bfloat16)[None]
    grad_down = summed[:, hidden_width:].astype(jnp.bfloat16)[None]
    return (grad_up, grad_down, grad_head, grad_out, list_loss)


SPARE_VMEM = 6 * 1024 * 1024
WIDE_GRANT = 63 * 1024 * 1024


def padded_bytes(x):
    lead = int(np.prod(x.shape[:-2])) if len(x.shape) > 2 else 1
    rows = -(-x.shape[-2] // 16) * 16 if len(x.shape) > 1 else 1
    return lead * rows * (-(-x.shape[-1] // 128) * 128) * x.dtype.itemsize


def vmem_call(kernel, outs, args, scratch=(), flops=0, smem=0, grant=None):
    held = sum(padded_bytes(a) for a in list(args)[smem:] + list(outs))
    held += sum(
        int(np.prod(b.shape)) * jnp.dtype(b.dtype).itemsize
        for b in scratch
        if b.memory_space == pltpu.VMEM
    )
    specs = [pl.BlockSpec(memory_space=pltpu.SMEM)] * smem + [
        pl.BlockSpec(memory_space=pltpu.HBM if grant else pltpu.VMEM)
    ] * (len(args) - smem)
    moved = sum(a.size * a.dtype.itemsize for a in args) + sum(
        o.size * o.dtype.itemsize for o in outs
    )
    return pl.pallas_call(
        kernel,
        out_shape=outs,
        in_specs=specs,
        out_specs=[pl.BlockSpec(memory_space=pltpu.VMEM)] * len(outs),
        scratch_shapes=list(scratch),
        cost_estimate=pl.CostEstimate(flops=flops, bytes_accessed=moved, transcendentals=0),
        compiler_params=pltpu.CompilerParams(vmem_limit_bytes=grant or held + SPARE_VMEM),
    )(*args)


def shaped(shape, dtype):
    return jax.ShapeDtypeStruct(shape, dtype)


def fill(buffer, refs, start=0, limit=None):
    at = 0
    for ref in refs:
        size = limit or ref.shape[0]
        buffer[pl.ds(at, size), :] = ref[:size, start : start + buffer.shape[1]]
        at += size


def dot_rows(a, b):
    return lax.dot_general(a, b, (((1,), (1,)), ((), ())), preferred_element_type=F32)


def pack_stage(tokens, ids, weights, owners):
    tok, width = tokens.shape
    half = width // 2
    per_row = width // tok
    top = ids.shape[0]
    extra = 2 * -(-owners // per_row)
    rows = tok + -(-extra // 8) * 8

    def kernel(tok_hbm, id_hbm, weight_hbm, out_ref, tok_ref, id_ref, weight_ref, sems):
        pulls = [
            pltpu.make_async_copy(source, target, sems.at[k])
            for k, (source, target) in enumerate(
                ((id_hbm, id_ref), (weight_hbm, weight_ref), (tok_hbm, tok_ref))
            )
        ]
        for pull in pulls:
            pull.start()
        for pull in pulls:
            pull.wait()
        swapped = lax.axis_index("dp") != 0
        out_ref[:tok, :half] = jnp.where(swapped, tok_ref[:, half:], tok_ref[:, :half])
        out_ref[:tok, half:] = jnp.where(swapped, tok_ref[:, :half], tok_ref[:, half:])
        lanes = [[] for _ in range(extra)]
        for owner in range(owners):
            value = jnp.zeros((1, tok), F32)
            for k in range(top):
                hit = id_ref[k : k + 1, :] == owner
                value = value + jnp.where(hit, weight_ref[k : k + 1, :], 0.0)
            high = value.astype(BF).astype(F32)
            row = owner // per_row
            lanes[2 * row].append(high)
            lanes[2 * row + 1].append(value - high)
        filled = []
        for row in lanes:
            row += [jnp.zeros((1, tok), F32)] * (per_row - len(row))
            filled.append(jnp.concatenate(row, axis=1))
        filled.append(jnp.zeros((rows - tok - extra, width), F32))
        out_ref[tok:, :] = jnp.concatenate(filled, axis=0).astype(BF)

    return vmem_call(
        kernel,
        [shaped((rows, width), BF)],
        [tokens, ids, weights],
        scratch=[
            pltpu.VMEM(tokens.shape, tokens.dtype),
            pltpu.VMEM(ids.shape, ids.dtype),
            pltpu.VMEM(weights.shape, weights.dtype),
            pltpu.SemaphoreType.DMA((3,)),
        ],
        grant=WIDE_GRANT,
    )[0]


def weight_column(ref, tok, owners, mine):
    width = ref.shape[1]
    per_row = width // tok
    extra = ref[tok:, :].astype(F32)
    row = jnp.zeros((1, tok), F32)
    for owner in range(owners):
        at, lane = 2 * (owner // per_row), (owner % per_row) * tok
        both = extra[at : at + 1, lane : lane + tok] + extra[at + 1 : at + 2, lane : lane + tok]
        row = row + jnp.where(mine == owner, both, 0.0)
    diagonal = lax.broadcasted_iota(jnp.int32, (tok, tok), 0) == lax.broadcasted_iota(
        jnp.int32, (tok, tok), 1
    )
    return jnp.sum(jnp.where(diagonal, row, 0.0), axis=1, keepdims=True)


def hidden_stage(blocks, groups, up, tok, owners):
    count = len(blocks)
    width = blocks[0].shape[1]
    hidden = up[0].shape[0]
    half = width // 2
    rows = count * tok
    sizes = [g * tok for g in groups]

    def kernel(*refs):
        xs, (up0, up1) = refs[:count], refs[count : count + 2]
        act_refs = refs[count + 2 : count + 2 + len(groups)]
        slope_refs = refs[count + 2 + len(groups) : count + 2 + 2 * len(groups)]
        buffer = refs[-1]
        fill(buffer, xs, limit=tok)
        at, j = 0, 0
        for index, g in enumerate(groups):
            x = buffer[pl.ds(at, g * tok), :]
            pre = dot_rows(x[:, :half], up0[...]) + dot_rows(x[:, half:], up1[...])
            sig = 1.0 / (1.0 + jnp.exp(-pre))
            for b in range(g):
                w = weight_column(xs[j], tok, owners, lax.axis_index("expert"))
                p = pre[b * tok : (b + 1) * tok]
                s = sig[b * tok : (b + 1) * tok]
                ws = w * s
                act_refs[index][pl.ds(b * tok, tok), :] = (ws * p).astype(BF)
                slope_refs[index][pl.ds(b * tok, tok), :] = (ws * (1.0 + p * (1.0 - s))).astype(BF)
                j += 1
            at += g * tok

    outs = [shaped((size, hidden), BF) for size in sizes]
    result = vmem_call(
        kernel,
        outs + outs,
        list(blocks) + [up[0], up[1]],
        scratch=[pltpu.VMEM((rows, width), BF)],
        flops=2 * rows * width * hidden,
    )
    return result[: len(groups)], result[len(groups) :]


def project(act, down, *adds):
    total = jnp.dot(act, down, preferred_element_type=F32)
    for add in adds:
        missing = act.shape[0] - add.shape[0]
        total = total + jnp.pad(add, ((missing, 0), (0, 0))).astype(F32)
    return total


def outer_sum(lefts, rights, out_dtype, rw, start=0, limit=None, base=None):
    nl, nr = len(lefts), len(rights)
    rows = sum(a.shape[0] for a in lefts)
    lw = lefts[0].shape[1]

    def kernel(*refs):
        out_ref, left, right = refs[-3:]
        fill(left, refs[:nl])
        fill(right, refs[nl : nl + nr], start, limit)
        at = 0
        while at < lw:
            size = min(256, lw - at)
            value = lax.dot_general(
                left[:, at : at + size],
                right[...],
                (((0,), (0,)), ((), ())),
                preferred_element_type=F32,
            )
            if base is not None:
                value = value + refs[nl + nr][at : at + size, :]
            out_ref[at : at + size, :] = value.astype(out_dtype)
            at += size

    return vmem_call(
        kernel,
        [shaped((lw, rw), out_dtype)],
        list(lefts) + list(rights) + ([] if base is None else [base]),
        scratch=[pltpu.VMEM((rows, lw), BF), pltpu.VMEM((rows, rw), BF)],
        flops=2 * rows * lw * rw,
    )[0]


def back_stage(grads, slopes, down):
    count = len(slopes)
    hidden = down[0].shape[0]

    def kernel(*refs):
        g0, g1 = refs[:count], refs[count : 2 * count]
        slope = refs[2 * count : 3 * count]
        down0, down1 = refs[3 * count : 3 * count + 2]
        outs = refs[3 * count + 2 :]
        for b in range(count):
            value = dot_rows(g0[b][...], down0[...]) + dot_rows(g1[b][...], down1[...])
            outs[b][...] = (value * slope[b][...].astype(F32)).astype(BF)

    rows = sum(s.shape[0] for s in slopes)
    return vmem_call(
        kernel,
        [shaped(s.shape, BF) for s in slopes],
        list(grads[0]) + list(grads[1]) + list(slopes) + list(down),
        flops=4 * rows * down[0].shape[1] * hidden,
    )


def eye(size):
    return lax.broadcasted_iota(jnp.int32, (size, size), 0) == lax.broadcasted_iota(
        jnp.int32, (size, size), 1
    )


def to_column(row):
    return jnp.sum(jnp.where(eye(row.shape[1]), row, 0.0), axis=1, keepdims=True)


def to_row(column):
    return jnp.sum(jnp.where(eye(column.shape[0]), column, 0.0), axis=0, keepdims=True)


def clicks_of(rank_ref, click_ref, alpha_ref, beta_ref):
    rank_row = rank_ref[...]
    hot = (
        lax.broadcasted_iota(jnp.int32, (alpha_ref.shape[1], rank_row.shape[1]), 0) == rank_row
    ).astype(F32)
    alpha = jnp.sum(hot * to_column(alpha_ref[...]), axis=0, keepdims=True)
    beta = jnp.sum(hot * to_column(beta_ref[...]), axis=0, keepdims=True)
    return (click_ref[...].astype(F32) - beta) / alpha


def lists_of(list_ref, count):
    row = list_ref[...]
    return (lax.broadcasted_iota(jnp.int32, (count, row.shape[1]), 0) == row).astype(F32)


def pool_of(pool_ref, cands):
    row = pool_ref[...]
    return (lax.broadcasted_iota(jnp.int32, (cands, row.shape[1]), 0) == row).astype(F32)


def units_of(head_refs, own_ref, other_ref):
    part = head_refs[1].shape[0]
    first = lax.axis_index("expert") % 2 == 0
    low, high = other_ref[:, :part], other_ref[:, part:]
    return [own_ref[...], jnp.where(first, low, high), jnp.where(first, high, low)]


def score_stage(rolled, sums, head, out_w, lists_in):
    width = rolled.shape[1]
    tok = sums[0].shape[0]
    half = width // 2
    cands = lists_in[1].shape[1]
    units = sum(h.shape[0] for h in head)
    per_half = len(sums) // 2

    def kernel(*refs):
        rolled_ref = refs[0]
        sum_refs = refs[1 : 1 + 2 * per_half]
        rest = refs[1 + 2 * per_half :]
        head_refs, out_refs = rest[:3], rest[3:5]
        pool_ref, list_ref, click_ref, rank_ref, alpha_ref, beta_ref = rest[5:11]
        normed_ref, inv_ref, pooled_ref, act_ref, exp_ref, corr_ref, tot_ref = rest[11:]
        mixed = []
        for h in range(2):
            value = rolled_ref[:tok, h * half : (h + 1) * half].astype(F32)
            for ref in sum_refs[h * per_half : (h + 1) * per_half]:
                value = value + ref[...].astype(F32)
            mixed.append(value)
        square = sum(jnp.sum(m * m, axis=1, keepdims=True) for m in mixed)
        inv = lax.rsqrt(square * (1.0 / width) + 1e-06)
        inv_ref[...] = inv
        hot = pool_of(pool_ref, cands)
        counts = jnp.sum(hot, axis=1, keepdims=True)
        pooled = []
        for h in range(2):
            normed = mixed[h] * inv
            normed_ref[:, h * half : (h + 1) * half] = normed
            pooled.append(
                jnp.dot(
                    hot, normed, precision=lax.Precision.HIGHEST, preferred_element_type=F32
                )
                / counts
            )
        swapped = lax.axis_index("dp") != 0
        pooled_ref[:, :half] = jnp.where(swapped, pooled[1], pooled[0]).astype(BF)
        pooled_ref[:, half:] = jnp.where(swapped, pooled[0], pooled[1]).astype(BF)
        both = pooled_ref[...]
        scores = jnp.zeros((cands, 1), F32)
        at = 0
        for head_ref, out_row in zip(head_refs, units_of(head_refs, *out_refs)):
            size = head_ref.shape[0]
            act = jnp.tanh(dot_rows(both, head_ref[...]))
            act_ref[:, at : at + size] = act
            scores = scores + jnp.sum(act * out_row, axis=1, keepdims=True)
            at += size
        score_row = to_row(scores)
        exp_row = jnp.exp(score_row)
        exp_ref[...] = exp_row
        corrected = clicks_of(rank_ref, click_ref, alpha_ref, beta_ref)
        corr_ref[...] = corrected
        member = lists_of(list_ref, LISTS)
        lane = lax.broadcasted_iota(jnp.int32, (LISTS, 128), 1)
        total = jnp.zeros((LISTS, 128), F32)
        for k, row in enumerate((exp_row, corrected * score_row, corrected)):
            total = jnp.where(lane == k, jnp.sum(member * row, axis=1, keepdims=True), total)
        tot_ref[...] = total

    return vmem_call(
        kernel,
        [
            shaped((tok, width), F32),
            shaped((tok, 1), F32),
            shaped((cands, width), BF),
            shaped((cands, units), F32),
            shaped((1, cands), F32),
            shaped((1, cands), F32),
            shaped((LISTS, 128), F32),
        ],
        [rolled] + sums + head + out_w + lists_in,
        flops=4 * cands * width * units,
    )


def slope_stage(normed, inv, head_act, head, out_w, pool_ids, cands):
    tok, width = normed.shape
    half = width // 2

    def kernel(normed_ref, inv_ref, act_ref, *refs):
        head_refs, out_refs, pool_ref, slope_ref = refs[:3], refs[3:5], refs[5], refs[6]
        back = jnp.zeros((cands, width), F32)
        at = 0
        for head_ref, out_row in zip(head_refs, units_of(head_refs, *out_refs)):
            size = head_ref.shape[0]
            act = act_ref[:, at : at + size]
            hid = (out_row * (1.0 - act * act)).astype(BF)
            back = back + jnp.dot(hid, head_ref[...], preferred_element_type=F32)
            at += size
        hot = pool_of(pool_ref, cands)
        back = back / jnp.sum(hot, axis=1, keepdims=True)
        swapped = lax.axis_index("dp") != 0
        parts = [
            jnp.where(swapped, back[:, half:], back[:, :half]),
            jnp.where(swapped, back[:, :half], back[:, half:]),
        ]
        grads = [
            lax.dot_general(
                hot,
                p,
                (((0,), (0,)), ((), ())),
                precision=lax.Precision.HIGHEST,
                preferred_element_type=F32,
            )
            for p in parts
        ]
        mean = sum(
            jnp.sum(g * normed_ref[:, h * half : (h + 1) * half], axis=1, keepdims=True)
            for h, g in enumerate(grads)
        ) * (1.0 / width)
        for h in range(2):
            at = slice(h * half, (h + 1) * half)
            slope_ref[:, at] = inv_ref[...] * (grads[h] - normed_ref[:, at] * mean)

    return vmem_call(
        kernel,
        [shaped((tok, width), F32)],
        [normed, inv, head_act] + head + out_w + [pool_ids],
        flops=2 * cands * width * sum(h.shape[0] for h in head),
    )[0]


def grad_stage(own, other, slope, pooled, exp_row, corrected, pool_ids, list_ids):
    tok, width = slope.shape
    half = width // 2
    cands = list_ids.shape[1]

    def kernel(*refs):
        own_ref, other_ref, slope_ref, pooled_ref, exp_ref, corr_ref, pool_ref, list_ref = refs[:8]
        loss_ref, low_ref, high_ref, packed_ref = refs[8:]
        totals = own_ref[...] + other_ref[...]
        exp_total, cross_total, click_total = totals[:, 0:1], totals[:, 1:2], totals[:, 2:3]
        loss_ref[...] = jnp.sum(
            click_total * jnp.log(exp_total) - cross_total, axis=0, keepdims=True
        )
        member = lists_of(list_ref, LISTS)
        cand_row = (
            jnp.sum(member * (click_total / exp_total), axis=0, keepdims=True) * exp_ref[...]
            - corr_ref[...]
        )
        cand = to_column(cand_row)
        hot = pool_of(pool_ref, cands)
        of_token = to_column(jnp.sum(hot * cand, axis=0, keepdims=True))
        low_ref[...] = (of_token * slope_ref[:, :half]).astype(BF)
        high_ref[...] = (of_token * slope_ref[:, half:]).astype(BF)
        packed_ref[:, :width] = pooled_ref[...]
        top = cand.astype(BF).astype(F32)
        middle = (cand - top).astype(BF).astype(F32)
        bottom = cand - top - middle
        lane = lax.broadcasted_iota(jnp.int32, (cands, 128), 1)
        packed_ref[:, width:] = jnp.where(
            lane == 0, top, jnp.where(lane == 1, middle, jnp.where(lane == 2, bottom, 0.0))
        ).astype(BF)

    return vmem_call(
        kernel,
        [
            shaped((1, 1), F32),
            shaped((tok, half), BF),
            shaped((tok, half), BF),
            shaped((cands, width + 128), BF),
        ],
        [own, other, slope, pooled, exp_row, corrected, pool_ids, list_ids],
    )


def head_stage(table, blocks, head, out_w):
    count = len(blocks)
    packed_width = blocks[0].shape[1]
    total = table.shape[0]
    units, width = head.shape
    each = sum(b.shape[0] for b in blocks) // total
    cands = each // 2

    def kernel(table_ref, *refs):
        block_refs = refs[:count]
        head_ref, out_ref, grad_ref, out_grad_ref, buffer = refs[count:]
        mine, plane = lax.axis_index("expert"), lax.axis_index("dp")
        j = 0
        for ref in block_refs:
            for piece in range(ref.shape[0] // each):
                at = table_ref[mine, j] * each
                for k in range(2):
                    place = pl.multiple_of(at + (plane ^ k) * cands, cands)
                    start = piece * each + k * cands
                    buffer[pl.ds(place, cands), :] = ref[start : start + cands, :]
                j += 1
        pooled = buffer[:, :width]
        act = jnp.tanh(dot_rows(pooled, head_ref[...]))
        tail = buffer[:, width:].astype(F32)
        cand = tail[:, 0:1] + tail[:, 1:2] + tail[:, 2:3]
        hid = (cand * out_ref[...] * (1.0 - act * act)).astype(BF)
        out_grad_ref[...] = jnp.sum(cand * act, axis=0, keepdims=True)
        grad_ref[...] = lax.dot_general(
            hid, pooled, (((0,), (0,)), ((), ())), preferred_element_type=F32
        )

    return vmem_call(
        kernel,
        [shaped((units, width), F32), shaped((1, units), F32)],
        [table] + blocks + [head, out_w],
        scratch=[pltpu.VMEM((total * each, packed_width), BF)],
        flops=4 * total * each * width * units,
        smem=1,
    )


def pick_half(head):
    rows = head.shape[0] // 2

    def kernel(head_ref, out_ref):
        first = lax.axis_index("expert") % 2 == 0
        out_ref[...] = jnp.where(first, head_ref[:rows, :], head_ref[rows:, :])

    return vmem_call(kernel, [shaped((rows, head.shape[1]), head.dtype)], [head])[0]


def after(value, *others):
    return lax.optimization_barrier((value,) + others)[0]


def dense_local(*args):
    return dense_step(*args)


def dense_step(
    tokens,
    route_ids,
    route_weights,
    up_weight,
    down_weight,
    head_weight,
    out_weight,
    pool_ids,
    list_ids,
    clicks,
    ranks,
    alpha_table,
    beta_table,
):
    n_exp = lax.axis_size("expert")
    ring = Ring(n_exp)
    last = ring.half
    tok, width = tokens.shape
    half = width // 2
    cands = list_ids.shape[1]

    def across(x):
        return lax.ppermute(x, "dp", [(0, 1), (1, 0)])

    up_own, down_own = up_weight[0].T, down_weight[0].T
    up = [up_own, across(up_own)]
    rolled = pack_stage(tokens, route_ids.T, route_weights.T, n_exp)

    mine, theirs = [rolled], [ring.swap(rolled)]
    mine_swapped, theirs_swapped = [None], [None]
    for r in range(1, last + 1):
        mine.append(ring.send(mine[-1]))
        mine_swapped.append(ring.swap(mine[-1]))
        if r < last:
            theirs.append(ring.send(theirs[-1]))
            theirs_swapped.append(ring.swap(theirs[-1]))

    down = [down_own, across(down_own)]
    head_came = across(pick_half(head_weight))
    head = [head_weight, head_came, ring.swap(head_came)]
    out_row = out_weight[None, :]
    out_w = [out_row, across(out_row)]

    acts, slopes = [], []
    for r in range(last + 1):
        if r == 0:
            blocks, groups = [mine[0], theirs[0]], [1, 1]
        elif r < last:
            blocks = [mine[r], theirs[r], mine_swapped[r], theirs_swapped[r]]
            groups = [2, 2]
        else:
            blocks, groups = [mine[r], mine_swapped[r]], [1, 1]
        a, s = hidden_stage(blocks, groups, up, tok, n_exp)
        acts.append(a)
        slopes.append(s)

    sums = []
    for h in range(2):
        first = project(acts[last][1], down[h]).astype(BF)
        given = ring.swap(first)
        moving = project(acts[last][0], down[h], given).astype(BF)
        for r in reversed(range(1, last)):
            block = after(acts[r][0], moving) if h else acts[r][0]
            given = ring.swap(project(block, down[h]).astype(BF))
            came = ring.send(moving)
            moving = project(acts[r][1], down[h], given, came).astype(BF)
        came = ring.send(moving)
        back = project(acts[0][1], down[h], came[:tok]).astype(BF)
        sums += [project(acts[0][0], down[h], came[tok:]), ring.swap(back)]

    lists_in = [pool_ids, list_ids, clicks, ranks, alpha_table[None, :], beta_table[None, :]]
    normed, inv, pooled, head_act, exp_row, corrected, totals = score_stage(
        rolled, sums, head, out_w, lists_in
    )
    slope = slope_stage(normed, inv, head_act, head, out_w, pool_ids, cands)
    list_loss, low, high, packed = grad_stage(
        totals, across(totals), slope, pooled, exp_row, corrected, pool_ids, list_ids
    )

    def gather_blocks(x):
        blocks = []
        for rounds in ring.gather(x):
            blocks += rounds
        return blocks

    grads = [None, None]
    grads[1] = gather_blocks(high)
    grads[0] = gather_blocks(low)
    flat = lambda lists: [x for part in lists for x in part]
    act_blocks, slope_blocks = flat(acts), flat(slopes)
    partial = outer_sum(act_blocks[:-3], grads[1][:-3], F32, half)
    partial = outer_sum(act_blocks[-3:], grads[1][-3:], BF, half, base=partial)
    sent_down = across(partial)
    split = 2 * (last - 1)
    early = back_stage([grads[0][:split], grads[1][:split]], slope_blocks[:split], down)
    late = back_stage([grads[0][split:], grads[1][split:]], slope_blocks[split:], down)
    pre_grads = list(early) + list(late)
    inputs = [mine[0], theirs[0]]
    for r in range(1, last):
        inputs += [mine[r], theirs[r], mine_swapped[r], theirs_swapped[r]]
    inputs += [mine[last], mine_swapped[last]]
    sent_up = across(outer_sum(pre_grads, inputs, BF, half, half, tok))
    down_local = outer_sum(act_blocks, grads[0], BF, half)
    up_local = outer_sum(pre_grads, inputs, BF, half, 0, tok)

    grad_down = (down_local.astype(F32) + sent_down.astype(F32)).astype(BF).T[None]
    pair = jnp.concatenate([packed, across(packed)])
    blocks = gather_blocks(pair)
    blocks[0], grad_down = lax.optimization_barrier((blocks[0], grad_down))
    grad_head, grad_out = head_stage(jnp.asarray(ring.table), blocks, head_weight, out_row)

    grad_up = (up_local.astype(F32) + sent_up.astype(F32)).astype(BF).T[None]
    return (grad_up, grad_down, grad_head, grad_out[0], list_loss[0])


def solution(mesh):
    paired = mesh.shape["dp"] == 2 and mesh.shape["expert"] % 4 == 0
    return jax.shard_map(
        dense_local if paired else routed_local,
        mesh=mesh,
        in_specs=(
            P(("dp", "expert"), None),
            P(("dp", "expert"), None),
            P(("dp", "expert"), None),
            P("expert", "dp", None),
            P("expert", "dp", None),
            P("dp", None),
            P("dp"),
            P(("dp", "expert"), None),
            P(("dp", "expert"), None),
            P(("dp", "expert"), None),
            P(("dp", "expert"), None),
            P(),
            P(),
        ),
        out_specs=(
            P("expert", "dp", None),
            P("expert", "dp", None),
            P("dp", None),
            P("dp"),
            P("expert"),
        ),
        check_vma=False,
    )
```

```python
import jax
import jax.numpy as jnp
import numpy as np
from jax import lax
from jax.experimental import pallas as pl
from jax.experimental.pallas import tpu as pltpu
from jax.sharding import PartitionSpec as P

EXPERT = "expert"
DP = "dp"
LISTS = 8
RANKS = 32
BF = jnp.bfloat16
F32 = jnp.float32


def ring_order(chips):
    cols = 1
    while cols * cols * 4 <= chips and chips % (cols * 2) == 0:
        cols *= 2
    rows = chips // cols
    if cols == 1:
        return list(range(chips))
    cycle = [(r, 0) for r in range(rows)]
    for turn, r in enumerate(reversed(range(rows))):
        across = list(range(1, cols))
        if turn % 2:
            across.reverse()
        cycle += [(r, c) for c in across]
    return [r * cols + c for r, c in cycle]


class Ring:
    def __init__(self, devices):
        self.chips = devices // 2
        self.half = self.chips // 2
        cycle = ring_order(self.chips)
        count = self.chips
        self.forward = []
        for p in range(count):
            self.forward.append((2 * cycle[p], 2 * cycle[(p + 1) % count]))
            self.forward.append((2 * cycle[p] + 1, 2 * cycle[(p - 1) % count] + 1))
        self.swap_pairs = [(d, d ^ 1) for d in range(devices)]
        position = {chip: p for p, chip in enumerate(cycle)}
        table = np.zeros((devices, devices), np.int32)
        for device in range(devices):
            pos, core = position[device // 2], device % 2
            sign = 1 if core else -1

            def at(step, which):
                return 2 * cycle[(pos + step) % count] + which

            order = [at(0, core), at(0, 1 - core)]
            for r in range(1, self.half):
                order += [at(sign * r, core), at(sign * r, 1 - core)]
                order += [at(-sign * r, 1 - core), at(-sign * r, core)]
            order += [at(self.half, core), at(self.half, 1 - core)]
            table[device] = order
        self.table = table

    def send(self, x):
        return lax.ppermute(x, EXPERT, self.forward)

    def swap(self, x):
        return lax.ppermute(x, EXPERT, self.swap_pairs)

    def gather(self, x):
        rows = x.shape[0]
        partner = self.swap(x)
        current = jnp.concatenate([x, partner], axis=0)
        rounds = [[x, partner]]
        for r in range(1, self.half + 1):
            outgoing = current[:rows] if r == self.half else current
            current = self.send(outgoing)
            rounds.append([current, self.swap(current)])
        return rounds


def silu_slope(pre_act):
    sigmoid = jax.nn.sigmoid(pre_act)
    return sigmoid * (1.0 + pre_act * (1.0 - sigmoid))


def routed_local(
    tokens,
    route_ids,
    route_weights,
    up_weight,
    down_weight,
    head_weight,
    out_weight,
    pool_ids,
    list_ids,
    clicks,
    ranks,
    alpha_table,
    beta_table,
):
    tok_count = tokens.shape[0]
    model_width = tokens.shape[1]
    top_count = route_ids.shape[1]
    owners = lax.axis_size(EXPERT)
    capacity = 3 * tok_count * top_count // (2 * owners)
    slot_total = owners * capacity
    flat_ids = route_ids.reshape(-1)
    expert_hot = (flat_ids[:, None] == jnp.arange(owners, dtype=jnp.int32)[None, :]).astype(
        jnp.int32
    )
    running = jnp.cumsum(expert_hot, axis=0) - 1
    slot_index = jnp.sum(running * expert_hot, axis=1)
    target = flat_ids * capacity + slot_index
    token_index = jnp.arange(tok_count * top_count, dtype=jnp.int32) // top_count
    outgoing = (
        jnp.zeros((slot_total, model_width), jnp.bfloat16).at[target].set(tokens[token_index])
    )
    received = lax.all_to_all(
        outgoing.reshape(owners, capacity, model_width),
        EXPERT,
        split_axis=0,
        concat_axis=0,
        tiled=True,
    )
    inputs = received.reshape(slot_total, model_width)
    up_local = up_weight[0]
    down_local = down_weight[0]
    hidden_width = up_local.shape[1]
    columns = inputs
    pre_act = jnp.dot(
        columns,
        lax.all_gather(up_local, DP, axis=0, tiled=True),
        preferred_element_type=jnp.float32,
    )
    activated = jax.nn.silu(pre_act).astype(jnp.bfloat16)
    expert_out = lax.dot_general(
        activated,
        lax.all_gather(down_local, DP, axis=0, tiled=True),
        (((1,), (1,)), ((), ())),
        preferred_element_type=jnp.float32,
    ).astype(jnp.bfloat16)
    returned = lax.all_to_all(
        expert_out.reshape(owners, capacity, model_width),
        EXPERT,
        split_axis=0,
        concat_axis=0,
        tiled=True,
    ).reshape(slot_total, model_width)
    routed_rows = returned[target].reshape(tok_count, top_count, model_width)
    routed = jnp.sum(route_weights[:, :, None] * routed_rows.astype(jnp.float32), axis=1)
    mixed = tokens.astype(jnp.float32) + routed
    inv_rms = lax.rsqrt(jnp.mean(mixed * mixed, axis=1, keepdims=True) + 1e-06)
    normed = mixed * inv_rms
    cand_count = list_ids.shape[1]
    member = (pool_ids[0][:, None] == jnp.arange(cand_count, dtype=jnp.int32)[None, :]).astype(
        jnp.float32
    )
    token_counts = jnp.sum(member, axis=0)
    pooled_sum = lax.dot_general(
        member,
        normed,
        (((0,), (0,)), ((), ())),
        precision=lax.Precision.HIGHEST,
        preferred_element_type=jnp.float32,
    )
    pooled = (pooled_sum / token_counts[:, None]).astype(jnp.bfloat16)
    all_pooled = lax.all_gather(pooled, DP, axis=0, tiled=True)
    head_act = jnp.tanh(
        lax.dot_general(
            all_pooled, head_weight, (((1,), (1,)), ((), ())), preferred_element_type=jnp.float32
        )
    )
    part_score = jnp.sum(head_act * out_weight[None, :], axis=1)
    rank_hot = (ranks[0][:, None] == jnp.arange(RANKS, dtype=jnp.int32)[None, :]).astype(
        jnp.float32
    )
    alpha_of = jnp.sum(rank_hot * alpha_table[None, :], axis=1)
    beta_of = jnp.sum(rank_hot * beta_table[None, :], axis=1)
    corrected = (clicks[0].astype(jnp.float32) - beta_of) / alpha_of
    list_hot = (list_ids[0][:, None] == jnp.arange(LISTS, dtype=jnp.int32)[None, :]).astype(
        jnp.float32
    )
    group_corrected, group_lists = (
        lax.all_gather(corrected, DP, axis=0, tiled=True),
        lax.all_gather(list_hot, DP, axis=0, tiled=True),
    )
    group_scores = lax.psum(part_score, DP)
    exp_scores = jnp.exp(group_scores)
    exp_total = jnp.sum(exp_scores[:, None] * group_lists, axis=0)
    click_total = jnp.sum(group_corrected[:, None] * group_lists, axis=0)
    cross_total = jnp.sum((group_corrected * group_scores)[:, None] * group_lists, axis=0)
    list_loss = jnp.sum(click_total * jnp.log(exp_total) - cross_total).reshape(1)
    group_grad = (
        jnp.sum(group_lists * (click_total / exp_total)[None, :], axis=1) * exp_scores
        - group_corrected
    )
    hid_grad = (group_grad[:, None] * out_weight[None, :] * (1.0 - head_act * head_act)).astype(
        jnp.bfloat16
    )
    head_term = lax.dot_general(
        hid_grad, all_pooled, (((0,), (0,)), ((), ())), preferred_element_type=jnp.float32
    )
    out_term = jnp.sum(group_grad[:, None] * head_act, axis=0)
    grad_head, grad_out = (
        lax.psum(head_term.astype(jnp.bfloat16), EXPERT).astype(jnp.float32),
        lax.psum(out_term.astype(jnp.bfloat16), EXPERT).astype(jnp.float32),
    )
    pooled_grad = lax.psum_scatter(
        jnp.dot(hid_grad, head_weight, preferred_element_type=jnp.float32).astype(jnp.bfloat16),
        DP,
        scatter_dimension=0,
        tiled=True,
    ).astype(jnp.float32)
    normed_grad = jnp.dot(
        member,
        pooled_grad / token_counts[:, None],
        precision=lax.Precision.HIGHEST,
        preferred_element_type=jnp.float32,
    )
    mixed_grad = inv_rms * (
        normed_grad - normed * jnp.mean(normed_grad * normed, axis=1, keepdims=True)
    )
    cotangent = (
        (route_weights[:, :, None] * mixed_grad[:, None, :])
        .astype(jnp.bfloat16)
        .reshape(tok_count * top_count, model_width)
    )
    outgoing_grad = jnp.zeros((slot_total, model_width), jnp.bfloat16).at[target].set(cotangent)
    slot_grad = lax.all_to_all(
        outgoing_grad.reshape(owners, capacity, model_width),
        EXPERT,
        split_axis=0,
        concat_axis=0,
        tiled=True,
    ).reshape(slot_total, model_width)
    columns = slot_grad
    act_grad = jnp.dot(
        columns,
        lax.all_gather(down_local, DP, axis=0, tiled=True),
        preferred_element_type=jnp.float32,
    )
    pre_grad = (act_grad * silu_slope(pre_act)).astype(jnp.bfloat16)
    up_term = lax.dot_general(
        inputs, pre_grad, (((0,), (0,)), ((), ())), preferred_element_type=jnp.float32
    )
    down_term = lax.dot_general(
        slot_grad, activated, (((0,), (0,)), ((), ())), preferred_element_type=jnp.float32
    )
    summed = lax.psum_scatter(
        jnp.concatenate([up_term, down_term], axis=1).astype(jnp.bfloat16),
        DP,
        scatter_dimension=0,
        tiled=True,
    ).astype(jnp.float32)
    grad_up = summed[:, :hidden_width].astype(jnp.bfloat16)[None]
    grad_down = summed[:, hidden_width:].astype(jnp.bfloat16)[None]
    return (grad_up, grad_down, grad_head, grad_out, list_loss)


SPARE_VMEM = 6 * 1024 * 1024
WIDE_GRANT = 63 * 1024 * 1024


def padded_bytes(x):
    lead = int(np.prod(x.shape[:-2])) if len(x.shape) > 2 else 1
    rows = -(-x.shape[-2] // 16) * 16 if len(x.shape) > 1 else 1
    return lead * rows * (-(-x.shape[-1] // 128) * 128) * x.dtype.itemsize


def vmem_call(kernel, outs, args, scratch=(), flops=0, smem=0, grant=None):
    held = sum(padded_bytes(a) for a in list(args)[smem:] + list(outs))
    held += sum(
        int(np.prod(b.shape)) * jnp.dtype(b.dtype).itemsize
        for b in scratch
        if b.memory_space == pltpu.VMEM
    )
    specs = [pl.BlockSpec(memory_space=pltpu.SMEM)] * smem + [
        pl.BlockSpec(memory_space=pltpu.HBM if grant else pltpu.VMEM)
    ] * (len(args) - smem)
    moved = sum(a.size * a.dtype.itemsize for a in args) + sum(
        o.size * o.dtype.itemsize for o in outs
    )
    return pl.pallas_call(
        kernel,
        out_shape=outs,
        in_specs=specs,
        out_specs=[pl.BlockSpec(memory_space=pltpu.VMEM)] * len(outs),
        scratch_shapes=list(scratch),
        cost_estimate=pl.CostEstimate(flops=flops, bytes_accessed=moved, transcendentals=0),
        compiler_params=pltpu.CompilerParams(vmem_limit_bytes=grant or held + SPARE_VMEM),
    )(*args)


def shaped(shape, dtype):
    return jax.ShapeDtypeStruct(shape, dtype)


def fill(buffer, refs, start=0, limit=None):
    at = 0
    for ref in refs:
        size = limit or ref.shape[0]
        buffer[pl.ds(at, size), :] = ref[:size, start : start + buffer.shape[1]]
        at += size


def dot_rows(a, b):
    return lax.dot_general(a, b, (((1,), (1,)), ((), ())), preferred_element_type=F32)


def pack_stage(tokens, ids, weights, owners):
    tok, width = tokens.shape
    half = width // 2
    per_row = width // tok
    top = ids.shape[0]
    extra = 2 * -(-owners // per_row)
    rows = tok + -(-extra // 8) * 8

    def kernel(tok_hbm, id_hbm, weight_hbm, out_ref, tok_ref, id_ref, weight_ref, sems):
        pulls = [
            pltpu.make_async_copy(source, target, sems.at[k])
            for k, (source, target) in enumerate(
                ((id_hbm, id_ref), (weight_hbm, weight_ref), (tok_hbm, tok_ref))
            )
        ]
        for pull in pulls:
            pull.start()
        for pull in pulls:
            pull.wait()
        swapped = lax.axis_index(DP) != 0
        out_ref[:tok, :half] = jnp.where(swapped, tok_ref[:, half:], tok_ref[:, :half])
        out_ref[:tok, half:] = jnp.where(swapped, tok_ref[:, :half], tok_ref[:, half:])
        lanes = [[] for _ in range(extra)]
        for owner in range(owners):
            value = jnp.zeros((1, tok), F32)
            for k in range(top):
                hit = id_ref[k : k + 1, :] == owner
                value = value + jnp.where(hit, weight_ref[k : k + 1, :], 0.0)
            high = value.astype(BF).astype(F32)
            row = owner // per_row
            lanes[2 * row].append(high)
            lanes[2 * row + 1].append(value - high)
        filled = []
        for row in lanes:
            row += [jnp.zeros((1, tok), F32)] * (per_row - len(row))
            filled.append(jnp.concatenate(row, axis=1))
        filled.append(jnp.zeros((rows - tok - extra, width), F32))
        out_ref[tok:, :] = jnp.concatenate(filled, axis=0).astype(BF)

    return vmem_call(
        kernel,
        [shaped((rows, width), BF)],
        [tokens, ids, weights],
        scratch=[
            pltpu.VMEM(tokens.shape, tokens.dtype),
            pltpu.VMEM(ids.shape, ids.dtype),
            pltpu.VMEM(weights.shape, weights.dtype),
            pltpu.SemaphoreType.DMA((3,)),
        ],
        grant=WIDE_GRANT,
    )[0]


def weight_column(ref, tok, owners, mine):
    width = ref.shape[1]
    per_row = width // tok
    extra = ref[tok:, :].astype(F32)
    row = jnp.zeros((1, tok), F32)
    for owner in range(owners):
        at, lane = 2 * (owner // per_row), (owner % per_row) * tok
        both = extra[at : at + 1, lane : lane + tok] + extra[at + 1 : at + 2, lane : lane + tok]
        row = row + jnp.where(mine == owner, both, 0.0)
    diagonal = lax.broadcasted_iota(jnp.int32, (tok, tok), 0) == lax.broadcasted_iota(
        jnp.int32, (tok, tok), 1
    )
    return jnp.sum(jnp.where(diagonal, row, 0.0), axis=1, keepdims=True)


def hidden_stage(blocks, groups, up, tok, owners):
    count = len(blocks)
    width = blocks[0].shape[1]
    hidden = up[0].shape[0]
    half = width // 2
    rows = count * tok
    sizes = [g * tok for g in groups]

    def kernel(*refs):
        xs, (up0, up1) = refs[:count], refs[count : count + 2]
        act_refs = refs[count + 2 : count + 2 + len(groups)]
        slope_refs = refs[count + 2 + len(groups) : count + 2 + 2 * len(groups)]
        buffer = refs[-1]
        fill(buffer, xs, limit=tok)
        at, j = 0, 0
        for index, g in enumerate(groups):
            x = buffer[pl.ds(at, g * tok), :]
            pre = dot_rows(x[:, :half], up0[...]) + dot_rows(x[:, half:], up1[...])
            sig = 1.0 / (1.0 + jnp.exp(-pre))
            for b in range(g):
                w = weight_column(xs[j], tok, owners, lax.axis_index(EXPERT))
                p = pre[b * tok : (b + 1) * tok]
                s = sig[b * tok : (b + 1) * tok]
                ws = w * s
                act_refs[index][pl.ds(b * tok, tok), :] = (ws * p).astype(BF)
                slope_refs[index][pl.ds(b * tok, tok), :] = (ws * (1.0 + p * (1.0 - s))).astype(BF)
                j += 1
            at += g * tok

    outs = [shaped((size, hidden), BF) for size in sizes]
    result = vmem_call(
        kernel,
        outs + outs,
        list(blocks) + [up[0], up[1]],
        scratch=[pltpu.VMEM((rows, width), BF)],
        flops=2 * rows * width * hidden,
    )
    return result[: len(groups)], result[len(groups) :]


def project(act, down, *adds):
    total = jnp.dot(act, down, preferred_element_type=F32)
    for add in adds:
        missing = act.shape[0] - add.shape[0]
        total = total + jnp.pad(add, ((missing, 0), (0, 0))).astype(F32)
    return total


def outer_sum(lefts, rights, out_dtype, rw, start=0, limit=None, base=None):
    nl, nr = len(lefts), len(rights)
    rows = sum(a.shape[0] for a in lefts)
    lw = lefts[0].shape[1]

    def kernel(*refs):
        out_ref, left, right = refs[-3:]
        fill(left, refs[:nl])
        fill(right, refs[nl : nl + nr], start, limit)
        at = 0
        while at < lw:
            size = min(256, lw - at)
            value = lax.dot_general(
                left[:, at : at + size],
                right[...],
                (((0,), (0,)), ((), ())),
                preferred_element_type=F32,
            )
            if base is not None:
                value = value + refs[nl + nr][at : at + size, :]
            out_ref[at : at + size, :] = value.astype(out_dtype)
            at += size

    return vmem_call(
        kernel,
        [shaped((lw, rw), out_dtype)],
        list(lefts) + list(rights) + ([] if base is None else [base]),
        scratch=[pltpu.VMEM((rows, lw), BF), pltpu.VMEM((rows, rw), BF)],
        flops=2 * rows * lw * rw,
    )[0]


def back_stage(grads, slopes, down):
    count = len(slopes)
    hidden = down[0].shape[0]

    def kernel(*refs):
        g0, g1 = refs[:count], refs[count : 2 * count]
        slope = refs[2 * count : 3 * count]
        down0, down1 = refs[3 * count : 3 * count + 2]
        outs = refs[3 * count + 2 :]
        for b in range(count):
            value = dot_rows(g0[b][...], down0[...]) + dot_rows(g1[b][...], down1[...])
            outs[b][...] = (value * slope[b][...].astype(F32)).astype(BF)

    rows = sum(s.shape[0] for s in slopes)
    return vmem_call(
        kernel,
        [shaped(s.shape, BF) for s in slopes],
        list(grads[0]) + list(grads[1]) + list(slopes) + list(down),
        flops=4 * rows * down[0].shape[1] * hidden,
    )


def eye(size):
    return lax.broadcasted_iota(jnp.int32, (size, size), 0) == lax.broadcasted_iota(
        jnp.int32, (size, size), 1
    )


def to_column(row):
    return jnp.sum(jnp.where(eye(row.shape[1]), row, 0.0), axis=1, keepdims=True)


def to_row(column):
    return jnp.sum(jnp.where(eye(column.shape[0]), column, 0.0), axis=0, keepdims=True)


def clicks_of(rank_ref, click_ref, alpha_ref, beta_ref):
    rank_row = rank_ref[...]
    hot = (
        lax.broadcasted_iota(jnp.int32, (alpha_ref.shape[1], rank_row.shape[1]), 0) == rank_row
    ).astype(F32)
    alpha = jnp.sum(hot * to_column(alpha_ref[...]), axis=0, keepdims=True)
    beta = jnp.sum(hot * to_column(beta_ref[...]), axis=0, keepdims=True)
    return (click_ref[...].astype(F32) - beta) / alpha


def lists_of(list_ref, count):
    row = list_ref[...]
    return (lax.broadcasted_iota(jnp.int32, (count, row.shape[1]), 0) == row).astype(F32)


def pool_of(pool_ref, cands):
    row = pool_ref[...]
    return (lax.broadcasted_iota(jnp.int32, (cands, row.shape[1]), 0) == row).astype(F32)


def score_stage(rolled, sums, head, out_w, lists_in):
    width = rolled.shape[1]
    tok = sums[0].shape[0]
    half = width // 2
    cands = lists_in[1].shape[1]
    units = sum(h.shape[0] for h in head)
    per_half = len(sums) // 2

    def kernel(*refs):
        rolled_ref = refs[0]
        sum_refs = refs[1 : 1 + 2 * per_half]
        rest = refs[1 + 2 * per_half :]
        head_refs, out_refs = rest[:2], rest[2:4]
        pool_ref, list_ref, click_ref, rank_ref, alpha_ref, beta_ref = rest[4:10]
        normed_ref, inv_ref, pooled_ref, act_ref, exp_ref, corr_ref, tot_ref = rest[10:]
        mixed = []
        for h in range(2):
            value = rolled_ref[:tok, h * half : (h + 1) * half].astype(F32)
            for ref in sum_refs[h * per_half : (h + 1) * per_half]:
                value = value + ref[...].astype(F32)
            mixed.append(value)
        square = sum(jnp.sum(m * m, axis=1, keepdims=True) for m in mixed)
        inv = lax.rsqrt(square * (1.0 / width) + 1e-06)
        inv_ref[...] = inv
        hot = pool_of(pool_ref, cands)
        counts = jnp.sum(hot, axis=1, keepdims=True)
        pooled = []
        for h in range(2):
            normed = mixed[h] * inv
            normed_ref[:, h * half : (h + 1) * half] = normed
            pooled.append(
                jnp.dot(
                    hot, normed, precision=lax.Precision.HIGHEST, preferred_element_type=F32
                )
                / counts
            )
        swapped = lax.axis_index(DP) != 0
        pooled_ref[:, :half] = jnp.where(swapped, pooled[1], pooled[0]).astype(BF)
        pooled_ref[:, half:] = jnp.where(swapped, pooled[0], pooled[1]).astype(BF)
        both = pooled_ref[...]
        scores = jnp.zeros((cands, 1), F32)
        at = 0
        for head_ref, out_row in zip(head_refs, out_refs):
            size = head_ref.shape[0]
            act = jnp.tanh(dot_rows(both, head_ref[...]))
            act_ref[:, at : at + size] = act
            scores = scores + jnp.sum(act * out_row[...], axis=1, keepdims=True)
            at += size
        score_row = to_row(scores)
        exp_row = jnp.exp(score_row)
        exp_ref[...] = exp_row
        corrected = clicks_of(rank_ref, click_ref, alpha_ref, beta_ref)
        corr_ref[...] = corrected
        member = lists_of(list_ref, LISTS)
        lane = lax.broadcasted_iota(jnp.int32, (LISTS, 128), 1)
        total = jnp.zeros((LISTS, 128), F32)
        for k, row in enumerate((exp_row, corrected * score_row, corrected)):
            total = jnp.where(lane == k, jnp.sum(member * row, axis=1, keepdims=True), total)
        tot_ref[...] = total

    return vmem_call(
        kernel,
        [
            shaped((tok, width), F32),
            shaped((tok, 1), F32),
            shaped((cands, width), BF),
            shaped((cands, units), F32),
            shaped((1, cands), F32),
            shaped((1, cands), F32),
            shaped((LISTS, 128), F32),
        ],
        [rolled] + sums + head + out_w + lists_in,
        flops=4 * cands * width * units,
    )


def slope_stage(normed, inv, head_act, head, out_w, pool_ids, cands):
    tok, width = normed.shape
    half = width // 2

    def kernel(normed_ref, inv_ref, act_ref, *refs):
        head_refs, out_refs, pool_ref, slope_ref = refs[:2], refs[2:4], refs[4], refs[5]
        back = jnp.zeros((cands, width), F32)
        at = 0
        for head_ref, out_row in zip(head_refs, out_refs):
            size = head_ref.shape[0]
            act = act_ref[:, at : at + size]
            hid = (out_row[...] * (1.0 - act * act)).astype(BF)
            back = back + jnp.dot(hid, head_ref[...], preferred_element_type=F32)
            at += size
        hot = pool_of(pool_ref, cands)
        back = back / jnp.sum(hot, axis=1, keepdims=True)
        swapped = lax.axis_index(DP) != 0
        parts = [
            jnp.where(swapped, back[:, half:], back[:, :half]),
            jnp.where(swapped, back[:, :half], back[:, half:]),
        ]
        grads = [
            lax.dot_general(
                hot,
                p,
                (((0,), (0,)), ((), ())),
                precision=lax.Precision.HIGHEST,
                preferred_element_type=F32,
            )
            for p in parts
        ]
        mean = sum(
            jnp.sum(g * normed_ref[:, h * half : (h + 1) * half], axis=1, keepdims=True)
            for h, g in enumerate(grads)
        ) * (1.0 / width)
        for h in range(2):
            at = slice(h * half, (h + 1) * half)
            slope_ref[:, at] = inv_ref[...] * (grads[h] - normed_ref[:, at] * mean)

    return vmem_call(
        kernel,
        [shaped((tok, width), F32)],
        [normed, inv, head_act] + head + out_w + [pool_ids],
        flops=2 * cands * width * sum(h.shape[0] for h in head),
    )[0]


def grad_stage(own, other, slope, pooled, exp_row, corrected, pool_ids, list_ids):
    tok, width = slope.shape
    half = width // 2
    cands = list_ids.shape[1]

    def kernel(*refs):
        own_ref, other_ref, slope_ref, pooled_ref, exp_ref, corr_ref, pool_ref, list_ref = refs[:8]
        loss_ref, low_ref, high_ref, packed_ref = refs[8:]
        totals = own_ref[...] + other_ref[...]
        exp_total, cross_total, click_total = totals[:, 0:1], totals[:, 1:2], totals[:, 2:3]
        loss_ref[...] = jnp.sum(
            click_total * jnp.log(exp_total) - cross_total, axis=0, keepdims=True
        )
        member = lists_of(list_ref, LISTS)
        cand_row = (
            jnp.sum(member * (click_total / exp_total), axis=0, keepdims=True) * exp_ref[...]
            - corr_ref[...]
        )
        cand = to_column(cand_row)
        hot = pool_of(pool_ref, cands)
        of_token = to_column(jnp.sum(hot * cand, axis=0, keepdims=True))
        low_ref[...] = (of_token * slope_ref[:, :half]).astype(BF)
        high_ref[...] = (of_token * slope_ref[:, half:]).astype(BF)
        packed_ref[:, :width] = pooled_ref[...]
        top = cand.astype(BF).astype(F32)
        middle = (cand - top).astype(BF).astype(F32)
        bottom = cand - top - middle
        lane = lax.broadcasted_iota(jnp.int32, (cands, 128), 1)
        packed_ref[:, width:] = jnp.where(
            lane == 0, top, jnp.where(lane == 1, middle, jnp.where(lane == 2, bottom, 0.0))
        ).astype(BF)

    return vmem_call(
        kernel,
        [
            shaped((1, 1), F32),
            shaped((tok, half), BF),
            shaped((tok, half), BF),
            shaped((cands, width + 128), BF),
        ],
        [own, other, slope, pooled, exp_row, corrected, pool_ids, list_ids],
    )


def head_stage(table, blocks, head, out_w):
    count = len(blocks)
    packed_width = blocks[0].shape[1]
    total = table.shape[0]
    units, width = head.shape
    each = sum(b.shape[0] for b in blocks) // total
    cands = each // 2

    def kernel(table_ref, *refs):
        block_refs = refs[:count]
        head_ref, out_ref, grad_ref, out_grad_ref, buffer = refs[count:]
        mine, plane = lax.axis_index(EXPERT), lax.axis_index(DP)
        j = 0
        for ref in block_refs:
            for piece in range(ref.shape[0] // each):
                at = table_ref[mine, j] * each
                for k in range(2):
                    place = pl.multiple_of(at + (plane ^ k) * cands, cands)
                    start = piece * each + k * cands
                    buffer[pl.ds(place, cands), :] = ref[start : start + cands, :]
                j += 1
        pooled = buffer[:, :width]
        act = jnp.tanh(dot_rows(pooled, head_ref[...]))
        tail = buffer[:, width:].astype(F32)
        cand = tail[:, 0:1] + tail[:, 1:2] + tail[:, 2:3]
        hid = (cand * out_ref[...] * (1.0 - act * act)).astype(BF)
        out_grad_ref[...] = jnp.sum(cand * act, axis=0, keepdims=True)
        grad_ref[...] = lax.dot_general(
            hid, pooled, (((0,), (0,)), ((), ())), preferred_element_type=F32
        )

    return vmem_call(
        kernel,
        [shaped((units, width), F32), shaped((1, units), F32)],
        [table] + blocks + [head, out_w],
        scratch=[pltpu.VMEM((total * each, packed_width), BF)],
        flops=4 * total * each * width * units,
        smem=1,
    )


def after(value, *others):
    return lax.optimization_barrier((value,) + others)[0]


def dense_local(*args):
    return dense_step(*args)


def dense_step(
    tokens,
    route_ids,
    route_weights,
    up_weight,
    down_weight,
    head_weight,
    out_weight,
    pool_ids,
    list_ids,
    clicks,
    ranks,
    alpha_table,
    beta_table,
):
    n_exp = lax.axis_size(EXPERT)
    ring = Ring(n_exp)
    last = ring.half
    tok, width = tokens.shape
    half = width // 2
    cands = list_ids.shape[1]

    def across(x):
        return lax.ppermute(x, DP, [(0, 1), (1, 0)])

    up_own, down_own = up_weight[0].T, down_weight[0].T
    up = [up_own, across(up_own)]
    rolled = pack_stage(tokens, route_ids.T, route_weights.T, n_exp)

    mine, theirs = [rolled], [ring.swap(rolled)]
    mine_swapped, theirs_swapped = [None], [None]
    for r in range(1, last + 1):
        mine.append(ring.send(mine[-1]))
        mine_swapped.append(ring.swap(mine[-1]))
        if r < last:
            theirs.append(ring.send(theirs[-1]))
            theirs_swapped.append(ring.swap(theirs[-1]))

    down = [down_own, across(down_own)]
    head = [head_weight, across(head_weight)]
    out_row = out_weight[None, :]
    out_w = [out_row, across(out_row)]

    acts, slopes = [], []
    for r in range(last + 1):
        if r == 0:
            blocks, groups = [mine[0], theirs[0]], [1, 1]
        elif r < last:
            blocks = [mine[r], theirs[r], mine_swapped[r], theirs_swapped[r]]
            groups = [2, 2]
        else:
            blocks, groups = [mine[r], mine_swapped[r]], [1, 1]
        a, s = hidden_stage(blocks, groups, up, tok, n_exp)
        acts.append(a)
        slopes.append(s)

    sums = []
    for h in range(2):
        first = project(acts[last][1], down[h]).astype(BF)
        given = ring.swap(first)
        moving = project(acts[last][0], down[h], given).astype(BF)
        for r in reversed(range(1, last)):
            block = after(acts[r][0], moving) if h else acts[r][0]
            given = ring.swap(project(block, down[h]).astype(BF))
            came = ring.send(moving)
            moving = project(acts[r][1], down[h], given, came).astype(BF)
        came = ring.send(moving)
        back = project(acts[0][1], down[h], came[:tok]).astype(BF)
        sums += [project(acts[0][0], down[h], came[tok:]), ring.swap(back)]

    lists_in = [pool_ids, list_ids, clicks, ranks, alpha_table[None, :], beta_table[None, :]]
    normed, inv, pooled, head_act, exp_row, corrected, totals = score_stage(
        rolled, sums, head, out_w, lists_in
    )
    slope = slope_stage(normed, inv, head_act, head, out_w, pool_ids, cands)
    list_loss, low, high, packed = grad_stage(
        totals, across(totals), slope, pooled, exp_row, corrected, pool_ids, list_ids
    )

    def gather_blocks(x):
        blocks = []
        for rounds in ring.gather(x):
            blocks += rounds
        return blocks

    grads = [None, None]
    grads[1] = gather_blocks(high)
    grads[0] = gather_blocks(low)
    flat = lambda lists: [x for part in lists for x in part]
    act_blocks, slope_blocks = flat(acts), flat(slopes)
    partial = outer_sum(act_blocks[:-3], grads[1][:-3], F32, half)
    partial = outer_sum(act_blocks[-3:], grads[1][-3:], BF, half, base=partial)
    sent_down = across(partial)
    split = 2 * (last - 1)
    early = back_stage([grads[0][:split], grads[1][:split]], slope_blocks[:split], down)
    late = back_stage([grads[0][split:], grads[1][split:]], slope_blocks[split:], down)
    pre_grads = list(early) + list(late)
    inputs = [mine[0], theirs[0]]
    for r in range(1, last):
        inputs += [mine[r], theirs[r], mine_swapped[r], theirs_swapped[r]]
    inputs += [mine[last], mine_swapped[last]]
    sent_up = across(outer_sum(pre_grads, inputs, BF, half, half, tok))
    down_local = outer_sum(act_blocks, grads[0], BF, half)
    up_local = outer_sum(pre_grads, inputs, BF, half, 0, tok)

    grad_down = (down_local.astype(F32) + sent_down.astype(F32)).astype(BF).T[None]
    pair = jnp.concatenate([packed, across(packed)])
    blocks = gather_blocks(pair)
    blocks[0], grad_down = lax.optimization_barrier((blocks[0], grad_down))
    grad_head, grad_out = head_stage(jnp.asarray(ring.table), blocks, head_weight, out_row)

    grad_up = (up_local.astype(F32) + sent_up.astype(F32)).astype(BF).T[None]
    return (grad_up, grad_down, grad_head, grad_out[0], list_loss[0])


def solution(mesh):
    paired = mesh.shape[DP] == 2 and mesh.shape[EXPERT] % 4 == 0
    return jax.shard_map(
        dense_local if paired else routed_local,
        mesh=mesh,
        in_specs=(
            P((DP, EXPERT), None),
            P((DP, EXPERT), None),
            P((DP, EXPERT), None),
            P(EXPERT, DP, None),
            P(EXPERT, DP, None),
            P(DP, None),
            P(DP),
            P((DP, EXPERT), None),
            P((DP, EXPERT), None),
            P((DP, EXPERT), None),
            P((DP, EXPERT), None),
            P(),
            P(),
        ),
        out_specs=(
            P(EXPERT, DP, None),
            P(EXPERT, DP, None),
            P(DP, None),
            P(DP),
            P(EXPERT),
        ),
        check_vma=False,
    )
```
